32 devices in a mesh: dp: 32 (over z, y, x, core).
Axes of the slice: x: 2, y: 2, z: 4, core: 2. Of those that a mesh axis runs over, the one named last changes fastest.
Arguments:
- tokens: bfloat16 [2, 5120, 1024], P(None, 'dp'), may hold values from -6 to 6
- grad_out: bfloat16 [2, 5120, 1024], P(None, 'dp'), may hold values from -6 to 6
- w_query: bfloat16 [1024, 1024], P('dp'), may hold values from -0.1875 to 0.1875
- w_key: bfloat16 [1024, 1024], P('dp'), may hold values from -0.1875 to 0.1875
- w_value: bfloat16 [1024, 1024], P('dp'), may hold values from -0.1875 to 0.1875
- b_query: bfloat16 [1024], P('dp'), may hold values from -3 to 3
- b_value: bfloat16 [1024], P('dp'), may hold values from -3 to 3
- w_attn_out: bfloat16 [1024, 1024], P('dp'), may hold values from -0.75 to 0.75
- b_attn_out: bfloat16 [1024], P('dp'), may hold values from -3 to 3
- w_up: bfloat16 [1024, 4096], P('dp'), may hold values from -0.1875 to 0.1875
- b_up: bfloat16 [4096], P('dp'), may hold values from -3 to 3
- w_down: bfloat16 [4096, 1024], P('dp'), may hold values from -0.09375 to 0.09375
- b_down: bfloat16 [1024], P('dp'), may hold values from -3 to 3
- ln1_gain: bfloat16 [1024], P('dp'), may hold values from 0.25 to 1.75
- ln1_bias: bfloat16 [1024], P('dp'), may hold values from -2 to 2
- ln2_gain: bfloat16 [1024], P('dp'), may hold values from 0.25 to 1.75
- ln2_bias: bfloat16 [1024], P('dp'), may hold values from -2 to 2
- leaf_parent: int32 [2, 4, 8], replicated, may hold values from 1 to 4, as said below
Outputs:
- output: bfloat16 [2, 5120, 1024], P(None, 'dp')
- grad_input: bfloat16 [2, 5120, 1024], P(None, 'dp')
- grad_w_query: float32 [1024, 1024], P('dp')
- grad_w_key: float32 [1024, 1024], P('dp')
- grad_w_value: float32 [1024, 1024], P('dp')
- grad_w_attn_out: float32 [1024, 1024], P('dp')
- grad_w_up: float32 [1024, 4096], P('dp')
- grad_w_down: float32 [4096, 1024], P('dp')
- grad_b_query: float32 [1024], P('dp')
- grad_b_value: float32 [1024], P('dp')
- grad_b_attn_out: float32 [1024], P('dp')
- grad_b_up: float32 [4096], P('dp')
- grad_b_down: float32 [1024], P('dp')
- grad_ln1_gain: float32 [1024], P('dp')
- grad_ln1_bias: float32 [1024], P('dp')
- grad_ln2_gain: float32 [1024], P('dp')
- grad_ln2_bias: float32 [1024], P('dp')
The draws below stay inside these ranges and needn't reach their ends.
Inputs may be any that keep to these rules, and one draw needn't show every extreme that they name: leaf_parent[m, t, l] is the branch segment of leaf l of tree t; each of the 4 branches of a tree is the parent of exactly 2 leaves.
All inputs are finite; a program needn't handle non-finite values.
Results may differ from the reference program's by a relative error of at most 0.012.
Values may be sent and summed in bfloat16 or wider, within the bound.
No kernel may reach another device: no remote copies, remote signals or barrier semaphores. Data moves between devices by JAX's collectives and lax.ppermute only.
A program may use at most 320 MiB of HBM per device.

```python
import jax
import jax.numpy as jnp
from jax import lax

D = 1024
HEADS = 16
FF = 4096
BLK = 32
MB = 2
TRUNK_BLK = 16
SEG_BLK = 2
BRANCHES = 4
LEAVES = 8
TREE_BLK = 40
TOKENS = 5120
TREES = 4


def draw_leaf_parent(key, part):
    keys = jax.random.split(key, MB * TREES)
    orders = jax.vmap(lambda single: jax.random.permutation(single, LEAVES))(keys)
    parents = 1 + orders // (LEAVES // BRANCHES)
    return parents.reshape(MB, TREES, LEAVES).astype(jnp.int32)


def with_spikes(values, key, source, target, parts, factor):
    owner, partner = [(jnp.arange(values.shape[axis_at]) // (values.shape[axis_at] // parts)).reshape([-1 if axis == axis_at else 1 for axis in range(values.ndim)]) for axis_at in (source, target)]
    chosen = jax.random.permutation(key, parts)[partner]
    strong = (owner == chosen) | (owner == (partner + parts // 2) % parts)
    return jnp.where(strong, factor * values, values)


def block_scale(stream_key, dims, cuts, smallest, high):
    factor_of = 1.0
    for position, blocks in cuts:
        steps = jax.random.uniform(jax.random.fold_in(jax.random.fold_in(stream_key, 6), position), (blocks,), jnp.float32, smallest / len(cuts), high / len(cuts))
        factor_of = factor_of * jnp.repeat(jnp.exp(steps), dims[position] // blocks).reshape((-1,) + (1,) * (len(dims) - 1 - position))
    return factor_of


def gaussian(key, dims, width, limit, cuts=(), held_as=jnp.bfloat16):
    values = jax.random.normal(key, dims, jnp.float32) * width
    if len(cuts) > 0:
        values = block_scale(key, dims, cuts, -0.22, 0.18) * values
    return jnp.clip(values, min=-limit, max=limit).astype(held_as)


def heavy_noise(rng, dims, deviation, bound, cuts, heavy, kind=jnp.bfloat16):
    array = deviation * jax.random.normal(rng, dims, jnp.float32)
    if cuts:
        array = array * block_scale(rng, dims, cuts, -0.22, 0.18)
    return jnp.clip(with_spikes(array, jax.random.fold_in(rng, 3), *heavy), -bound, bound).astype(kind)


def setup_inputs(seed: int = 0) -> dict:
    streams_of = jax.random.split(jax.random.key(seed), 19)
    tokens = heavy_noise(streams_of[0], (MB, TOKENS, D), 1.0, 6.0, ((1, 32),), (1, 2, 32, 2.75))
    grad_out = gaussian(streams_of[1], (MB, TOKENS, D), 1.0, 6.0, ((1, 32),))
    w_query = gaussian(streams_of[2], (D, D), D ** -0.5, 0.1875, ((0, 32),))
    w_key = gaussian(streams_of[3], (D, D), D ** -0.5, 0.1875, ((0, 32),))
    w_value = gaussian(streams_of[4], (D, D), D ** -0.5, 0.1875, ((0, 32),))
    b_query = gaussian(streams_of[5], (D,), 0.5, 3.0, ((0, 32),))
    b_value = gaussian(streams_of[6], (D,), 0.5, 3.0, ((0, 32),))
    w_attn_out = gaussian(streams_of[7], (D, D), (D // 16) ** -0.5, 0.75, ((0, 32),))
    b_attn_out = gaussian(streams_of[8], (D,), 0.5, 3.0, ((0, 32),))
    w_up = gaussian(streams_of[9], (D, FF), D ** -0.5, 0.1875, ((0, 32),))
    b_up = gaussian(streams_of[10], (FF,), 0.5, 3.0, ((0, 32),))
    w_down = gaussian(streams_of[11], (FF, D), FF ** -0.5, 0.09375, ((0, 32),))
    b_down = gaussian(streams_of[12], (D,), 0.5, 3.0, ((0, 32),))
    ln1_gain = jnp.clip(1.0 + 0.15 * jax.random.normal(streams_of[13], (D,), jnp.float32), 0.25, 1.75).astype(jnp.bfloat16)
    ln1_bias = gaussian(streams_of[14], (D,), 0.3, 2.0, ((0, 32),))
    ln2_gain = jnp.clip(1.0 + 0.15 * jax.random.normal(streams_of[15], (D,), jnp.float32), 0.25, 1.75).astype(jnp.bfloat16)
    ln2_bias = gaussian(streams_of[16], (D,), 0.3, 2.0, ((0, 32),))
    leaf_parent = draw_leaf_parent(jax.random.fold_in(streams_of[18], 71), 0)
    return {"tokens": tokens, "grad_out": grad_out, "w_query": w_query, "w_key": w_key, "w_value": w_value, "b_query": b_query, "b_value": b_value, "w_attn_out": w_attn_out, "b_attn_out": b_attn_out, "w_up": w_up, "b_up": b_up, "w_down": w_down, "b_down": b_down, "ln1_gain": ln1_gain, "ln1_bias": ln1_bias, "ln2_gain": ln2_gain, "ln2_bias": ln2_bias, "leaf_parent": leaf_parent}


eps = 1e-05

@jax.custom_vjp
def low(v):
    return lax.optimization_barrier(v.astype(jnp.bfloat16)).astype(jnp.float32)

@jax.custom_vjp
def low_back(v):
    return v

def low_keep(v):
    return (low(v), None)

def low_pass(kept, grad):
    return (grad,)

def back_keep(v):
    return (v, None)

def back_low(kept, grad):
    return (low(grad),)
low.defvjp(low_keep, low_pass)
low_back.defvjp(back_keep, back_low)

def layer_norm(values, gain, shift):
    center = values - lax.optimization_barrier(jnp.mean(values, axis=-1, keepdims=True))
    spread = lax.optimization_barrier(jnp.mean(center * center, axis=-1, keepdims=True))
    return center * lax.rsqrt(spread + eps) * gain + shift

def path_info(first_block, count, block_len, parents):
    blocks = first_block + jnp.arange(count, dtype=jnp.int32)
    tree_ids = blocks // TREE_BLK
    local_block = blocks % TREE_BLK
    after_trunk = local_block - TRUNK_BLK
    leaf_part = after_trunk - BRANCHES * SEG_BLK
    is_trunk = local_block < TRUNK_BLK
    is_branch = jnp.logical_and(local_block >= TRUNK_BLK, leaf_part < 0)
    segment = jnp.where(is_trunk, 0, jnp.where(is_branch, 1 + after_trunk // SEG_BLK, 1 + BRANCHES + leaf_part // SEG_BLK))
    offset = jnp.where(is_trunk, local_block, jnp.where(is_branch, TRUNK_BLK + after_trunk % SEG_BLK, TRUNK_BLK + SEG_BLK + leaf_part % SEG_BLK))
    tree_hit = (tree_ids[:, None] == jnp.arange(parents.shape[0], dtype=jnp.int32)[None, :]).astype(jnp.int32)
    tree_rows = lax.optimization_barrier(jnp.sum(tree_hit[:, :, None] * parents[None, :, :], axis=1))
    leaf_hit = ((segment - 1 - BRANCHES)[:, None] == jnp.arange(parents.shape[1], dtype=jnp.int32)[None, :]).astype(jnp.int32)
    parent = lax.optimization_barrier(jnp.sum(leaf_hit * tree_rows, axis=1))
    within = jnp.arange(block_len, dtype=jnp.int32)
    seg_tok = jnp.repeat(segment, block_len)
    par_tok = jnp.repeat(parent, block_len)
    pos_tok = (offset[:, None] * block_len + within[None, :]).reshape(-1).astype(jnp.int32)
    return (seg_tok, par_tok, pos_tok)

def visible(query_info, key_info):
    query_seg, query_par, query_pos = query_info
    key_seg, key_par, key_pos = key_info
    related = (key_seg[None, :] == query_seg[:, None]) | (key_seg[None, :] == 0) | (key_seg[None, :] == query_par[:, None])
    return related & (key_pos[None, :] <= query_pos[:, None])

def alibi_bias(query_pos, key_pos, head_count):
    slopes = jnp.exp2(-8.0 * (jnp.arange(head_count, dtype=jnp.float32) + 1.0) / head_count)
    distance = (query_pos[:, None] - key_pos[None, :]).astype(jnp.float32)
    return -slopes[:, None, None] * distance[None, :, :]

def matmul_high(left, right):
    return jnp.dot(left, right, precision=lax.Precision.HIGHEST)

def tree_attention(query, key, value, token_info, score_scale):
    row_count, feature_width = query.shape
    head_count = HEADS
    head_dim = feature_width // head_count
    tree_tok = TREE_BLK * BLK
    tree_count = row_count // tree_tok

    def one_tree(packed):
        query_t, key_t, value_t, seg_t, par_t, pos_t = packed
        raw_scores = jnp.einsum('qhd,khd->hqk', query_t, key_t, precision=lax.Precision.HIGHEST) * score_scale
        raw_scores = raw_scores + alibi_bias(pos_t, pos_t, head_count)
        raw_scores = low_back(raw_scores)
        info_t = (seg_t, par_t, pos_t)
        masked = jnp.where(visible(info_t, info_t)[None], raw_scores, -jnp.inf)
        probs = low(jax.nn.softmax(masked, axis=-1))
        return jnp.einsum('hqk,khd->qhd', probs, value_t, precision=lax.Precision.HIGHEST)
    shaped = lambda arr: arr.reshape(tree_count, tree_tok, head_count, head_dim)
    seg_tok, par_tok, pos_tok = token_info
    result = lax.map(jax.checkpoint(one_tree), (shaped(query), shaped(key), shaped(value), seg_tok.reshape(tree_count, tree_tok), par_tok.reshape(tree_count, tree_tok), pos_tok.reshape(tree_count, tree_tok)))
    return result.reshape(row_count, feature_width)

def forward(resid, params, token_info, score_scale):
    mat_query, mat_key, mat_value, mat_out, mat_up, mat_down, vec_query, vec_value, vec_out, vec_up, vec_down, gain_one, shift_one, gain_two, shift_two = params
    normed1 = low(layer_norm(resid, gain_one, shift_one))
    query = low_back(low(matmul_high(normed1, mat_query) + vec_query))
    key = low_back(low(matmul_high(normed1, mat_key)))
    value = low_back(low(matmul_high(normed1, mat_value) + vec_value))
    context = low_back(low(tree_attention(query, key, value, token_info, score_scale)))
    branch = low_back(matmul_high(context, mat_out) + vec_out)
    middle = resid + branch
    normed2 = low(layer_norm(middle, gain_two, shift_two))
    upper = low_back(matmul_high(normed2, mat_up) + vec_up)
    active = low(jax.nn.gelu(upper, approximate=True))
    return middle + matmul_high(active, mat_down) + vec_down

def reference(tokens, grad_out, w_query, w_key, w_value, b_query, b_value, w_attn_out, b_attn_out, w_up, b_up, w_down, b_down, ln1_gain, ln1_bias, ln2_gain, ln2_bias, leaf_parent):
    params = tuple((piece.astype(jnp.float32) for piece in (w_query, w_key, w_value, w_attn_out, w_up, w_down, b_query, b_value, b_attn_out, b_up, b_down, ln1_gain, ln1_bias, ln2_gain, ln2_bias)))
    score_scale = (D // HEADS) ** (-0.5)
    grads = tuple((jnp.zeros(piece.shape, jnp.float32) for piece in params))
    outputs = []
    input_grads = []
    for micro_index in range(MB):
        token_info = path_info(0, TOKENS // BLK, BLK, leaf_parent[micro_index])
        resid = tokens[micro_index].astype(jnp.float32)
        result, pullback = jax.vjp(lambda resid_in, *param_list: forward(resid_in, param_list, token_info, score_scale), resid, *params)
        back = pullback(grad_out[micro_index].astype(jnp.float32))
        outputs.append(result.astype(jnp.bfloat16))
        input_grads.append(back[0].astype(jnp.bfloat16))
        grads = tuple((first + second for first, second in zip(grads, back[1:])))
    return (jnp.stack(outputs), jnp.stack(input_grads), grads[0], grads[1], grads[2], grads[3], grads[4], grads[5], grads[6], grads[7], grads[8], grads[9], grads[10], grads[11], grads[12], grads[13], grads[14])
```

```python
from functools import partial

import jax
import jax.numpy as jnp
from jax import lax
from jax.experimental import pallas as pl
from jax.experimental.pallas import tpu as pltpu
from jax.sharding import PartitionSpec as P

HEADS = 16
BLK = 32
TRUNK_BLK = 16
SEG_BLK = 2
BRANCHES = 4
LEAVES = 8
TREE_BLK = 40

GROUP = 8
TREE = TREE_BLK * BLK
TRUNK = TRUNK_BLK * BLK
SEG = SEG_BLK * BLK
ROWS = 256
HALF = 128
HID = 64
NEG = -1e30

eps = 1e-05
bf16 = jnp.bfloat16
f32 = jnp.float32

FIRST = (2, 4)
SECOND = (4, 2)


def swap(value, mask):
    count = lax.axis_size("dp")
    return lax.ppermute(value, "dp", [(source, source ^ mask) for source in range(count)])


def plane_gather(own):
    near = [swap(own[m], FIRST[m]) for m in range(2)]
    pair = [jnp.stack((own[m], near[m])) for m in range(2)]
    far = [swap(pair[m], SECOND[m]) for m in range(2)]
    odd_a = [swap(pair[m], 1) for m in range(2)]
    odd_b = [swap(far[m], 1) for m in range(2)]
    return [
        (jnp.concatenate((pair[m], far[m])), jnp.concatenate((odd_a[m], odd_b[m])))
        for m in range(2)
    ]


def plane_scatter(even, odd):
    back = [swap(odd[m].astype(bf16), 1) for m in range(2)]
    total = [even[m].astype(f32) + back[m].astype(f32) for m in range(2)]
    far = [swap(total[m][2:].astype(bf16), SECOND[m]) for m in range(2)]
    pair = [total[m][:2] + far[m].astype(f32) for m in range(2)]
    near = [swap(pair[m][1].astype(bf16), FIRST[m]) for m in range(2)]
    return [pair[m][0] + near[m].astype(f32) for m in range(2)]


def plane_groups():
    count = lax.axis_size("dp")
    return [list(range(first, first + GROUP)) for first in range(0, count, GROUP)]


def column_groups():
    count = lax.axis_size("dp")
    return [list(range(place, count, GROUP)) for place in range(GROUP)]


def plane_exchange(value):
    return lax.all_to_all(value, "dp", 0, 0, tiled=True, axis_index_groups=plane_groups())


def column_gather(value, column_place):
    planes = lax.axis_size("dp") // GROUP
    if planes > 4:
        return lax.all_gather(value, "dp", axis=0, axis_index_groups=column_groups())
    parts = jnp.stack([value] + [swap(value, GROUP * step) for step in range(1, planes)])
    return jnp.stack(
        [
            lax.dynamic_index_in_dim(parts, column_place ^ plane, 0, keepdims=False)
            for plane in range(planes)
        ]
    )


def column_scatter(value, column_place):
    planes = lax.axis_size("dp") // GROUP
    if planes > 4:
        return lax.psum_scatter(
            value, "dp", scatter_dimension=0, axis_index_groups=column_groups()
        )
    total = lax.dynamic_index_in_dim(value, column_place, 0, keepdims=False)
    for step in range(1, planes):
        part = lax.dynamic_index_in_dim(value, column_place ^ step, 0, keepdims=False)
        total = total + swap(part.astype(bf16), GROUP * step).astype(f32)
    return total


def layer_norm_parts(values):
    center = values - jnp.mean(values, axis=-1, keepdims=True)
    spread = jnp.mean(center * center, axis=-1, keepdims=True)
    scale = lax.rsqrt(spread + eps)
    return center * scale, scale


def layer_norm_back(grad, unit, scale, gain):
    scaled = grad * gain
    return scale * (
        scaled
        - jnp.mean(scaled, axis=-1, keepdims=True)
        - unit * jnp.mean(scaled * unit, axis=-1, keepdims=True)
    )


def gelu_tanh(values):
    return jax.nn.gelu(values, approximate=True)


def mm(left, right, contract):
    return lax.dot_general(left, right, (contract, ((), ())), preferred_element_type=f32)


NN = ((1,), (0,))
NT = ((1,), (1,))
TN = ((0,), (0,))


def split3(values):
    high = values.astype(bf16)
    rest = values - high.astype(f32)
    middle = rest.astype(bf16)
    low = (rest - middle.astype(f32)).astype(bf16)
    return high, middle, low


def key_positions():
    row = lax.broadcasted_iota(jnp.int32, (TREE, 128), 0)
    after = row - TRUNK
    return jnp.where(
        row < TRUNK,
        row,
        jnp.where(
            after < BRANCHES * SEG, TRUNK + (after & (SEG - 1)), TRUNK + SEG + (after & (SEG - 1))
        ),
    )


def load_tree(order_ref, packed_ref, query_s, key_s, slope_ref, micro):
    lane = lax.broadcasted_iota(jnp.int32, (TREE, 128), 1)
    rows = TREE // GROUP
    for block in range(GROUP):
        part = packed_ref[0, order_ref[micro, block]]
        at = pl.ds(block * rows, rows)
        query_s[0, at, :] = part[:, 0:128]
        key_s[0, at, :] = part[:, 128:256]
    query = query_s[0] * jnp.asarray(0.125, bf16)
    key = key_s[0]
    place = key_positions().astype(f32)
    one = jnp.ones((TREE, 128), bf16)
    zero = jnp.zeros((TREE, 128), bf16)
    for head in range(2):
        mine = (lane < HID) if head == 0 else (lane >= HID)
        base = HID if head == 0 else 0
        high, middle, low = split3(place * slope_ref[head])
        extra = jnp.where(
            lane == base,
            high,
            jnp.where(lane == base + 1, middle, jnp.where(lane == base + 2, low, zero)),
        )
        ones = jnp.where((lane >= base) & (lane < base + 3), one, zero)
        query_s[head] = jnp.where(mine, query, ones)
        key_s[head] = jnp.where(mine, key, extra)


def tile_masks():
    row = lax.broadcasted_iota(jnp.int32, (HALF, HALF), 1)
    col = lax.broadcasted_iota(jnp.int32, (HALF, HALF), 0)
    same = (row // SEG) == (col // SEG)
    segment = jnp.where(same & (col <= row), 0.0, NEG)
    parent = jnp.where(same, 0.0, NEG)
    trow = lax.broadcasted_iota(jnp.int32, (ROWS, ROWS), 1)
    tcol = lax.broadcasted_iota(jnp.int32, (ROWS, ROWS), 0)
    causal = jnp.where(tcol <= trow, 0.0, NEG)
    return segment, parent, causal


def parent_rows(parent_ref, micro, leaf):
    start = TRUNK + (parent_ref[micro, leaf] - 1) * SEG
    return pl.ds(pl.multiple_of(start, SEG), SEG)


def tile_pieces(tile):
    if tile < TRUNK // ROWS:
        return (tile + 1) * ROWS, True, [], []
    start = tile * ROWS
    own = [start, start + HALF]
    first_leaf = TRUNK + BRANCHES * SEG
    leaves = []
    if start >= first_leaf:
        leaf = (start - first_leaf) // SEG
        leaves = [(leaf, leaf + 1), (leaf + 2, leaf + 3)]
    return TRUNK, False, own, leaves


def tile_scores(tile, key_ref, query, parent_ref, micro, masks, side):
    segment, parent, causal = masks
    trunk, last, own, leaves = tile_pieces(tile)
    scores = mm(key_ref[0:trunk, :], query, NT)
    pieces = []
    if last:
        if trunk > ROWS:
            pieces.append(scores[: trunk - ROWS])
        pieces.append(scores[trunk - ROWS :] + causal)
    else:
        pieces.append(scores)
    if own:
        pieces.append(
            jnp.concatenate(
                [
                    mm(key_ref[at : at + HALF, :], query[i * HALF : (i + 1) * HALF], NT) + segment
                    for i, at in enumerate(own)
                ],
                axis=1,
            )
        )
    if leaves:
        pieces.append(
            jnp.concatenate(
                [
                    mm(rows, query[i * HALF : (i + 1) * HALF], NT) + parent
                    for i, rows in enumerate(side)
                ],
                axis=1,
            )
        )
    return pieces


def forward_kernel(
    order_ref, parent_ref, slope_ref, packed_ref, ctx_ref, log_ref, query_s, key_s, value_s
):
    micro = pl.program_id(0)
    rows = TREE // GROUP
    load_tree(order_ref, packed_ref, query_s, key_s, slope_ref, micro)
    for block in range(GROUP):
        value_s[pl.ds(block * rows, rows), :] = packed_ref[0, order_ref[micro, block]][:, 256:384]
    masks = tile_masks()
    for tile in range(TREE // ROWS):
        trunk, last, own, leaves = tile_pieces(tile)
        at = slice(tile * ROWS, (tile + 1) * ROWS)
        contexts = []
        side_values = [
            jnp.concatenate([value_s[parent_rows(parent_ref, micro, leaf), :] for leaf in pair])
            for pair in leaves
        ]
        for head in range(2):
            query = query_s[head, at, :]
            side = [
                jnp.concatenate(
                    [key_s[head, parent_rows(parent_ref, micro, leaf), :] for leaf in pair]
                )
                for pair in leaves
            ]
            pieces = tile_scores(tile, key_s.at[head], query, parent_ref, micro, masks, side)
            peak = pieces[0].max(axis=0, keepdims=True)
            for piece in pieces[1:]:
                peak = jnp.maximum(peak, piece.max(axis=0, keepdims=True))
            probs = [jnp.exp(piece - peak) for piece in pieces]
            total = probs[0].sum(axis=0, keepdims=True)
            for piece in probs[1:]:
                total = total + piece.sum(axis=0, keepdims=True)
            probs = [piece.astype(bf16) for piece in probs]
            ntrunk = len(probs) - bool(own) - bool(leaves)
            context = jnp.zeros((128, ROWS), f32)
            start = 0
            for piece in probs[:ntrunk]:
                context = context + mm(value_s[start : start + piece.shape[0], :], piece, TN)
                start += piece.shape[0]
            if own:
                context = context + jnp.concatenate(
                    [
                        mm(
                            value_s[first : first + HALF, :],
                            probs[ntrunk][:, i * HALF : (i + 1) * HALF],
                            TN,
                        )
                        for i, first in enumerate(own)
                    ],
                    axis=1,
                )
            if leaves:
                context = context + jnp.concatenate(
                    [
                        mm(
                            side_values[i],
                            probs[ntrunk + 1][:, i * HALF : (i + 1) * HALF],
                            TN,
                        )
                        for i in range(2)
                    ],
                    axis=1,
                )
            half = slice(head * HID, (head + 1) * HID)
            contexts.append(context[half] / total)
            log_ref[0, head : head + 1, at] = peak + jnp.log(total)
        merged = jnp.concatenate(contexts, axis=0).T.astype(bf16)
        query_s[0, at, :] = merged
    for block in range(GROUP):
        ctx_ref[block, 0] = query_s[0, block * rows : (block + 1) * rows, :]


def backward_kernel(
    order_ref,
    parent_ref,
    slope_ref,
    packed_ref,
    ctx_ref,
    grad_ref,
    log_ref,
    out_ref,
    query_s,
    key_s,
    value_s,
    grad_s,
    dkey_s,
    dvalue_s,
    dquery_s,
):
    micro = pl.program_id(0)
    rows = TREE // GROUP
    load_tree(order_ref, packed_ref, query_s, key_s, slope_ref, micro)
    lane = lax.broadcasted_iota(jnp.int32, (rows, 128), 1)
    zero = jnp.zeros((rows, 128), bf16)
    for block in range(GROUP):
        at = pl.ds(block * rows, rows)
        value = packed_ref[0, order_ref[micro, block]][:, 256:384]
        grad = grad_ref[block, 0]
        for head in range(2):
            mine = (lane < HID) if head == 0 else (lane >= HID)
            value_s[head, at, :] = jnp.where(mine, value, zero)
            grad_s[head, at, :] = jnp.where(mine, grad, zero)
        dquery_s[at, :] = grad.astype(f32) * ctx_ref[block, 0].astype(f32)
    dkey_s[...] = jnp.zeros_like(dkey_s)
    dvalue_s[...] = jnp.zeros_like(dvalue_s)
    masks = tile_masks()
    for tile in range(TREE // ROWS):
        trunk, last, own, leaves = tile_pieces(tile)
        at = slice(tile * ROWS, (tile + 1) * ROWS)
        deltas = dquery_s[at, :].T
        dqueries = []
        for head in range(2):
            half = slice(head * HID, (head + 1) * HID)
            query = query_s[head, at, :]
            grad = grad_s[head, at, :]
            keys = key_s.at[head]
            values = value_s.at[head]
            side = [
                jnp.concatenate(
                    [key_s[head, parent_rows(parent_ref, micro, leaf), :] for leaf in pair]
                )
                for pair in leaves
            ]
            pieces = tile_scores(tile, keys, query, parent_ref, micro, masks, side)
            level = log_ref[0, head : head + 1, at]
            delta = deltas[half].sum(axis=0, keepdims=True)
            ntrunk = len(pieces) - bool(own) - bool(leaves)
            dquery = jnp.zeros((128, ROWS), f32)
            start = 0
            for piece in pieces[:ntrunk]:
                size = piece.shape[0]
                span = slice(start, start + size)
                probs = jnp.exp(piece - level)
                dprobs = mm(values[span, :], grad, NT)
                dscores = (probs * (dprobs - delta)).astype(bf16)
                dvalue_s[span, :] += mm(probs.astype(bf16), grad, NN)
                dkey_s[head, span, :] += mm(dscores, query, NN)
                dquery = dquery + mm(keys[span, :], dscores, TN)
                start += size
            extra = []
            for i, first in enumerate(own):
                cols = slice(i * HALF, (i + 1) * HALF)
                span = slice(first, first + HALF)
                probs = jnp.exp(pieces[ntrunk][:, cols] - level[:, cols])
                dprobs = mm(values[span, :], grad[cols], NT)
                dscores = (probs * (dprobs - delta[:, cols])).astype(bf16)
                dvalue_s[span, :] += mm(probs.astype(bf16), grad[cols], NN)
                dkey_s[head, span, :] += mm(dscores, query[cols], NN)
                extra.append(mm(keys[span, :], dscores, TN))
            if own:
                dquery = dquery + jnp.concatenate(extra, axis=1)
            extra = []
            for i, pair in enumerate(leaves):
                cols = slice(i * HALF, (i + 1) * HALF)
                side_value = jnp.concatenate(
                    [value_s[head, parent_rows(parent_ref, micro, leaf), :] for leaf in pair]
                )
                probs = jnp.exp(pieces[ntrunk + 1][:, cols] - level[:, cols])
                dprobs = mm(side_value, grad[cols], NT)
                dscores = (probs * (dprobs - delta[:, cols])).astype(bf16)
                dval = mm(probs.astype(bf16), grad[cols], NN)
                dkey = mm(dscores, query[cols], NN)
                for j, leaf in enumerate(pair):
                    span = parent_rows(parent_ref, micro, leaf)
                    dvalue_s[span, :] += dval[j * SEG : (j + 1) * SEG]
                    dkey_s[head, span, :] += dkey[j * SEG : (j + 1) * SEG]
                extra.append(mm(side[i], dscores, TN))
            if leaves:
                dquery = dquery + jnp.concatenate(extra, axis=1)
            dqueries.append(dquery[half] * 0.125)
        dquery_s[at, :] = jnp.concatenate(dqueries, axis=0).T
    for block in range(GROUP):
        at = slice(block * rows, (block + 1) * rows)
        slot = order_ref[micro, block]
        dkey = jnp.where(lane < HID, dkey_s[0, at, :], dkey_s[1, at, :])
        out_ref[0, slot] = jnp.concatenate(
            (dquery_s[at, :].astype(bf16), dkey.astype(bf16), dvalue_s[at, :].astype(bf16)), axis=1
        )


def attention_forward(order, parents, slopes, packed):
    micro_count, _, rows, width = packed.shape
    return pl.pallas_call(
        forward_kernel,
        out_shape=(
            jax.ShapeDtypeStruct((GROUP, micro_count, rows, 128), bf16),
            jax.ShapeDtypeStruct((micro_count, 8, TREE), f32),
        ),
        grid_spec=pltpu.PrefetchScalarGridSpec(
            num_scalar_prefetch=3,
            grid=(micro_count,),
            in_specs=[pl.BlockSpec((1, GROUP, rows, width), lambda m, *_: (m, 0, 0, 0))],
            out_specs=(
                pl.BlockSpec((GROUP, 1, rows, 128), lambda m, *_: (0, m, 0, 0)),
                pl.BlockSpec((1, 8, TREE), lambda m, *_: (m, 0, 0)),
            ),
            scratch_shapes=[
                pltpu.VMEM((2, TREE, 128), bf16),
                pltpu.VMEM((2, TREE, 128), bf16),
                pltpu.VMEM((TREE, 128), bf16),
            ],
        ),
        compiler_params=pltpu.CompilerParams(vmem_limit_bytes=40 << 20),
        cost_estimate=pl.CostEstimate(
            flops=4_000_000_000, transcendentals=3_000_000, bytes_accessed=3_000_000
        ),
        name="tree_attention",
    )(order, parents, slopes, packed)


def attention_backward(order, parents, slopes, packed, ctx, grad, logs):
    micro_count, _, rows, width = packed.shape
    return pl.pallas_call(
        backward_kernel,
        out_shape=jax.ShapeDtypeStruct(packed.shape, bf16),
        grid_spec=pltpu.PrefetchScalarGridSpec(
            num_scalar_prefetch=3,
            grid=(micro_count,),
            in_specs=[
                pl.BlockSpec((1, GROUP, rows, width), lambda m, *_: (m, 0, 0, 0)),
                pl.BlockSpec((GROUP, 1, rows, 128), lambda m, *_: (0, m, 0, 0)),
                pl.BlockSpec((GROUP, 1, rows, 128), lambda m, *_: (0, m, 0, 0)),
                pl.BlockSpec((1, 8, TREE), lambda m, *_: (m, 0, 0)),
            ],
            out_specs=pl.BlockSpec((1, GROUP, rows, width), lambda m, *_: (m, 0, 0, 0)),
            scratch_shapes=[
                pltpu.VMEM((2, TREE, 128), bf16),
                pltpu.VMEM((2, TREE, 128), bf16),
                pltpu.VMEM((2, TREE, 128), bf16),
                pltpu.VMEM((2, TREE, 128), bf16),
                pltpu.VMEM((2, TREE, 128), f32),
                pltpu.VMEM((TREE, 128), f32),
                pltpu.VMEM((TREE, 128), f32),
            ],
        ),
        compiler_params=pltpu.CompilerParams(vmem_limit_bytes=48 << 20),
        cost_estimate=pl.CostEstimate(
            flops=10_000_000_000, transcendentals=3_000_000, bytes_accessed=6_000_000
        ),
        name="tree_attention_back",
    )(order, parents, slopes, packed, ctx, grad, logs)


def on_device(
    tokens,
    grad_out,
    w_query,
    w_key,
    w_value,
    b_query,
    b_value,
    w_attn_out,
    b_attn_out,
    w_up,
    b_up,
    w_down,
    b_down,
    ln1_gain,
    ln1_bias,
    ln2_gain,
    ln2_bias,
    leaf_parent,
):
    micro_count, row_count, width = tokens.shape
    count = lax.axis_size("dp")
    planes = count // GROUP
    index = lax.axis_index("dp")
    place = index % GROUP
    plane = index // GROUP
    wrow = w_query.shape[0]
    frow = w_down.shape[0]
    head_width = width // GROUP
    unit_width = planes * frow
    both = range(micro_count)

    gathered_x = plane_gather([tokens[m] for m in both])

    def by_place(weight, shape):
        return weight.reshape(shape)

    packed_w = jnp.concatenate(
        [w.reshape(wrow, GROUP, head_width) for w in (w_query, w_key, w_value)], axis=2
    ).transpose(1, 0, 2)
    up_w = w_up.reshape(wrow, planes, GROUP, frow).transpose(2, 0, 1, 3)
    up_w = up_w.reshape(GROUP, wrow, unit_width)
    small = (b_query, b_value, b_attn_out, b_down, ln1_gain, ln1_bias, ln2_gain, ln2_bias, b_up)
    vector = jnp.concatenate(small)
    lanes = packed_w.shape[2] + unit_width
    vector = jnp.pad(vector, (0, lanes - vector.shape[0]))
    sent = jnp.concatenate((packed_w, up_w), axis=2)
    sent = jnp.concatenate((sent, jnp.broadcast_to(vector, (GROUP, 1, lanes))), axis=1)
    got = plane_exchange(sent)
    qkv_rows = column_gather(got[:, :, : 3 * head_width], plane)
    mat_qkv = qkv_rows[:, :, :wrow].reshape(width, 3 * head_width)
    vectors = qkv_rows[:, :, wrow].reshape(count, 3 * head_width)
    bounds = [0]
    for piece in small:
        bounds.append(bounds[-1] + piece.shape[0])
    (
        vec_query,
        vec_value,
        vec_out,
        vec_down,
        gain_one,
        shift_one,
        gain_two,
        shift_two,
        vec_up,
    ) = [
        vectors[:, bounds[at] : bounds[at + 1]].reshape(-1).astype(f32)
        for at in range(len(small))
    ]
    vec_up = lax.dynamic_index_in_dim(
        vec_up.reshape(planes, GROUP, frow), place, 1, keepdims=False
    ).reshape(-1)
    zero_vec = jnp.zeros((head_width,), f32)
    vec_qkv = jnp.concatenate(
        (
            lax.dynamic_slice_in_dim(vec_query, place * head_width, head_width),
            zero_vec,
            lax.dynamic_slice_in_dim(vec_value, place * head_width, head_width),
        )
    )

    ffn_rows = lax.all_gather(
        jnp.concatenate(
            (got[:, :wrow, 3 * head_width :].reshape(-1, unit_width), w_down.reshape(-1, unit_width))
        ),
        "dp",
        axis=0,
        axis_index_groups=column_groups(),
    )
    mat_up = ffn_rows[:, : GROUP * wrow].reshape(width, unit_width)
    mat_down = ffn_rows[:, GROUP * wrow :].reshape(unit_width, width)
    mat_out = lax.all_gather(w_attn_out, "dp", axis=0, tiled=True)

    gathered_dy = plane_gather([grad_out[m] for m in both])
    groups = [(m, half) for m in both for half in range(2)]

    normed1 = {}
    packed = []
    for m in both:
        parts = []
        for half in range(2):
            values = gathered_x[m][half].reshape(-1, width).astype(f32)
            unit, _ = layer_norm_parts(values)
            normed1[m, half] = (unit * gain_one + shift_one).astype(bf16)
            parts.append(
                (mm(normed1[m, half], mat_qkv, NN) + vec_qkv)
                .astype(bf16)
                .reshape(4, row_count, 3 * head_width)
            )
        packed.append(jnp.concatenate(parts))
    packed = jnp.stack(packed)

    blocks = place ^ jnp.arange(GROUP, dtype=jnp.int32)
    slots = []
    for m in both:
        table = [0] * GROUP
        for at, mask in enumerate((0, FIRST[m], SECOND[m], FIRST[m] ^ SECOND[m])):
            table[mask] = at
            table[mask ^ 1] = at + 4
        hit = blocks[:, None] == jnp.arange(GROUP, dtype=jnp.int32)[None, :]
        slots.append(
            jnp.sum(jnp.where(hit, jnp.asarray(table, jnp.int32)[None, :], 0), axis=1)
        )
    order = jnp.stack(slots).astype(jnp.int32)
    parents = lax.dynamic_index_in_dim(leaf_parent, plane, 1, keepdims=False)
    heads = 2 * place + jnp.arange(2, dtype=jnp.int32)
    slopes = jnp.exp2(-8.0 * (heads.astype(f32) + 1.0) / HEADS)
    context, logs = attention_forward(order, parents, slopes, packed)
    own_context = plane_exchange(context)
    own_context = own_context.transpose(1, 2, 0, 3).reshape(micro_count * row_count, width)

    resid = tokens.reshape(-1, width).astype(f32)
    middle = resid + mm(own_context, mat_out, NN) + vec_out
    unit2, scale2 = layer_norm_parts(middle)
    normed2 = (unit2 * gain_two + shift_two).astype(bf16)
    normed2 = normed2.reshape(micro_count, row_count, width)
    gathered_a2 = plane_gather([normed2[m] for m in both])

    down_even, down_odd, back_even, back_odd = [], [], [], []
    grad_up = grad_down = grad_vec_up = 0.0
    for m, half in groups:
        a2 = gathered_a2[m][half].reshape(-1, width)
        dy = gathered_dy[m][half].reshape(-1, width)
        upper = mm(a2, mat_up, NN) + vec_up
        active, pull = jax.vjp(gelu_tanh, upper)
        active = active.astype(bf16)
        y_part = mm(active, mat_down, NN).reshape(4, row_count, width)
        du = pull(mm(dy, mat_down, NT))[0].astype(bf16)
        da_part = mm(du, mat_up, NT).reshape(4, row_count, width)
        (down_odd if half else down_even).append(y_part)
        (back_odd if half else back_even).append(da_part)
        grad_down = grad_down + mm(active, dy, TN)
        grad_up = grad_up + mm(a2, du, TN)
        grad_vec_up = grad_vec_up + jnp.sum(du, axis=0, dtype=f32)
    grad_normed2 = plane_scatter(back_even, back_odd)
    ffn_out = plane_scatter(down_even, down_odd)
    output = (
        middle.reshape(tokens.shape) + jnp.stack(ffn_out) + vec_down
    ).astype(bf16)

    grad_y = grad_out.reshape(-1, width).astype(f32)
    grad_normed2 = jnp.stack(grad_normed2).reshape(-1, width)
    grad_gain_two = jnp.sum(grad_normed2 * unit2, axis=0)
    grad_shift_two = jnp.sum(grad_normed2, axis=0)
    grad_middle = grad_y + layer_norm_back(grad_normed2, unit2, scale2, gain_two)
    grad_attn = grad_middle.astype(bf16)
    grad_ctx = mm(grad_attn, mat_out, NT).astype(bf16)
    grad_ctx = grad_ctx.reshape(micro_count, row_count, GROUP, head_width).transpose(2, 0, 1, 3)
    plane_grad_ctx = plane_exchange(grad_ctx)
    grad_out_mat = mm(own_context, grad_attn, TN)
    grad_vec_out = jnp.sum(grad_attn, axis=0, dtype=f32)
    grad_vec_down = jnp.sum(grad_y, axis=0)

    grad_packed = attention_backward(
        order, parents, slopes, packed, context, plane_grad_ctx, logs
    )
    grad_qkv = grad_vec_qkv = 0.0
    first_even, first_odd = [], []
    grad_gain_one = grad_shift_one = 0.0
    for m, half in groups:
        dqkv = grad_packed[m, 4 * half : 4 * half + 4].reshape(-1, 3 * head_width)
        da1 = mm(dqkv, mat_qkv, NT)
        (first_odd if half else first_even).append(da1.reshape(4, row_count, width))
        grad_qkv = grad_qkv + mm(normed1[m, half], dqkv, TN)
        grad_vec_qkv = grad_vec_qkv + jnp.sum(dqkv, axis=0, dtype=f32)
    grad_normed1 = jnp.stack(plane_scatter(first_even, first_odd)).reshape(-1, width)
    unit1, scale1 = layer_norm_parts(resid)
    grad_gain_one = jnp.sum(grad_normed1 * unit1, axis=0)
    grad_shift_one = jnp.sum(grad_normed1, axis=0)
    grad_input = grad_middle + layer_norm_back(grad_normed1, unit1, scale1, gain_one)
    grad_input = grad_input.astype(bf16).reshape(tokens.shape)

    sum_down = column_scatter(grad_down.reshape(planes, frow, width), plane)
    sum_up = column_scatter(grad_up.reshape(planes, GROUP * wrow, unit_width), plane)
    sum_qkv = column_scatter(grad_qkv.reshape(planes, GROUP * wrow, 3 * head_width), plane)
    home = plane_exchange(
        jnp.concatenate((sum_qkv, sum_up), axis=1).reshape(GROUP, wrow, lanes)
    )
    home_up = home[:, :, 3 * head_width :].reshape(GROUP, wrow, planes, frow)
    home_up = home_up.transpose(1, 2, 0, 3).reshape(wrow, -1)
    home_qkv = [
        home[:, :, at * head_width : (at + 1) * head_width].transpose(1, 0, 2).reshape(wrow, width)
        for at in range(3)
    ]
    sum_out = lax.psum_scatter(
        grad_out_mat.astype(bf16), "dp", scatter_dimension=0, tiled=True
    ).astype(f32)

    def placed(piece):
        return lax.dynamic_update_slice_in_dim(
            jnp.zeros((width,), f32), piece, place * head_width, 0
        )

    up_terms = lax.dynamic_update_slice_in_dim(
        jnp.zeros((planes, GROUP, frow), f32),
        grad_vec_up.reshape(planes, 1, frow),
        place,
        1,
    )
    terms = jnp.concatenate(
        [
            piece.reshape(count, -1)
            for piece in (
                placed(grad_vec_qkv[:head_width]),
                placed(grad_vec_qkv[2 * head_width :]),
                grad_vec_out,
                grad_vec_down,
                grad_gain_one,
                grad_shift_one,
                grad_gain_two,
                grad_shift_two,
                up_terms,
            )
        ],
        axis=1,
    )
    sums = jnp.sum(lax.all_to_all(terms, "dp", 0, 0, tiled=True), axis=0)
    pieces = [sums[bounds[at] : bounds[at + 1]] for at in range(len(small))]
    return (
        output,
        grad_input,
        home_qkv[0],
        home_qkv[1],
        home_qkv[2],
        sum_out,
        home_up,
        sum_down,
        pieces[0],
        pieces[1],
        pieces[2],
        pieces[8],
        pieces[3],
        pieces[4],
        pieces[5],
        pieces[6],
        pieces[7],
    )


def solution(mesh):
    row = P("dp", None)
    vec = P("dp")
    tok = P(None, "dp", None)
    return jax.shard_map(
        on_device,
        mesh=mesh,
        in_specs=(
            tok, tok, row, row, row, vec, vec, row, vec, row, vec, row, vec, vec, vec, vec, vec, P(),
        ),
        out_specs=(
            tok, tok, row, row, row, row, row, row, vec, vec, vec, vec, vec, vec, vec, vec, vec,
        ),
        check_vma=False,
    )
```

```python
from functools import partial

import jax
import jax.numpy as jnp
from jax import lax
from jax.experimental import pallas as pl
from jax.experimental.pallas import tpu as pltpu
from jax.sharding import PartitionSpec as P

HEADS = 16
BLK = 32
TRUNK_BLK = 16
SEG_BLK = 2
BRANCHES = 4
LEAVES = 8
TREE_BLK = 40

GROUP = 8
TREE = TREE_BLK * BLK
TRUNK = TRUNK_BLK * BLK
SEG = SEG_BLK * BLK
ROWS = 256
HALF = 128
HID = 64
NEG = -1e30

eps = 1e-05
bf16 = jnp.bfloat16
f32 = jnp.float32


def swap(value, mask, group=None):
    count = lax.axis_size("dp")
    pairs = [(source, source ^ mask) for source in range(count)]
    return lax.ppermute(value, "dp", pairs)


def after(value, *others):
    return lax.optimization_barrier((value, *others))[0]


class Chain:
    def __init__(self):
        self.last = None

    def hold(self, value):
        if self.last is None:
            return value
        return after(value, self.last)


chain = Chain()


class Part:
    def __init__(self, array, micro=None, turned=False, far=False, rows=None):
        self.array, self.micro, self.turned, self.far, self.rows = array, micro, turned, far or turned, rows

    def of(self, array):
        return Part(array, self.micro, self.turned, self.far, self.rows)


def far(array, micro=None, rows=None):
    return Part(array, micro, far=True, rows=rows)


def is_far(x):
    return isinstance(x, Part) and x.far


def array_of(x):
    return x.array if isinstance(x, Part) else x


def dims_of(x):
    if not isinstance(x, Part):
        return x.shape
    if x.rows is not None:
        return *x.array.shape[:-2], x.rows[1], x.array.shape[-1]
    if x.micro is None and not x.turned:
        return x.array.shape
    if x.turned:
        places, planes, rows, width = x.array.shape
        return places * planes * rows, width
    return x.array.shape[1:]


def pieces_of(dims, dtype):
    unit = 16 if dtype == bf16 else 8
    size = jnp.dtype(dtype).itemsize
    total = size
    for dim in dims:
        total *= dim
    if len(dims) == 3 and dims[0] >= 4:
        return [(at,) for at in range(dims[0])]
    lead = range(dims[0]) if len(dims) == 3 else [None]
    rows = dims[-2]
    best = 1
    for number in range(1, 9):
        if rows % (number * unit) == 0 and total // len(lead) // number >= 1 << 16:
            best = number
    step = rows // best
    cuts = [slice(at * step, (at + 1) * step) for at in range(best)]
    return [(cut,) if first is None else (first, cut) for first in lead for cut in cuts]


class Loaded:
    def __init__(self, x, source, target, semaphore):
        self.target, self.copy = target, None
        if x.turned:
            places, planes, rows, _ = x.array.shape
            for place in range(places):
                for plane in range(planes):
                    at = (plane * places + place) * rows
                    pltpu.make_async_copy(
                        source.at[place, plane], target.at[at : at + rows], semaphore
                    ).start()
            self.copy = pltpu.make_async_copy(target, target, semaphore)
            return
        if x.micro is not None:
            source = source.at[x.micro]
        if x.rows is not None:
            source = source.at[:, pl.ds(*x.rows)]
        for piece in pieces_of(target.shape, target.dtype):
            pltpu.make_async_copy(source.at[piece], target.at[piece], semaphore).start()
        self.copy = pltpu.make_async_copy(source, target, semaphore)

    def ready(self):
        if self.copy is not None:
            self.copy.wait()
            self.copy = None
        return self.target

    shape = property(lambda self: self.target.shape)
    dtype = property(lambda self: self.target.dtype)
    at = property(lambda self: self.ready().at)

    def __getitem__(self, index):
        return self.ready()[index]


class Stored:
    def __init__(self, x, target, source, semaphore):
        self.source, self.semaphore = source, semaphore
        self.target = target if x.micro is None else target.at[x.micro]
        if x.rows is not None:
            self.target = target.at[:, pl.ds(*x.rows)]
        self.gone = False

    shape = property(lambda self: self.source.shape)
    dtype = property(lambda self: self.source.dtype)
    at = property(lambda self: self.source.at)

    def __getitem__(self, index):
        return self.source[index]

    def __setitem__(self, index, value):
        self.source[index] = value

    def leave(self):
        if not self.gone:
            for piece in pieces_of(self.source.shape, self.source.dtype):
                pltpu.make_async_copy(
                    self.source.at[piece], self.target.at[piece], self.semaphore
                ).start()
            self.gone = True

    def done(self):
        pltpu.make_async_copy(self.source, self.target, self.semaphore).wait()


def leave(*refs):
    for ref in refs:
        if isinstance(ref, Stored):
            ref.leave()


def near(x, ref):
    return ref.at[x.micro] if isinstance(x, Part) and x.micro is not None else ref


def call(kernel, outs, args, name, scalars=(), scratch=(), flops=0, ordered=True, into=(), limit=12, group=None):
    args = list(args)
    if ordered:
        first = args[0]
        held = chain.hold(array_of(first))
        args[0] = first.of(held) if isinstance(first, Part) else held
    outside = lambda x: pltpu.with_memory_space_constraint(x, pltpu.HBM)
    arrays = [outside(x.array) if is_far(x) else array_of(x) for x in args]
    arrays += [outside(x) for x in into]
    shapes = [array_of(x) for x in outs]
    colored = [
        pltpu.HBM(x.shape, x.dtype) if is_far(out) else x for out, x in zip(outs, shapes)
    ]
    nscalar, nargs, nouts = len(scalars), len(args), len(outs)
    far_in = [i for i, x in enumerate(args) if is_far(x)]
    far_out = [i for i, x in enumerate(outs) if is_far(x)]

    def body(*refs):
        numbers = refs[:nscalar]
        inputs = list(refs[nscalar : nscalar + nargs])
        outputs = list(refs[nscalar + len(arrays) : nscalar + len(arrays) + nouts])
        rest = list(refs[nscalar + len(arrays) + nouts :])
        sems = rest[-2:]
        loaded = [
            Loaded(args[i], inputs[i], rest[k], sems[0].at[k]) for k, i in enumerate(far_in)
        ]
        stored = [
            Stored(outs[i], outputs[i], rest[len(far_in) + k], sems[1].at[k])
            for k, i in enumerate(far_out)
        ]
        inputs = [near(x, ref) for x, ref in zip(args, inputs)]
        outputs = [near(x, ref) for x, ref in zip(outs, outputs)]
        for k, i in enumerate(far_in):
            inputs[i] = loaded[k]
        for k, i in enumerate(far_out):
            outputs[i] = stored[k]
        kernel(*numbers, *inputs, *outputs, *rest[len(far_in) + len(far_out) : -2])
        for x in loaded:
            x.ready()
        leave(*stored)
        for x in stored:
            x.done()

    bytes_accessed = sum(x.size * x.dtype.itemsize for x in arrays + shapes)
    place = lambda x: pl.BlockSpec(memory_space=pltpu.HBM if is_far(x) else pltpu.VMEM)
    kernel_call = pl.pallas_call(
        body,
        out_shape=tuple(colored),
        in_specs=[pl.BlockSpec(memory_space=pltpu.SMEM)] * nscalar
        + [place(x) for x in args]
        + [pl.BlockSpec(memory_space=pltpu.HBM) for _ in into],
        out_specs=tuple(place(x) for x in outs),
        scratch_shapes=[pltpu.VMEM(dims_of(args[i]), array_of(args[i]).dtype) for i in far_in]
        + [pltpu.VMEM(dims_of(outs[i]), array_of(outs[i]).dtype) for i in far_out]
        + list(scratch)
        + [
            pltpu.SemaphoreType.DMA((max(1, len(far_in)),)),
            pltpu.SemaphoreType.DMA((max(1, len(far_out)),)),
        ],
        input_output_aliases={nscalar + nargs + i: i for i in range(len(into))},
        compiler_params=pltpu.CompilerParams(vmem_limit_bytes=limit << 20),
        cost_estimate=pl.CostEstimate(
            flops=flops, transcendentals=0, bytes_accessed=bytes_accessed
        ),
        name=name,
    )
    result = kernel_call(*scalars, *arrays)
    if ordered:
        chain.last = result[-1]
    return result


def shape(dims, dtype=bf16):
    return jax.ShapeDtypeStruct(dims, dtype)


def kinds(dims, masks=range(GROUP)):
    return [shape(dims, bf16 if mask else f32) for mask in masks]


def plane_gather(own, sides=None, corners=None):
    side = {2: swap(own, 2, sides), 4: swap(own, 4, sides)}
    corner = [swap(side[2][0], 4, corners), swap(side[4][1], 2, corners)]
    even = {0: own, 2: side[2], 4: side[4]}
    blocks = [even[mask] if mask in even else swap(even[mask ^ 1], 1) for mask in range(6)]
    return [[block] for block in blocks] + [corner, [swap(c, 1) for c in corner]]


def of_micro(blocks, m):
    return Part(blocks[0], m) if len(blocks) == 1 else blocks[m]


def add_kernel(plan, *refs):
    ninputs = len(refs) - len(plan)
    for out_ref, rows in zip(refs[ninputs:], plan):
        for lead, addends in enumerate(rows):
            total = None
            for number, at in addends:
                value = (refs[number][...] if at is None else refs[number][at]).astype(f32)
                total = value if total is None else total + value
            if len(rows) == 1:
                out_ref[...] = total.astype(out_ref.dtype)
            else:
                out_ref[lead] = total.astype(out_ref.dtype)


def swap_back(parts):
    masks = (6, 2, 4, 0)
    return dict(zip(masks, lax.optimization_barrier([swap(parts[mask ^ 1], 1) for mask in masks])))


class Scatter:
    def __init__(self, parts):
        self.parts = parts
        self.back = swap_back([array_of(part) for part in parts])

    def first(self, group=None):
        dims = dims_of(self.parts[6])[1:]
        plan = [[[(0, m), (1, m)]] for m in range(2)]
        total = call(partial(add_kernel, plan), [shape(dims)] * 2, [self.back[6], self.parts[6]], "corner")
        self.corner = swap(total[0], 4, group), swap(total[1], 2, group)

    def second(self, group=None):
        dims = dims_of(self.parts[2])
        plan = [
            [[(0, 0), (1, 0), (4, None)], [(0, 1), (1, 1)]],
            [[(2, 0), (3, 0)], [(2, 1), (3, 1), (5, None)]],
        ]
        total = call(
            partial(add_kernel, plan), [shape(dims)] * 2,
            [self.back[2], self.parts[2], self.back[4], self.parts[4], *self.corner], "sides",
        )
        self.sides = swap(total[0], 2, group), swap(total[1], 4, group)

    def addends(self):
        return self.parts[0], self.back[0], *self.sides


class ScatterOne:
    def __init__(self, parts, micro):
        self.parts = parts
        self.via = 4 if micro == 0 else 2
        self.back = swap_back(parts)

    def first(self, group=None):
        total = call(
            partial(add_kernel, [[[(0, None), (1, None)]]]), [shape(self.parts[6].shape)],
            [self.back[6], self.parts[6]], "corner",
        )[0]
        self.corner = swap(total, self.via, group)

    def second(self, group=None):
        via = self.via
        plan = [[[(0, None), (1, None)]], [[(2, None), (3, None), (4, None)]]]
        total = call(
            partial(add_kernel, plan), [shape(self.parts[6].shape)] * 2,
            [self.back[via], self.parts[via], self.back[6 ^ via], self.parts[6 ^ via], self.corner], "sides",
        )
        self.sides = swap(total[0], via, group), swap(total[1], 6 ^ via, group)

    def addends(self):
        return self.parts[0], self.back[0], *self.sides


def plane_groups():
    count = lax.axis_size("dp")
    return [list(range(first, first + GROUP)) for first in range(0, count, GROUP)]


def column_groups():
    count = lax.axis_size("dp")
    return [list(range(place, count, GROUP)) for place in range(GROUP)]


def plane_exchange(value):
    return lax.all_to_all(value, "dp", 0, 0, tiled=True, axis_index_groups=plane_groups())


def column_parts(value, group=None):
    planes = lax.axis_size("dp") // GROUP
    if planes > 4:
        return [
            lax.all_gather(value, "dp", axis=0, axis_index_groups=column_groups(), tiled=True)
        ]
    return [value] + [swap(value, GROUP * step, group) for step in range(1, planes)]


def column_send(parts, group=None):
    return [swap(part, GROUP * (step + 1), group) for step, part in enumerate(parts)]


def few(planes):
    return planes <= 4


def order_kernel(wrow, plane_ref, *refs):
    *parts, mat_ref, out_ref = refs
    rows = mat_ref.shape[0] // len(parts)
    for step, part in enumerate(parts):
        plane = plane_ref[0] ^ step
        at = pl.ds(pl.multiple_of(plane * rows, rows), rows)
        for i in range(3):
            mat_ref[at, i * 128 : (i + 1) * 128] = part[i * rows : (i + 1) * rows]
        for i in range(GROUP):
            start = 3 * rows + i * wrow
            out_ref[plane, :, i * 128 : (i + 1) * 128] = part[start : start + wrow]


def ffn_order_kernel(plane_ref, *refs):
    *parts, up_ref, down_ref = refs
    rows, units = up_ref.shape[0] // len(parts), up_ref.shape[1]
    frow = units // len(parts)
    for step, part in enumerate(parts):
        plane = plane_ref[0] ^ step
        up_ref[pl.ds(pl.multiple_of(plane * rows, rows), rows), :] = part[0:rows]
        at = pl.ds(pl.multiple_of(plane * frow, frow), frow)
        down_ref[at, 0:units] = part[rows : rows + frow]
        down_ref[at, units:] = part[rows + frow :]


def mm(left, right, contract):
    return lax.dot_general(left, right, (contract, ((), ())), preferred_element_type=f32)


NN = ((1,), (0,))
NT = ((1,), (1,))
TN = ((0,), (0,))


def split3(values):
    high = values.astype(bf16)
    rest = values - high.astype(f32)
    middle = rest.astype(bf16)
    low = (rest - middle.astype(f32)).astype(bf16)
    return high, middle, low


def norm_parts(values):
    center = values - jnp.mean(values, axis=-1, keepdims=True)
    spread = jnp.mean(center * center, axis=-1, keepdims=True)
    scale = lax.rsqrt(spread + eps)
    return center * scale, scale


def norm_back(grad, unit, scale, gain):
    scaled = grad * gain
    return scale * (
        scaled
        - jnp.mean(scaled, axis=-1, keepdims=True)
        - unit * jnp.mean(scaled * unit, axis=-1, keepdims=True)
    )


def fill_heads(query, key, slope_ref, query_s, key_s, place, start, rows):
    lane = lax.broadcasted_iota(jnp.int32, (rows, 128), 1)
    one = jnp.ones((rows, 128), bf16)
    zero = jnp.zeros((rows, 128), bf16)
    at = pl.ds(start, rows)
    for head in range(2):
        mine = (lane < HID) if head == 0 else (lane >= HID)
        base = HID if head == 0 else 0
        high, middle, low = split3(place * slope_ref[head])
        extra = jnp.where(
            lane == base,
            high,
            jnp.where(lane == base + 1, middle, jnp.where(lane == base + 2, low, zero)),
        )
        ones = jnp.where((lane >= base) & (lane < base + 3), one, zero)
        query_s[head, at, :] = jnp.where(mine, query, ones)
        key_s[head, at, :] = jnp.where(mine, key, extra)


def positions(start, rows):
    row = lax.broadcasted_iota(jnp.int32, (rows, 128), 0) + start
    after_trunk = row - TRUNK
    inside = after_trunk & (SEG - 1)
    return jnp.where(
        row < TRUNK, row, TRUNK + inside + jnp.where(after_trunk < BRANCHES * SEG, 0, SEG)
    ).astype(f32)


def tile_masks():
    row = lax.broadcasted_iota(jnp.int32, (HALF, HALF), 1)
    col = lax.broadcasted_iota(jnp.int32, (HALF, HALF), 0)
    same = (row // SEG) == (col // SEG)
    segment = jnp.where(same & (col <= row), 0.0, NEG)
    parent = jnp.where(same, 0.0, NEG)
    trow = lax.broadcasted_iota(jnp.int32, (ROWS, ROWS), 1)
    tcol = lax.broadcasted_iota(jnp.int32, (ROWS, ROWS), 0)
    causal = jnp.where(tcol <= trow, 0.0, NEG)
    return segment, parent, causal


def parent_rows(parent_ref, leaf):
    start = TRUNK + (parent_ref[leaf] - 1) * SEG
    return pl.ds(pl.multiple_of(start, SEG), SEG)


def tile_pieces(tile):
    if tile < TRUNK // ROWS:
        return (tile + 1) * ROWS, True, [], []
    start = tile * ROWS
    own = [start, start + HALF]
    first_leaf = TRUNK + BRANCHES * SEG
    leaves = []
    if start >= first_leaf:
        leaf = (start - first_leaf) // SEG
        leaves = [(leaf, leaf + 1), (leaf + 2, leaf + 3)]
    return TRUNK, False, own, leaves


def tile_scores(tile, key_ref, query, masks, side):
    segment, parent, causal = masks
    trunk, last, own, leaves = tile_pieces(tile)
    scores = mm(key_ref[0:trunk, :], query, NT)
    pieces = []
    if last:
        if trunk > ROWS:
            pieces.append(scores[: trunk - ROWS])
        pieces.append(scores[trunk - ROWS :] + causal)
    else:
        pieces.append(scores)
    if own:
        pieces.append(
            jnp.concatenate(
                [
                    mm(key_ref[at : at + HALF, :], query[i * HALF : (i + 1) * HALF], NT) + segment
                    for i, at in enumerate(own)
                ],
                axis=1,
            )
        )
    if leaves:
        pieces.append(
            jnp.concatenate(
                [
                    mm(rows, query[i * HALF : (i + 1) * HALF], NT) + parent
                    for i, rows in enumerate(side)
                ],
                axis=1,
            )
        )
    return pieces


def forward_kernel(
    micro, place_ref, parent_ref, slope_ref,
    a0, a1, a2, a3, a4, a5, a6, a7, vec_ref, mat_ref, bias_ref,
    ctx_ref, log_ref, packed_ref, unit_ref,
    query_s, key_s, value_s, ctx_s,
):
    rows = TREE // GROUP
    for mask, block_ref in zip((1, 2, 3, 4, 5, 0, 6, 7), (a1, a2, a3, a4, a5, a0, a6, a7)):
        start = pl.multiple_of((place_ref[0] ^ mask) * rows, rows)
        unit, _ = norm_parts(block_ref[...].astype(f32))
        unit_ref[mask] = unit.astype(bf16)
        normed = (unit * vec_ref[0:1] + vec_ref[1:2]).astype(bf16)
        part = (mm(normed, mat_ref[...], NN) + bias_ref[...]).astype(bf16)
        packed_ref.source[pl.ds(start, rows), :] = part
        value_s[pl.ds(start, rows), :] = part[:, 256:384]
        fill_heads(
            part[:, 0:128] * jnp.asarray(0.125, bf16), part[:, 128:256],
            slope_ref, query_s, key_s, positions(start, rows), start, rows,
        )
    leave(unit_ref, packed_ref)
    masks = tile_masks()
    for tile in range(TREE // ROWS):
        trunk, last, own, leaves = tile_pieces(tile)
        at = slice(tile * ROWS, (tile + 1) * ROWS)
        contexts = []
        side_values = [
            jnp.concatenate([value_s[parent_rows(parent_ref, leaf), :] for leaf in pair])
            for pair in leaves
        ]
        for head in range(2):
            query = query_s[head, at, :]
            side = [
                jnp.concatenate([key_s[head, parent_rows(parent_ref, leaf), :] for leaf in pair])
                for pair in leaves
            ]
            pieces = tile_scores(tile, key_s.at[head], query, masks, side)
            peak = pieces[0].max(axis=0, keepdims=True)
            for piece in pieces[1:]:
                peak = jnp.maximum(peak, piece.max(axis=0, keepdims=True))
            probs = [jnp.exp(piece - peak) for piece in pieces]
            total = probs[0].sum(axis=0, keepdims=True)
            for piece in probs[1:]:
                total = total + piece.sum(axis=0, keepdims=True)
            probs = [piece.astype(bf16) for piece in probs]
            ntrunk = len(probs) - bool(own) - bool(leaves)
            start = 0
            context = None
            for piece in probs[:ntrunk]:
                term = mm(value_s[start : start + piece.shape[0], :], piece, TN)
                context = term if context is None else context + term
                start += piece.shape[0]
            if own:
                context = context + jnp.concatenate(
                    [
                        mm(value_s[first : first + HALF, :], probs[ntrunk][:, i * HALF : (i + 1) * HALF], TN)
                        for i, first in enumerate(own)
                    ],
                    axis=1,
                )
            if leaves:
                context = context + jnp.concatenate(
                    [
                        mm(side_values[i], probs[ntrunk + 1][:, i * HALF : (i + 1) * HALF], TN)
                        for i in range(2)
                    ],
                    axis=1,
                )
            half = slice(head * HID, (head + 1) * HID)
            contexts.append(context[half] / total)
            log_ref[head : head + 1, at] = peak + jnp.log(total)
        ctx_s[at, :] = jnp.concatenate(contexts, axis=0).T.astype(bf16)
    for block in range(GROUP):
        ctx_ref[block] = ctx_s[block * rows : (block + 1) * rows, :]


def attention_forward(group, micro, place, parents, slopes, blocks, vec, mat, bias):
    rows, width = TREE // GROUP, mat.shape[0]
    return call(
        partial(forward_kernel, micro),
        [
            shape((GROUP, rows, 128)), shape((8, TREE), f32),
            far(shape((TREE, 384))), far(shape((GROUP, rows, width))),
        ],
        [*blocks, vec, mat, bias],
        "tree_attention",
        group=group,
        scalars=(place[None], parents, slopes),
        scratch=[
            pltpu.VMEM((2, TREE, 128), bf16),
            pltpu.VMEM((2, TREE, 128), bf16),
            pltpu.VMEM((TREE, 128), bf16),
            pltpu.VMEM((TREE, 128), bf16),
        ],
        flops=4_000_000_000,
        limit=20,
    )


def backward_kernel(
    micro, place_ref, parent_ref, slope_ref,
    grad_ref, packed_ref, ctx_ref, log_ref, mat_ref,
    o0, o1, o2, o3, o4, o5, o6, o7, dqkv_ref, sum_ref,
    query_s, key_s, value_s, grad_s, dkey_s, dvalue_s, dquery_s,
):
    rows = TREE // GROUP
    lane = lax.broadcasted_iota(jnp.int32, (rows, 128), 1)
    zero = jnp.zeros((rows, 128), bf16)
    for block in range(GROUP):
        start = block * rows
        at = pl.ds(start, rows)
        part = packed_ref[at, :]
        fill_heads(
            part[:, 0:128] * jnp.asarray(0.125, bf16), part[:, 128:256],
            slope_ref, query_s, key_s, positions(start, rows), start, rows,
        )
        value = part[:, 256:384]
        grad = grad_ref[block, micro]
        for head in range(2):
            mine = (lane < HID) if head == 0 else (lane >= HID)
            value_s[head, at, :] = jnp.where(mine, value, zero)
            grad_s[head, at, :] = jnp.where(mine, grad, zero)
        dquery_s[at, :] = grad.astype(f32) * ctx_ref[block].astype(f32)
    dkey_s[...] = jnp.zeros_like(dkey_s)
    dvalue_s[...] = jnp.zeros_like(dvalue_s)
    masks = tile_masks()
    for tile in range(TREE // ROWS):
        trunk, last, own, leaves = tile_pieces(tile)
        at = slice(tile * ROWS, (tile + 1) * ROWS)
        deltas = dquery_s[at, :].T
        dqueries = []
        for head in range(2):
            half = slice(head * HID, (head + 1) * HID)
            query = query_s[head, at, :]
            grad = grad_s[head, at, :]
            keys = key_s.at[head]
            values = value_s.at[head]
            side = [
                jnp.concatenate([key_s[head, parent_rows(parent_ref, leaf), :] for leaf in pair])
                for pair in leaves
            ]
            pieces = tile_scores(tile, keys, query, masks, side)
            level = log_ref[head : head + 1, at]
            delta = deltas[half].sum(axis=0, keepdims=True)
            ntrunk = len(pieces) - bool(own) - bool(leaves)
            dquery = None
            start = 0
            for piece in pieces[:ntrunk]:
                size = piece.shape[0]
                span = slice(start, start + size)
                probs = jnp.exp(piece - level)
                dprobs = mm(values[span, :], grad, NT)
                dscores = (probs * (dprobs - delta)).astype(bf16)
                dvalue_s[span, :] += mm(probs.astype(bf16), grad, NN)
                dkey_s[head, span, :] += mm(dscores, query, NN)
                term = mm(keys[span, :], dscores, TN)
                dquery = term if dquery is None else dquery + term
                start += size
            extra = []
            for i, first in enumerate(own):
                cols = slice(i * HALF, (i + 1) * HALF)
                span = slice(first, first + HALF)
                probs = jnp.exp(pieces[ntrunk][:, cols] - level[:, cols])
                dprobs = mm(values[span, :], grad[cols], NT)
                dscores = (probs * (dprobs - delta[:, cols])).astype(bf16)
                dvalue_s[span, :] += mm(probs.astype(bf16), grad[cols], NN)
                dkey_s[head, span, :] += mm(dscores, query[cols], NN)
                extra.append(mm(keys[span, :], dscores, TN))
            if own:
                dquery = dquery + jnp.concatenate(extra, axis=1)
            extra = []
            for i, pair in enumerate(leaves):
                cols = slice(i * HALF, (i + 1) * HALF)
                side_value = jnp.concatenate(
                    [value_s[head, parent_rows(parent_ref, leaf), :] for leaf in pair]
                )
                probs = jnp.exp(pieces[ntrunk + 1][:, cols] - level[:, cols])
                dprobs = mm(side_value, grad[cols], NT)
                dscores = (probs * (dprobs - delta[:, cols])).astype(bf16)
                dval = mm(probs.astype(bf16), grad[cols], NN)
                dkey = mm(dscores, query[cols], NN)
                for j, leaf in enumerate(pair):
                    span = parent_rows(parent_ref, leaf)
                    dvalue_s[span, :] += dval[j * SEG : (j + 1) * SEG]
                    dkey_s[head, span, :] += dkey[j * SEG : (j + 1) * SEG]
                extra.append(mm(side[i], dscores, TN))
            if leaves:
                dquery = dquery + jnp.concatenate(extra, axis=1)
            dqueries.append(dquery[half] * 0.125)
        dquery_s[at, :] = jnp.concatenate(dqueries, axis=0).T
    sums = jnp.zeros((1, 384), f32)
    for mask, out_ref in reversed(list(enumerate((o0, o1, o2, o3, o4, o5, o6, o7)))):
        at = pl.ds(pl.multiple_of((place_ref[0] ^ mask) * rows, rows), rows)
        dkey = jnp.where(lane < HID, dkey_s[0, at, :], dkey_s[1, at, :])
        dqkv = jnp.concatenate(
            (dquery_s[at, :].astype(bf16), dkey.astype(bf16), dvalue_s[at, :].astype(bf16)), axis=1
        )
        dqkv_ref[mask] = dqkv
        sums = sums + jnp.sum(dqkv.astype(f32), axis=0, keepdims=True)
        out_ref[...] = mm(dqkv, mat_ref[...], NT).astype(out_ref.dtype)
    sum_ref[...] = jnp.broadcast_to(sums, (8, 384))


def attention_backward(group, micro, place, parents, slopes, packed, ctx, grad, logs, mat):
    rows = TREE // GROUP
    width = mat.shape[0]
    result = call(
        partial(backward_kernel, micro),
        [*kinds((rows, width)), far(shape((GROUP, rows, 384))), shape((8, 384), f32)],
        [grad, far(packed), ctx, logs, mat],
        "tree_attention_back",
        group=group,
        scalars=(place[None], parents, slopes),
        scratch=[
            pltpu.VMEM((2, TREE, 128), bf16),
            pltpu.VMEM((2, TREE, 128), bf16),
            pltpu.VMEM((2, TREE, 128), bf16),
            pltpu.VMEM((2, TREE, 128), bf16),
            pltpu.VMEM((2, TREE, 128), f32),
            pltpu.VMEM((TREE, 128), f32),
            pltpu.VMEM((TREE, 128), f32),
        ],
        flops=10_000_000_000,
        limit=24,
    )
    return result[:GROUP], result[GROUP], result[GROUP + 1][0]


def project_kernel(p0, p1, x_ref, vec_ref, mat_ref, middle_ref, normed_ref, ctx_ref, total_s):
    micros, rows, width = middle_ref.shape
    for m, part in enumerate((p0, p1)):
        for block in range(GROUP):
            total_s[m * rows : (m + 1) * rows, block * 128 : (block + 1) * 128] = part[block]
    attn = mm(total_s[...], mat_ref[...], NN) + vec_ref[0:1]
    for m in range(micros):
        ctx_ref[m] = total_s[m * rows : (m + 1) * rows]
        middle = x_ref[m].astype(f32) + attn[m * rows : (m + 1) * rows]
        middle_ref[m] = middle
        unit, _ = norm_parts(middle)
        normed_ref[m] = (unit * vec_ref[1:2] + vec_ref[2:3]).astype(bf16)


def project(parts, x, vec, mat):
    dims = dims_of(x)
    return call(
        project_kernel,
        [shape(dims, f32), shape(dims), far(shape(dims))],
        [*parts, x, vec, mat],
        "project",
        scratch=[pltpu.VMEM((dims[0] * dims[1], dims[2]), bf16)],
        flops=2 * dims[0] * dims[1] * dims[2] * dims[2],
        limit=16,
    )


def rows_of(refs):
    if len(refs) == 1:
        micros, rows, width = refs[0].shape
        return refs[0][...].reshape(micros * rows, width)
    return jnp.concatenate([ref[...] for ref in refs])


def ffn_kernel(counts, *refs):
    refs = list(refs)

    def take(number):
        taken = refs[:number]
        del refs[:number]
        return taken

    a_refs = [take(number) for number in counts]
    dy_refs = [take(number) for number in counts]
    up_ref, down_ref, bias_ref = take(3)
    y_refs, da_refs = take(len(counts)), take(len(counts))
    act_ref, du_ref, sum_ref = refs
    sums = jnp.zeros((1, up_ref.shape[1]), f32)
    for i in range(len(counts)):
        upper = mm(rows_of(a_refs[i]), up_ref[...], NN) + bias_ref[...]
        square = upper * upper
        bent = jnp.tanh(upper * (0.7978845608028654 + (0.7978845608028654 * 0.044715) * square))
        half = 0.5 * (1.0 + bent)
        active = (upper * half).astype(bf16)
        slope = half + (0.5 * upper) * (1.0 - bent * bent) * (
            0.7978845608028654 + (3.0 * 0.7978845608028654 * 0.044715) * square
        )
        act_ref[i] = active
        du = mm(rows_of(dy_refs[i]), down_ref[...], NT) * slope
        sums = sums + jnp.sum(du, axis=0, keepdims=True)
        du = du.astype(bf16)
        du_ref[i] = du
        kind = da_refs[i].dtype
        da_refs[i][...] = mm(du, up_ref[...], NT).astype(kind).reshape(da_refs[i].shape)
        y_refs[i][...] = mm(active, down_ref[...], NN).astype(bf16).reshape(y_refs[i].shape)
        leave(y_refs[i])
    sum_ref[...] = jnp.broadcast_to(sums, sum_ref.shape)


def feed_forward(a, dy, masks, up, down, bias, more, group):
    counts = tuple(len(a[mask]) for mask in masks)
    micros, (rows, width), units = 2, array_of(a[masks[0]][0]).shape[-2:], up.shape[1]
    dims = (micros, rows, width)
    long = (micros, rows + more, width)
    number = len(masks)
    result = call(
        partial(ffn_kernel, counts),
        [far(shape(long), rows=(0, rows)) for _ in masks]
        + kinds(dims, masks)
        + [far(shape((number, micros * rows, units))) for _ in range(2)]
        + [shape((8, units), f32)],
        [x for mask in masks for x in a[mask]]
        + [far(x) for mask in masks for x in dy[mask]]
        + [up, down, bias],
        "feed_forward",
        group=group,
        flops=8 * number * micros * rows * width * units,
        limit=28,
    )
    return result[:number], result[number : 2 * number], result[-3], result[-2], result[-1][0]


def ffn_grads_kernel(counts, planes, plane_ref, *refs):
    refs = list(refs)

    def take(number):
        taken = refs[:number]
        del refs[:number]
        return taken

    a_refs = [take(number) for number in counts]
    act_refs, du_refs = take(3), take(3)
    dy_refs = [take(number) for number in counts]
    outs = refs
    units = du_refs[0].shape[-1]
    flat = lambda ref: ref[...].reshape(-1, units)
    width = a_refs[0][0].shape[-1]
    rows, frow = width // planes, units // planes
    du = jnp.concatenate([flat(ref) for ref in du_refs])
    for step in range(planes):
        at = pl.ds(pl.multiple_of((plane_ref[0] ^ step) * rows, 128), rows)
        parts = []
        for group in a_refs:
            for ref in group:
                part = ref[..., at]
                parts.append(part.reshape(-1, rows))
        outs[step][0:rows] = mm(jnp.concatenate(parts), du, TN).astype(outs[step].dtype)
    dy = jnp.concatenate([rows_of(group) for group in dy_refs])
    for step in range(planes):
        at = pl.ds(pl.multiple_of((plane_ref[0] ^ step) * frow, 128), frow)
        act = jnp.concatenate([ref.at[:, :, at][...].reshape(-1, frow) for ref in act_refs])
        down = mm(act, dy, TN).astype(outs[step].dtype)
        outs[step][rows : rows + frow] = down[:, :units]
        outs[step][rows + frow :] = down[:, units:]


def ffn_grads(a, dy, masks, act, du, plane, planes):
    counts = tuple(len(a[mask]) for mask in masks)
    width, units = array_of(a[masks[0]][0]).shape[-1], du[0].shape[-1]
    return call(
        partial(ffn_grads_kernel, counts, planes),
        kinds((width // planes + 2 * (units // planes), units), range(planes)),
        [x for mask in masks for x in a[mask]]
        + [far(x) for x in (*act, *du)]
        + [far(x) for mask in masks for x in dy[mask]],
        "ffn_grads",
        group=6,
        scalars=(plane[None],),
        flops=8 * TREE * width * units,
        limit=40,
    )


def second_back_kernel(
    own_ref, back_ref, first_ref, second_ref, dy_ref, middle_ref, vec_ref, mat_ref,
    dh_ref, dattn_ref, dctx_ref, sum_ref,
):
    micros, rows, width = middle_ref.shape
    sums = []
    for m in range(micros):
        grad = (
            own_ref[m].astype(f32)
            + back_ref[m].astype(f32)
            + first_ref[m].astype(f32)
            + second_ref[m].astype(f32)
        )
        unit, scale = norm_parts(middle_ref[m])
        dy = dy_ref[m].astype(f32)
        dh = dy + norm_back(grad, unit, scale, vec_ref[1:2])
        dh_ref[m] = dh
        dattn = dh.astype(bf16)
        dattn_ref[m] = dattn
        sums.append(
            [
                jnp.sum(value, axis=0, keepdims=True)
                for value in (dattn.astype(f32), dy, grad * unit, grad)
            ]
        )
    leave(dh_ref)
    dattn = dattn_ref[...].reshape(micros * rows, width)
    dctx = mm(dattn, mat_ref[...], NT).astype(bf16)
    for m in range(micros):
        for block in range(GROUP):
            dctx_ref[block, m] = dctx[m * rows : (m + 1) * rows, block * 128 : (block + 1) * 128]
    sum_ref[...] = jnp.concatenate(
        [first + second for first, second in zip(*sums)] + [jnp.zeros((4, width), f32)]
    )


def second_back(addends, dy, middle, vec, mat):
    dims = middle.shape
    return call(
        second_back_kernel,
        [
            far(shape(dims, f32)), shape(dims), shape((GROUP, dims[0], dims[1], 128)),
            shape((8, dims[2]), f32),
        ],
        [*addends, dy, middle, vec, mat],
        "norm2_back",
        flops=2 * middle.size * dims[2],
        limit=16,
    )


def first_back_kernel(*refs):
    groups, (x_ref, dh_ref, vec_ref, out_ref) = (refs[0:4], refs[4:8]), refs[8:]
    for m, group in enumerate(groups):
        grad = group[0][...].astype(f32)
        for ref in group[1:]:
            grad = grad + ref[...].astype(f32)
        unit, scale = norm_parts(x_ref[m].astype(f32))
        out_ref[m] = (dh_ref[m] + norm_back(grad, unit, scale, vec_ref[0:1])).astype(bf16)


def output_kernel(more, own_ref, back_ref, first_ref, second_ref, middle_ref, vec_ref, out_ref, *rest):
    micros, rows, width = middle_ref.shape
    for m in range(micros):
        part = slice(0, rows)
        total = own_ref[m, part].astype(f32) + back_ref[m, part].astype(f32)
        total = total + first_ref[m, part].astype(f32) + second_ref[m, part].astype(f32)
        out_ref[m] = (middle_ref[m] + (total + vec_ref[3:4])).astype(bf16)
    leave(out_ref)
    if more:
        part = slice(rows, rows + more)
        for m in range(micros):
            total = own_ref[m, part].astype(f32) + back_ref[m, part].astype(f32)
            total = total + first_ref[m, part].astype(f32) + second_ref[m, part].astype(f32)
            rest[0][m * more : (m + 1) * more] = total


def out_grads_kernel(planes, place_ref, dattn_ref, ctx_ref, *refs):
    outs, total_s = refs[:GROUP], refs[GROUP]
    total_s[...] = mm(rows_of([ctx_ref]), rows_of([dattn_ref]), TN)
    micros, more, _ = outs[0].shape
    size = micros * more // planes
    for mask in range(GROUP):
        for plane in range(planes):
            start = plane * GROUP * size + (place_ref[0] ^ mask) * size
            m, at = divmod(plane * size, more)
            outs[mask][m, at : at + size, :] = total_s[
                pl.ds(pl.multiple_of(start, size), size), :
            ].astype(bf16)
        leave(outs[mask])


def out_grads(place, ctx, dattn, parts, planes):
    width = dattn.shape[-1]
    rows = dattn.shape[1]
    more = parts[0].shape[1] - rows
    return call(
        partial(out_grads_kernel, planes),
        [far(shape(part.shape), rows=(rows, more)) for part in parts],
        [dattn, far(ctx)],
        "out_grads",
        scalars=(place[None],),
        scratch=[pltpu.VMEM((width, width), f32)],
        limit=16,
        flops=2 * dattn.size * width,
        into=parts,
    )


def qkv_grads_kernel(planes, plane_ref, sum_ref, g0, g1, u0, u1, mat_ref, vec_ref, rows_ref, *refs):
    own_ref, own_out_ref, *outs, terms_ref = refs
    width = mat_ref.shape[0]
    rows = width // planes
    size = rows_ref.shape[0] // planes
    own_out_ref[...] = rows_ref[pl.ds(pl.multiple_of(plane_ref[0] * size, size), size), :]
    for step, out_ref in enumerate(outs):
        start = (plane_ref[0] ^ (step + 1)) * size
        part = rows_ref[pl.ds(pl.multiple_of(start, size), size), :].astype(bf16)
        for i in range(GROUP):
            at = 3 * rows + i * size
            out_ref[at : at + size] = part[:, i * 128 : (i + 1) * 128]
    sums = sum_ref[0:1]
    lane = lax.broadcasted_iota(jnp.int32, (rows, 128), 1)
    grads = jnp.concatenate([rows_of_tree(ref) for ref in (g0, g1)])
    u0.ready()
    u1.ready()
    for step in (*range(1, planes), 0):
        plane = plane_ref[0] ^ step
        cols = pl.ds(pl.multiple_of(plane * rows, 128), rows)
        at = pl.ds(pl.multiple_of(plane * rows, rows), rows)
        units = jnp.concatenate([ref.at[:, :, cols][...].reshape(-1, rows) for ref in (u0, u1)])
        product = mm(units, grads, TN)
        mat = mat_ref[at, :].astype(f32)
        total = product * vec_ref[at, 0:1] + vec_ref[at, 1:2] * sums
        if step == 0:
            own_ref[...] = total
        else:
            for i in range(3):
                outs[step - 1][i * rows : (i + 1) * rows] = total[:, i * 128 : (i + 1) * 128].astype(bf16)
        gain = jnp.sum(product * mat, axis=1, keepdims=True)
        bias = jnp.sum(mat * sums, axis=1, keepdims=True)
        terms_ref[at, :] = jnp.where(lane == 0, gain, jnp.where(lane == 1, bias, 0.0))


def rows_of_tree(ref):
    blocks, rows, width = ref.shape
    return ref[...].reshape(blocks * rows, width)


def qkv_grads(sums, grads, units, mat, vec_columns, out_rows, plane, planes):
    width = mat.shape[0]
    wrow = out_rows.shape[0] // planes
    return call(
        partial(qkv_grads_kernel, planes),
        [
            shape((width // planes, 384), f32), shape((wrow, width), f32),
            *[shape((3 * width // planes + GROUP * wrow, 128)) for _ in range(planes - 1)],
            shape((width, 128), f32),
        ],
        [sums, *[far(x) for x in grads], *[far(x) for x in units], mat, vec_columns, out_rows],
        "qkv_grads",
        group=10,
        scalars=(plane[None],),
        flops=2 * TREE * 2 * width * 384,
        limit=28,
    )


def pack_kernel(planes, q_ref, k_ref, v_ref, up_ref, *refs):
    vectors, (sent_ref, vec_ref) = refs[:9], refs[9:]
    frow = up_ref.shape[1] // (planes * GROUP)
    for place in range(GROUP):
        for at, ref in enumerate((q_ref, k_ref, v_ref)):
            sent_ref[place, :, at * 128 : (at + 1) * 128] = ref[:, place * 128 : (place + 1) * 128]
        for plane in range(planes):
            start = (plane * GROUP + place) * frow
            sent_ref[place, :, 384 + plane * frow : 384 + (plane + 1) * frow] = up_ref[
                :, start : start + frow
            ]
    vec_ref[...] = jnp.zeros(vec_ref.shape, f32)
    for at, ref in enumerate(vectors):
        vec_ref[at : at + 1, 0 : ref.shape[1]] = ref[...].astype(f32)


def split_kernel(got_ref, out_ref, down_ref, first_ref, second_ref):
    places, size, lanes = got_ref.shape
    rows, wrow, frow = places * size, out_ref.shape[0], down_ref.shape[0]
    for place in range(places):
        for i in range(3):
            at = i * rows + place * size
            first_ref[at : at + size] = got_ref[place, :, i * 128 : (i + 1) * 128]
        second_ref[place * size : (place + 1) * size] = got_ref[place, :, 384:]
    for i in range(GROUP):
        at = 3 * rows + i * wrow
        first_ref[at : at + wrow] = out_ref[:, i * 128 : (i + 1) * 128]
    half = down_ref.shape[1] // 2
    second_ref[rows : rows + frow] = down_ref[:, 0:half]
    second_ref[rows + frow :] = down_ref[:, half:]


def home_kernel(planes, *refs):
    own_ref, own_out_ref, *refs = refs
    mats, ffns, (home_ref, down_ref, out_ref) = refs[: planes - 1], refs[planes - 1 : 2 * planes - 1], refs[2 * planes - 1 :]
    rows, frow, wrow = own_ref.shape[0], down_ref.shape[0], out_ref.shape[0]

    def total(parts, at):
        result = parts[0][at].astype(f32)
        for part in parts[1:]:
            result = result + part[at].astype(f32)
        return result

    size = rows // GROUP
    up = total(ffns, slice(0, rows))
    for place in range(GROUP):
        home_ref[place, :, 384:] = up[place * size : (place + 1) * size]
    for i in range(3):
        mat = own_ref[:, i * 128 : (i + 1) * 128] + total(mats, slice(i * rows, (i + 1) * rows))
        for place in range(GROUP):
            home_ref[place, :, i * 128 : (i + 1) * 128] = mat[place * size : (place + 1) * size]
    for i in range(GROUP):
        at = 3 * rows + i * wrow
        out_ref[:, i * 128 : (i + 1) * 128] = own_out_ref[:, i * 128 : (i + 1) * 128] + total(
            mats, slice(at, at + wrow)
        )
    half = down_ref.shape[1] // 2
    down_ref[:, 0:half] = total(ffns, slice(rows, rows + frow))
    down_ref[:, half:] = total(ffns, slice(rows + frow, rows + 2 * frow))


def unpack_kernel(planes, home_ref, q_ref, k_ref, v_ref, up_ref):
    frow = up_ref.shape[1] // (planes * GROUP)
    for place in range(GROUP):
        for at, ref in enumerate((q_ref, k_ref, v_ref)):
            ref[:, place * 128 : (place + 1) * 128] = home_ref[place, :, at * 128 : (at + 1) * 128]
        for plane in range(planes):
            start = (plane * GROUP + place) * frow
            up_ref[:, start : start + frow] = home_ref[
                place, :, 384 + plane * frow : 384 + (plane + 1) * frow
            ]


def on_device(
    tokens, grad_out, w_query, w_key, w_value, b_query, b_value, w_attn_out, b_attn_out,
    w_up, b_up, w_down, b_down, ln1_gain, ln1_bias, ln2_gain, ln2_bias, leaf_parent,
):
    micro_count, row_count, width = tokens.shape
    count = lax.axis_size("dp")
    planes = count // GROUP
    index = lax.axis_index("dp")
    place = index % GROUP
    plane = index // GROUP
    wrow = w_query.shape[0]
    frow = w_down.shape[0]
    head_width = width // GROUP
    unit_width = planes * frow
    lanes = 3 * head_width + unit_width
    both = range(micro_count)
    chain.last = None

    small = (b_query, b_value, b_attn_out, b_down, ln1_gain, ln1_bias, ln2_gain, ln2_bias, b_up)
    if few(planes):
        sent, vector = call(
            partial(pack_kernel, planes),
            [shape((GROUP, wrow, lanes)), shape((16, 128), f32)],
            [far(x) for x in (w_query, w_key, w_value, w_up, *[piece.reshape(1, -1) for piece in small])],
            "pack",
        )
    else:
        qkv_w = [w.reshape(wrow, GROUP, head_width) for w in (w_query, w_key, w_value)]
        up_w = w_up.reshape(wrow, planes, GROUP, frow).transpose(0, 2, 1, 3)
        sent = jnp.concatenate((*qkv_w, up_w.reshape(wrow, GROUP, unit_width)), axis=2)
        sent = sent.transpose(1, 0, 2)
        vector = jnp.stack(
            [jnp.pad(piece.astype(f32), (0, 128 - piece.shape[0])) for piece in small]
        )
        vector = jnp.pad(vector, ((0, 7), (0, 0)))
    got = plane_exchange(sent)
    blocks_x = plane_gather(after(tokens, sent))
    vectors = lax.all_to_all(
        jnp.broadcast_to(vector, (count, 16, 128)), "dp", 0, 0, tiled=True
    )
    piece = width // count
    long = vectors[:, :8, :piece].transpose(1, 0, 2).reshape(8, width)
    vec_up = lax.dynamic_index_in_dim(
        vectors.reshape(planes, GROUP, 16, 128)[:, :, 8, :frow], place, 1, keepdims=False
    ).reshape(1, -1)
    vec_qkv = lax.dynamic_slice_in_dim(long[:2], place * head_width, head_width, axis=1)
    vec_qkv = jnp.concatenate(
        (vec_qkv[0], jnp.zeros((head_width,), f32), vec_qkv[1])
    )[None]
    vec_one = long[4:6]
    vec_two = jnp.stack((long[2], long[6], long[7], long[3]))

    if few(planes):
        first, second = call(
            split_kernel,
            [
                shape((3 * GROUP * wrow + GROUP * wrow, 128)),
                shape((GROUP * wrow + 2 * frow, unit_width)),
            ],
            [after(got, *blocks_x[2], *blocks_x[4], vectors), far(w_attn_out), far(w_down)],
            "split",
        )
        first_parts = column_parts(first)
        second_parts = column_parts(after(second, *first_parts), 2)
        mat_qkv, out_rows = call(
            partial(order_kernel, wrow),
            [shape((width, 3 * head_width)), shape((planes, wrow, width))],
            [after(first_parts[0], *blocks_x[6]), *first_parts[1:]],
            "rows",
            scalars=(plane[None],),
        )
        mat_out = Part(
            lax.all_gather(out_rows, "dp", axis=0, axis_index_groups=plane_groups()), turned=True
        )
    else:
        got = got.reshape(GROUP * wrow, lanes)
        mat_qkv = column_parts(got[:, : 3 * head_width])[0]
        down_rows = jnp.concatenate((w_down[:, :unit_width], w_down[:, unit_width:]))
        ffn_rows = column_parts(jnp.concatenate((got[:, 3 * head_width :], down_rows)))[0]
        ffn_rows = ffn_rows.reshape(planes, -1, unit_width)
        mat_up = ffn_rows[:, : GROUP * wrow].reshape(width, unit_width)
        halves = ffn_rows[:, GROUP * wrow :].reshape(planes, 2, frow, unit_width)
        mat_down = halves.transpose(0, 2, 1, 3).reshape(unit_width, width)
        mat_out = far(lax.all_gather(w_attn_out, "dp", axis=0, tiled=True))
    blocks_dy = plane_gather(after(grad_out, *blocks_x[6]), 2, 3)

    parents = lax.dynamic_index_in_dim(leaf_parent, plane, 1, keepdims=False)
    heads = 2 * place + jnp.arange(2, dtype=jnp.int32)
    slopes = jnp.exp2(-8.0 * (heads.astype(f32) + 1.0) / HEADS)
    forward = []
    for m in both:
        blocks = [far(tokens, m)] + [of_micro(blocks_x[mask], m) for mask in range(1, GROUP)]
        forward.append(
            attention_forward(2 + m, m, place, parents[m], slopes, blocks, vec_one, mat_qkv, vec_qkv)
        )
    middle, normed2, context = project(
        [plane_exchange(forward[m][0]) for m in both], far(tokens), vec_two, mat_out
    )
    blocks_a2 = plane_gather(normed2, 4, 5)

    if few(planes):
        mat_up, mat_down = call(
            ffn_order_kernel,
            [shape((width, unit_width)), shape((unit_width, width))],
            second_parts,
            "units",
            scalars=(plane[None],),
        )

    more = 2 * wrow if few(planes) else 0
    split = ((0, 1), (2, 4, 3, 5), (6, 7))
    order = [mask for masks in split for mask in masks]
    grad_vec_up = 0.0
    y_parts, a_parts, act, du = [None] * GROUP, [None] * GROUP, [], []
    for group, masks in zip((4, 5, None), split):
        y, da, act_part, du_part, up_sum = feed_forward(
            blocks_a2, blocks_dy, masks, mat_up, mat_down, vec_up, more, group
        )
        act.append(act_part)
        du.append(du_part)
        grad_vec_up = grad_vec_up + up_sum
        for i, mask in enumerate(masks):
            y_parts[mask] = y[i]
            a_parts[mask] = da[i]
    scatter2 = Scatter(a_parts)
    scatter2.first(6)
    if few(planes):
        grad_ffn = ffn_grads(blocks_a2, blocks_dy, order, act, du, plane, planes)
    else:
        flat = lambda blocks: jnp.concatenate(
            [x.reshape(-1, width) for mask in order for x in blocks[mask]]
        )
        units_flat = lambda parts: jnp.concatenate([x.reshape(-1, unit_width) for x in parts])
        grad_up = mm(flat(blocks_a2), units_flat(du), TN)
        grad_down = mm(units_flat(act), flat(blocks_dy), TN)
    scatter2.second()
    dh, dattn, dctx, small_own = second_back(
        scatter2.addends(), far(grad_out), middle, vec_two, mat_out
    )
    plane_dctx = plane_exchange(dctx)
    if few(planes):
        ffn_terms = column_send(grad_ffn[1:], 8)
        y_parts = out_grads(place, context, dattn, y_parts, planes)
    scatter_y = Scatter([far(part) for part in y_parts])
    scatter_y.first(8)

    scatter1, grad_qkv, sum_qkv = [], [], 0.0
    for m in both:
        parts, dqkv, dsum = attention_backward(
            8 + m, m, place, parents[m], slopes, forward[m][2], forward[m][0], plane_dctx, forward[m][1], mat_qkv
        )
        scatter1.append(ScatterOne(parts, m))
        scatter1[m].first(9 + m)
        grad_qkv.append(dqkv)
        sum_qkv = sum_qkv + dsum
        if m == 0:
            scatter_y.second(9)
    scatter1[0].second(10)
    output, *out_total = call(
        partial(output_kernel, more),
        [far(shape(tokens.shape))] + ([shape((2 * more, width), f32)] if more else []),
        [*scatter_y.addends(), middle, vec_two],
        "output",
        group=10,
        limit=16,
    )
    sums8 = jnp.broadcast_to(sum_qkv, (8, 384))
    if few(planes):
        own_mat, own_out, *others, norm_terms = qkv_grads(
            sums8, grad_qkv, [forward[m][3] for m in both], mat_qkv, vec_one.T, out_total[0], plane, planes
        )
        others = column_send(others)
    else:
        units = jnp.concatenate([forward[m][3].reshape(-1, width) for m in both])
        product = mm(units, jnp.concatenate([g.reshape(-1, 384) for g in grad_qkv]), TN)
        grad_mat = product * vec_one[0][:, None] + vec_one[1][:, None] * sum_qkv[None]
        mat32 = mat_qkv.astype(f32)
        norm_terms = jnp.stack(
            (jnp.sum(product * mat32, axis=1), jnp.sum(mat32 * sum_qkv[None], axis=1)), axis=1
        )
    scatter1[1].second()
    sides1 = chain.last

    if few(planes):
        home, sum_down, sum_out = call(
            partial(home_kernel, planes),
            [
                shape((GROUP, wrow, lanes), f32), far(shape((frow, width), f32)),
                far(shape((wrow, width), f32)),
            ],
            [own_mat, own_out, *others, grad_ffn[0], *ffn_terms],
            "home",
        )
        home = plane_exchange(home)
    else:

        def scattered(value):
            value = value.reshape(planes, -1, value.shape[1])
            return lax.psum_scatter(
                value, "dp", scatter_dimension=0, axis_index_groups=column_groups()
            )

        home = plane_exchange(
            jnp.concatenate((scattered(grad_mat), scattered(grad_up)), axis=1).reshape(
                GROUP, wrow, lanes
            )
        )
        sum_down = scattered(grad_down)
        grad_out_mat = mm(context.reshape(-1, width), dattn.reshape(-1, width), TN)
        sum_out = lax.psum_scatter(grad_out_mat, "dp", scatter_dimension=0, tiled=True)
    (grad_input,) = call(
        first_back_kernel,
        [far(shape(tokens.shape))],
        [*scatter1[0].addends(), *scatter1[1].addends(), far(tokens), far(dh), vec_one],
        "norm1_back",
    )
    if few(planes):
        *home_qkv, home_up = call(
            partial(unpack_kernel, planes),
            [far(shape((wrow, width), f32))] * 3 + [far(shape((wrow, unit_width * GROUP), f32))],
            [home],
            "unpack",
        )
    else:
        home_up = home[:, :, 3 * head_width :].reshape(GROUP, wrow, planes, frow)
        home_up = home_up.transpose(1, 2, 0, 3).reshape(wrow, -1)
        home_qkv = [
            home[:, :, at * head_width : (at + 1) * head_width].transpose(1, 0, 2).reshape(wrow, width)
            for at in range(3)
        ]

    sum_qkv, small_own, norm_terms, grad_vec_up, _ = lax.optimization_barrier(
        (sum_qkv, small_own, norm_terms, grad_vec_up, sides1)
    )

    def placed(piece):
        return lax.dynamic_update_slice_in_dim(
            jnp.zeros((width,), f32), piece, place * head_width, 0
        )

    up_terms = lax.dynamic_update_slice_in_dim(
        jnp.zeros((planes, GROUP, frow), f32),
        grad_vec_up.reshape(planes, 1, frow),
        place,
        1,
    )
    terms = jnp.concatenate(
        [
            piece.reshape(count, -1)
            for piece in (
                placed(sum_qkv[:head_width]),
                placed(sum_qkv[2 * head_width :]),
                small_own[0],
                small_own[1],
                norm_terms[:, 0],
                norm_terms[:, 1],
                small_own[2],
                small_own[3],
                up_terms,
            )
        ],
        axis=1,
    )
    sums = jnp.sum(lax.all_to_all(terms, "dp", 0, 0, tiled=True), axis=0)
    bounds = [0]
    for piece in small:
        bounds.append(bounds[-1] + piece.shape[0])
    pieces = [sums[bounds[at] : bounds[at + 1]] for at in range(len(small))]
    return (
        output, grad_input,
        home_qkv[0], home_qkv[1], home_qkv[2], sum_out, home_up, sum_down,
        pieces[0], pieces[1], pieces[2], pieces[8], pieces[3],
        pieces[4], pieces[5], pieces[6], pieces[7],
    )


def solution(mesh):
    row = P("dp", None)
    vec = P("dp")
    tok = P(None, "dp", None)
    return jax.shard_map(
        on_device,
        mesh=mesh,
        in_specs=(
            tok, tok, row, row, row, vec, vec, row, vec, row, vec, row, vec, vec, vec, vec, vec, P(),
        ),
        out_specs=(
            tok, tok, row, row, row, row, row, row, vec, vec, vec, vec, vec, vec, vec, vec, vec,
        ),
        check_vma=False,
    )
```

```python
from functools import partial

import jax
import jax.numpy as jnp
from jax import lax
from jax.experimental import pallas as pl
from jax.experimental.pallas import tpu as pltpu
from jax.sharding import PartitionSpec as P

HEADS = 16
BLK = 32
TRUNK_BLK = 16
SEG_BLK = 2
BRANCHES = 4
LEAVES = 8
TREE_BLK = 40

GROUP = 8
TREE = TREE_BLK * BLK
TRUNK = TRUNK_BLK * BLK
SEG = SEG_BLK * BLK
ROWS = 256
HALF = 128
HID = 64
NEG = -1e30

eps = 1e-05
bf16 = jnp.bfloat16
f32 = jnp.float32


def swap(value, mask):
    count = lax.axis_size("dp")
    pairs = [(source, source ^ mask) for source in range(count)]
    return lax.ppermute(value, "dp", pairs)


def after(value, *others):
    return lax.optimization_barrier((value, *others))[0]


class Chain:
    def __init__(self):
        self.last = None

    def hold(self, value):
        if self.last is None:
            return value
        return after(value, self.last)


chain = Chain()


class Part:
    def __init__(self, array, micro=None, turned=False, far=False, rows=None):
        self.array, self.micro, self.turned, self.far, self.rows = array, micro, turned, far or turned, rows

    def of(self, array):
        return Part(array, self.micro, self.turned, self.far, self.rows)


def far(array, micro=None, rows=None):
    return Part(array, micro, far=True, rows=rows)


def is_far(x):
    return isinstance(x, Part) and x.far


def array_of(x):
    return x.array if isinstance(x, Part) else x


def dims_of(x):
    if not isinstance(x, Part):
        return x.shape
    if x.rows is not None:
        return *x.array.shape[:-2], x.rows[1], x.array.shape[-1]
    if x.micro is None and not x.turned:
        return x.array.shape
    if x.turned:
        places, planes, rows, width = x.array.shape
        return places * planes * rows, width
    return x.array.shape[1:]


def pieces_of(dims, dtype):
    unit = 16 if dtype == bf16 else 8
    size = jnp.dtype(dtype).itemsize
    total = size
    for dim in dims:
        total *= dim
    if len(dims) == 3 and dims[0] >= 4:
        return [(at,) for at in range(dims[0])]
    lead = range(dims[0]) if len(dims) == 3 else [None]
    rows = dims[-2]
    best = 1
    for number in range(1, 9):
        if rows % (number * unit) == 0 and total // len(lead) // number >= 1 << 16:
            best = number
    step = rows // best
    cuts = [slice(at * step, (at + 1) * step) for at in range(best)]
    return [(cut,) if first is None else (first, cut) for first in lead for cut in cuts]


def window(ref, rows):
    return ref.at[pl.ds(*rows)] if len(ref.shape) == 2 else ref.at[:, pl.ds(*rows)]


class Loaded:
    def __init__(self, x, source, target, semaphore):
        self.target, self.copy = target, None
        if x.turned:
            places, planes, rows, _ = x.array.shape
            for place in range(places):
                for plane in range(planes):
                    at = (plane * places + place) * rows
                    pltpu.make_async_copy(
                        source.at[place, plane], target.at[at : at + rows], semaphore
                    ).start()
            self.copy = pltpu.make_async_copy(target, target, semaphore)
            return
        if x.micro is not None:
            source = source.at[x.micro]
        if x.rows is not None:
            source = window(source, x.rows)
        for piece in pieces_of(target.shape, target.dtype):
            pltpu.make_async_copy(source.at[piece], target.at[piece], semaphore).start()
        self.copy = pltpu.make_async_copy(source, target, semaphore)

    def ready(self):
        if self.copy is not None:
            self.copy.wait()
            self.copy = None
        return self.target

    shape = property(lambda self: self.target.shape)
    dtype = property(lambda self: self.target.dtype)
    at = property(lambda self: self.ready().at)

    def __getitem__(self, index):
        return self.ready()[index]


class Stored:
    def __init__(self, x, target, source, semaphore):
        self.source, self.semaphore = source, semaphore
        self.target = target if x.micro is None else target.at[x.micro]
        if x.rows is not None:
            self.target = window(target, x.rows)
        self.gone = False

    shape = property(lambda self: self.source.shape)
    dtype = property(lambda self: self.source.dtype)
    at = property(lambda self: self.source.at)

    def __getitem__(self, index):
        return self.source[index]

    def __setitem__(self, index, value):
        self.source[index] = value

    def leave(self):
        if not self.gone:
            for piece in pieces_of(self.source.shape, self.source.dtype):
                pltpu.make_async_copy(
                    self.source.at[piece], self.target.at[piece], self.semaphore
                ).start()
            self.gone = True

    def done(self):
        pltpu.make_async_copy(self.source, self.target, self.semaphore).wait()


def leave(*refs):
    for ref in refs:
        if isinstance(ref, Stored):
            ref.leave()


def near(x, ref):
    return ref.at[x.micro] if isinstance(x, Part) and x.micro is not None else ref


def call(kernel, outs, args, name, scalars=(), scratch=(), flops=0, ordered=True, into=(), limit=12, light=False):
    args = list(args)
    if ordered:
        first = args[0]
        held = chain.hold(array_of(first))
        args[0] = first.of(held) if isinstance(first, Part) else held
    outside = lambda x: pltpu.with_memory_space_constraint(x, pltpu.HBM)
    arrays = [outside(x.array) if is_far(x) else array_of(x) for x in args]
    arrays += [outside(x) for x in into]
    shapes = [array_of(x) for x in outs]
    colored = [
        pltpu.HBM(x.shape, x.dtype) if is_far(out) else x for out, x in zip(outs, shapes)
    ]
    nscalar, nargs, nouts = len(scalars), len(args), len(outs)
    far_in = [i for i, x in enumerate(args) if is_far(x)]
    far_out = [i for i, x in enumerate(outs) if is_far(x)]

    def body(*refs):
        numbers = refs[:nscalar]
        inputs = list(refs[nscalar : nscalar + nargs])
        outputs = list(refs[nscalar + len(arrays) : nscalar + len(arrays) + nouts])
        rest = list(refs[nscalar + len(arrays) + nouts :])
        sems = rest[-2:]
        loaded = [
            Loaded(args[i], inputs[i], rest[k], sems[0].at[k]) for k, i in enumerate(far_in)
        ]
        stored = [
            Stored(outs[i], outputs[i], rest[len(far_in) + k], sems[1].at[k])
            for k, i in enumerate(far_out)
        ]
        inputs = [near(x, ref) for x, ref in zip(args, inputs)]
        outputs = [near(x, ref) for x, ref in zip(outs, outputs)]
        for k, i in enumerate(far_in):
            inputs[i] = loaded[k]
        for k, i in enumerate(far_out):
            outputs[i] = stored[k]
        kernel(*numbers, *inputs, *outputs, *rest[len(far_in) + len(far_out) : -2])
        for x in loaded:
            x.ready()
        leave(*stored)
        for x in stored:
            x.done()

    bytes_accessed = 0 if light else sum(x.size * x.dtype.itemsize for x in arrays + shapes)
    place = lambda x: pl.BlockSpec(memory_space=pltpu.HBM if is_far(x) else pltpu.VMEM)
    kernel_call = pl.pallas_call(
        body,
        out_shape=tuple(colored),
        in_specs=[pl.BlockSpec(memory_space=pltpu.SMEM)] * nscalar
        + [place(x) for x in args]
        + [pl.BlockSpec(memory_space=pltpu.HBM) for _ in into],
        out_specs=tuple(place(x) for x in outs),
        scratch_shapes=[pltpu.VMEM(dims_of(args[i]), array_of(args[i]).dtype) for i in far_in]
        + [pltpu.VMEM(dims_of(outs[i]), array_of(outs[i]).dtype) for i in far_out]
        + list(scratch)
        + [
            pltpu.SemaphoreType.DMA((max(1, len(far_in)),)),
            pltpu.SemaphoreType.DMA((max(1, len(far_out)),)),
        ],
        input_output_aliases={nscalar + nargs + i: i for i in range(len(into))},
        compiler_params=pltpu.CompilerParams(vmem_limit_bytes=limit << 20),
        cost_estimate=pl.CostEstimate(
            flops=flops, transcendentals=0, bytes_accessed=bytes_accessed
        ),
        name=name,
    )
    result = kernel_call(*scalars, *arrays)
    if ordered:
        chain.last = result[-1]
    return result


def shape(dims, dtype=bf16):
    return jax.ShapeDtypeStruct(dims, dtype)


def kinds(dims, masks=range(GROUP)):
    return [shape(dims, bf16 if mask else f32) for mask in masks]


class Gather:
    def __init__(self, own):
        self.own = own
        self.side = {2: swap(own, 2), 4: swap(own, 4)}

    def corners(self, *gate):
        cut = lax.optimization_barrier(([self.side[2][0], self.side[4][1]], gate))[0]
        self.corner = [swap(cut[0], 4), swap(cut[1], 2)]

    def blocks(self, gate, corner_gate=()):
        even = lax.optimization_barrier(({0: self.own, **self.side}, gate))[0]
        self.corner = lax.optimization_barrier((self.corner, gate, corner_gate))[0]
        blocks = [even[mask] if mask in even else swap(even[mask ^ 1], 1) for mask in range(6)]
        return [[block] for block in blocks] + [self.corner, [swap(c, 1) for c in self.corner]]


def of_micro(blocks, m):
    return far(blocks[0], m) if len(blocks) == 1 else far(blocks[m])


def add_kernel(plan, *refs):
    ninputs = len(refs) - len(plan)
    for out_ref, rows in zip(refs[ninputs:], plan):
        for lead, addends in enumerate(rows):
            total = None
            for number, at in addends:
                value = (refs[number][...] if at is None else refs[number][at]).astype(f32)
                total = value if total is None else total + value
            if len(rows) == 1:
                out_ref[...] = total.astype(out_ref.dtype)
            else:
                out_ref[lead] = total.astype(out_ref.dtype)


def swap_back(parts, others=()):
    masks = (6, 2, 4, 0)
    odd = lax.optimization_barrier(([parts[mask ^ 1] for mask in masks], others))[0]
    return dict(zip(masks, lax.optimization_barrier([swap(part, 1) for part in odd])))


class Scatter:
    def __init__(self, parts):
        self.parts = parts
        self.back = swap_back(parts)

    def first(self):
        dims = self.parts[6].shape[1:]
        plan = [[[(0, m), (1, m)]] for m in range(2)]
        total = call(
            partial(add_kernel, plan), [shape(dims)] * 2, [far(self.back[6]), far(self.parts[6])], "corner", light=True
        )
        self.corner = swap(total[0], 4), swap(total[1], 2)

    def second(self):
        dims = self.parts[2].shape
        plan = [
            [[(0, 0), (1, 0), (4, None)], [(0, 1), (1, 1)]],
            [[(2, 0), (3, 0)], [(2, 1), (3, 1), (5, None)]],
        ]
        total = call(
            partial(add_kernel, plan), [shape(dims)] * 2,
            [far(x) for x in (self.back[2], self.parts[2], self.back[4], self.parts[4], *self.corner)],
            "sides", light=True,
        )
        self.sides = swap(total[0], 2), swap(total[1], 4)

    def addends(self):
        return [far(x) for x in (self.parts[0], self.back[0], *self.sides)]


class ScatterOne:
    def __init__(self, parts, micro, others):
        self.parts = parts
        self.via = 4 if micro == 0 else 2
        self.back = swap_back(parts, others)

    def first(self, *gate):
        total = call(
            partial(add_kernel, [[[(0, None), (1, None)]]]), [shape(self.parts[6].shape)],
            [far(after(self.back[6], *gate)), far(self.parts[6])], "corner", light=True,
        )[0]
        self.corner = swap(total, self.via)

    def second(self):
        via = self.via
        plan = [[[(0, None), (1, None)]], [[(2, None), (3, None), (4, None)]]]
        total = call(
            partial(add_kernel, plan), [shape(self.parts[6].shape)] * 2,
            [
                far(x)
                for x in (self.back[via], self.parts[via], self.back[6 ^ via], self.parts[6 ^ via], self.corner)
            ],
            "sides", light=True,
        )
        self.sides = swap(total[0], via), swap(total[1], 6 ^ via)

    def addends(self):
        return [far(x) for x in (self.parts[0], self.back[0], *self.sides)]


def plane_groups():
    count = lax.axis_size("dp")
    return [list(range(first, first + GROUP)) for first in range(0, count, GROUP)]


def column_groups():
    count = lax.axis_size("dp")
    return [list(range(place, count, GROUP)) for place in range(GROUP)]


def plane_exchange(value):
    return lax.all_to_all(value, "dp", 0, 0, tiled=True, axis_index_groups=plane_groups())


def column_parts(value):
    planes = lax.axis_size("dp") // GROUP
    if planes > 4:
        return [
            lax.all_gather(value, "dp", axis=0, axis_index_groups=column_groups(), tiled=True)
        ]
    return [value] + [swap(value, GROUP * step) for step in range(1, planes)]


def column_send(parts):
    return [swap(part, GROUP * (step + 1)) for step, part in enumerate(parts)]


def few(planes):
    return planes <= 4


def order_kernel(wrow, plane_ref, place_ref, *refs):
    *parts, dy_ref, mat_ref, long_ref, qkv_ref, one_ref, two_ref, up_ref, long_s = refs
    for m in range(2):
        long_ref[m, 0 : dy_ref.shape[1]] = dy_ref[m]
    planes = len(parts)
    rows = mat_ref.shape[0] // planes
    piece = mat_ref.shape[0] // (planes * GROUP)
    source = lax.broadcasted_iota(jnp.int32, (128, 128), 0)
    target = lax.broadcasted_iota(jnp.int32, (128, 128), 1)
    each = 128 // piece
    for step, part in enumerate(parts):
        plane = plane_ref[0] ^ step
        at = pl.ds(pl.multiple_of(plane * rows, rows), rows)
        for i in range(3):
            mat_ref[at, i * 128 : (i + 1) * 128] = part[i * rows : (i + 1) * rows]
        start = 3 * rows
        for i in range(GROUP):
            value = part[start + i * wrow : start + (i + 1) * wrow]
            at = pl.ds(pl.multiple_of(dy_ref.shape[1] + (plane % (planes // 2)) * wrow, wrow), wrow)
            long_ref.at[plane // (planes // 2), at, i * 128 : (i + 1) * 128][...] = value
        start += GROUP * wrow
        for first in range(0, GROUP, each):
            total = jnp.zeros((16, 128), f32)
            for i in range(each):
                chosen = (source < piece) & (source + i * piece == target)
                tile = part[start + (first + i) * 16 : start + (first + i + 1) * 16]
                total = total + mm(tile, jnp.where(chosen, 1.0, 0.0).astype(bf16), NN)
            lane = (plane * GROUP + first) * piece
            long_s[:, pl.ds(pl.multiple_of(lane, 128), 128)] = total
        frow = up_ref.shape[1] // planes
        tile = part[pl.ds(pl.multiple_of(start + place_ref[0] * 16, 16), 16), :].astype(f32)
        up_ref[0:1, pl.ds(pl.multiple_of(plane * frow, 128), frow)] = tile[8:9]
    at = pl.ds(pl.multiple_of(place_ref[0] * 128, 128), 128)
    heads = long_s[0:8, at]
    qkv_ref[...] = jnp.concatenate((heads[0:1], jnp.zeros((1, 128), f32), heads[1:2]), axis=1)
    one_ref[...] = long_s[4:6]
    two_ref[0:1] = long_s[2:3]
    two_ref[1:3] = long_s[6:8]
    two_ref[3:4] = long_s[3:4]


def ffn_order_kernel(rows_ref, up_ref, down_ref):
    planes = rows_ref.shape[0]
    rows, units = up_ref.shape[0] // planes, up_ref.shape[1]
    frow = units // planes
    for plane in range(planes):
        up_ref[plane * rows : (plane + 1) * rows] = rows_ref[plane, 0:rows]
        down_ref[plane * frow : (plane + 1) * frow, 0:units] = rows_ref[plane, rows : rows + frow]
        down_ref[plane * frow : (plane + 1) * frow, units:] = rows_ref[plane, rows + frow :]


def out_order_kernel(planes, place_ref, *refs):
    *blocks, out_ref = refs
    size = out_ref.shape[0] // (planes * GROUP)
    half = planes // 2
    at = 0
    for mask in range(GROUP):
        for plane in range(planes):
            m, step = divmod(plane, half)
            ref = blocks[mask] if mask < 6 else blocks[6 + (mask - 6) * 2 + m]
            value = ref[m, step * size : (step + 1) * size] if mask < 6 else ref[step * size : (step + 1) * size]
            start = plane * GROUP * size + (place_ref[0] ^ mask) * size
            out_ref[pl.ds(pl.multiple_of(start, size), size), :] = value


def mm(left, right, contract):
    return lax.dot_general(left, right, (contract, ((), ())), preferred_element_type=f32)


NN = ((1,), (0,))
NT = ((1,), (1,))
TN = ((0,), (0,))


def split3(values):
    high = values.astype(bf16)
    rest = values - high.astype(f32)
    middle = rest.astype(bf16)
    low = (rest - middle.astype(f32)).astype(bf16)
    return high, middle, low


def norm_parts(values):
    center = values - jnp.mean(values, axis=-1, keepdims=True)
    spread = jnp.mean(center * center, axis=-1, keepdims=True)
    scale = lax.rsqrt(spread + eps)
    return center * scale, scale


def norm_back(grad, unit, scale, gain):
    scaled = grad * gain
    return scale * (
        scaled
        - jnp.mean(scaled, axis=-1, keepdims=True)
        - unit * jnp.mean(scaled * unit, axis=-1, keepdims=True)
    )


def fill_heads(query, key, slope_ref, query_s, key_s, place, start, rows):
    lane = lax.broadcasted_iota(jnp.int32, (rows, 128), 1)
    one = jnp.ones((rows, 128), bf16)
    zero = jnp.zeros((rows, 128), bf16)
    at = pl.ds(start, rows)
    for head in range(2):
        mine = (lane < HID) if head == 0 else (lane >= HID)
        base = HID if head == 0 else 0
        high, middle, low = split3(place * slope_ref[head])
        extra = jnp.where(
            lane == base,
            high,
            jnp.where(lane == base + 1, middle, jnp.where(lane == base + 2, low, zero)),
        )
        ones = jnp.where((lane >= base) & (lane < base + 3), one, zero)
        query_s[head, at, :] = jnp.where(mine, query, ones)
        key_s[head, at, :] = jnp.where(mine, key, extra)


def positions(start, rows):
    row = lax.broadcasted_iota(jnp.int32, (rows, 128), 0) + start
    after_trunk = row - TRUNK
    inside = after_trunk & (SEG - 1)
    return jnp.where(
        row < TRUNK, row, TRUNK + inside + jnp.where(after_trunk < BRANCHES * SEG, 0, SEG)
    ).astype(f32)


def tile_masks():
    row = lax.broadcasted_iota(jnp.int32, (HALF, HALF), 1)
    col = lax.broadcasted_iota(jnp.int32, (HALF, HALF), 0)
    same = (row // SEG) == (col // SEG)
    segment = jnp.where(same & (col <= row), 0.0, NEG)
    parent = jnp.where(same, 0.0, NEG)
    trow = lax.broadcasted_iota(jnp.int32, (ROWS, ROWS), 1)
    tcol = lax.broadcasted_iota(jnp.int32, (ROWS, ROWS), 0)
    causal = jnp.where(tcol <= trow, 0.0, NEG)
    return segment, parent, causal


def parent_rows(parent_ref, leaf):
    start = TRUNK + (parent_ref[leaf] - 1) * SEG
    return pl.ds(pl.multiple_of(start, SEG), SEG)


def tile_pieces(tile):
    if tile < TRUNK // ROWS:
        return (tile + 1) * ROWS, True, [], []
    start = tile * ROWS
    own = [start, start + HALF]
    first_leaf = TRUNK + BRANCHES * SEG
    leaves = []
    if start >= first_leaf:
        leaf = (start - first_leaf) // SEG
        leaves = [(leaf, leaf + 1), (leaf + 2, leaf + 3)]
    return TRUNK, False, own, leaves


def tile_scores(tile, key_ref, query, masks, side):
    segment, parent, causal = masks
    trunk, last, own, leaves = tile_pieces(tile)
    scores = mm(key_ref[0:trunk, :], query, NT)
    pieces = []
    if last:
        if trunk > ROWS:
            pieces.append(scores[: trunk - ROWS])
        pieces.append(scores[trunk - ROWS :] + causal)
    else:
        pieces.append(scores)
    if own:
        pieces.append(
            jnp.concatenate(
                [
                    mm(key_ref[at : at + HALF, :], query[i * HALF : (i + 1) * HALF], NT) + segment
                    for i, at in enumerate(own)
                ],
                axis=1,
            )
        )
    if leaves:
        pieces.append(
            jnp.concatenate(
                [
                    mm(rows, query[i * HALF : (i + 1) * HALF], NT) + parent
                    for i, rows in enumerate(side)
                ],
                axis=1,
            )
        )
    return pieces


def forward_kernel(
    micro, place_ref, parent_ref, slope_ref,
    a0, a1, a2, a3, a4, a5, a6, a7, vec_ref, mat_ref, bias_ref,
    ctx_ref, log_ref, packed_ref, unit_ref,
    query_s, key_s, value_s, ctx_s,
):
    rows = TREE // GROUP
    for mask, block_ref in zip((1, 2, 3, 4, 5, 0, 6, 7), (a1, a2, a3, a4, a5, a0, a6, a7)):
        start = pl.multiple_of((place_ref[0] ^ mask) * rows, rows)
        unit, _ = norm_parts(block_ref[...].astype(f32))
        unit_ref[mask] = unit.astype(bf16)
        normed = (unit * vec_ref[0:1] + vec_ref[1:2]).astype(bf16)
        part = (mm(normed, mat_ref[...], NN) + bias_ref[...]).astype(bf16)
        packed_ref.source[pl.ds(start, rows), :] = part
        value_s[pl.ds(start, rows), :] = part[:, 256:384]
        fill_heads(
            part[:, 0:128] * jnp.asarray(0.125, bf16), part[:, 128:256],
            slope_ref, query_s, key_s, positions(start, rows), start, rows,
        )
    leave(unit_ref, packed_ref)
    masks = tile_masks()
    for tile in range(TREE // ROWS):
        trunk, last, own, leaves = tile_pieces(tile)
        at = slice(tile * ROWS, (tile + 1) * ROWS)
        contexts = []
        side_values = [
            jnp.concatenate([value_s[parent_rows(parent_ref, leaf), :] for leaf in pair])
            for pair in leaves
        ]
        for head in range(2):
            query = query_s[head, at, :]
            side = [
                jnp.concatenate([key_s[head, parent_rows(parent_ref, leaf), :] for leaf in pair])
                for pair in leaves
            ]
            pieces = tile_scores(tile, key_s.at[head], query, masks, side)
            peak = pieces[0].max(axis=0, keepdims=True)
            for piece in pieces[1:]:
                peak = jnp.maximum(peak, piece.max(axis=0, keepdims=True))
            probs = [jnp.exp(piece - peak) for piece in pieces]
            total = probs[0].sum(axis=0, keepdims=True)
            for piece in probs[1:]:
                total = total + piece.sum(axis=0, keepdims=True)
            probs = [piece.astype(bf16) for piece in probs]
            ntrunk = len(probs) - bool(own) - bool(leaves)
            start = 0
            context = None
            for piece in probs[:ntrunk]:
                term = mm(value_s[start : start + piece.shape[0], :], piece, TN)
                context = term if context is None else context + term
                start += piece.shape[0]
            if own:
                context = context + jnp.concatenate(
                    [
                        mm(value_s[first : first + HALF, :], probs[ntrunk][:, i * HALF : (i + 1) * HALF], TN)
                        for i, first in enumerate(own)
                    ],
                    axis=1,
                )
            if leaves:
                context = context + jnp.concatenate(
                    [
                        mm(side_values[i], probs[ntrunk + 1][:, i * HALF : (i + 1) * HALF], TN)
                        for i in range(2)
                    ],
                    axis=1,
                )
            half = slice(head * HID, (head + 1) * HID)
            contexts.append(context[half] / total)
            log_ref[head : head + 1, at] = peak + jnp.log(total)
        ctx_s[at, :] = jnp.concatenate(contexts, axis=0).T.astype(bf16)
    for block in range(GROUP):
        ctx_ref[block] = ctx_s[block * rows : (block + 1) * rows, :]


def attention_forward(micro, place, parents, slopes, blocks, vec, mat, bias):
    rows, width = TREE // GROUP, mat.shape[0]
    return call(
        partial(forward_kernel, micro),
        [
            shape((GROUP, rows, 128)), shape((8, TREE), f32),
            far(shape((TREE, 384))), far(shape((GROUP, rows, width))),
        ],
        [*blocks, vec, mat, bias],
        "tree_attention",
        scalars=(place[None], parents, slopes),
        scratch=[
            pltpu.VMEM((2, TREE, 128), bf16),
            pltpu.VMEM((2, TREE, 128), bf16),
            pltpu.VMEM((TREE, 128), bf16),
            pltpu.VMEM((TREE, 128), bf16),
        ],
        flops=4_000_000_000,
        limit=14,
    )


def backward_kernel(
    micro, place_ref, parent_ref, slope_ref,
    grad_ref, packed_ref, ctx_ref, log_ref, mat_ref,
    o0, o1, o2, o3, o4, o5, o6, o7, dqkv_ref, sum_ref,
    query_s, key_s, value_s, grad_s, dkey_s, dvalue_s, dquery_s,
):
    rows = TREE // GROUP
    lane = lax.broadcasted_iota(jnp.int32, (rows, 128), 1)
    zero = jnp.zeros((rows, 128), bf16)
    for block in range(GROUP):
        start = block * rows
        at = pl.ds(start, rows)
        part = packed_ref[at, :]
        fill_heads(
            part[:, 0:128] * jnp.asarray(0.125, bf16), part[:, 128:256],
            slope_ref, query_s, key_s, positions(start, rows), start, rows,
        )
        value = part[:, 256:384]
        grad = grad_ref[block, micro]
        for head in range(2):
            mine = (lane < HID) if head == 0 else (lane >= HID)
            value_s[head, at, :] = jnp.where(mine, value, zero)
            grad_s[head, at, :] = jnp.where(mine, grad, zero)
        dquery_s[at, :] = grad.astype(f32) * ctx_ref[block].astype(f32)
    dkey_s[...] = jnp.zeros_like(dkey_s)
    dvalue_s[...] = jnp.zeros_like(dvalue_s)
    masks = tile_masks()
    for tile in range(TREE // ROWS):
        trunk, last, own, leaves = tile_pieces(tile)
        at = slice(tile * ROWS, (tile + 1) * ROWS)
        deltas = dquery_s[at, :].T
        dqueries = []
        for head in range(2):
            half = slice(head * HID, (head + 1) * HID)
            query = query_s[head, at, :]
            grad = grad_s[head, at, :]
            keys = key_s.at[head]
            values = value_s.at[head]
            side = [
                jnp.concatenate([key_s[head, parent_rows(parent_ref, leaf), :] for leaf in pair])
                for pair in leaves
            ]
            pieces = tile_scores(tile, keys, query, masks, side)
            level = log_ref[head : head + 1, at]
            delta = deltas[half].sum(axis=0, keepdims=True)
            ntrunk = len(pieces) - bool(own) - bool(leaves)
            dquery = None
            start = 0
            for piece in pieces[:ntrunk]:
                size = piece.shape[0]
                span = slice(start, start + size)
                probs = jnp.exp(piece - level)
                dprobs = mm(values[span, :], grad, NT)
                dscores = (probs * (dprobs - delta)).astype(bf16)
                dvalue_s[span, :] += mm(probs.astype(bf16), grad, NN)
                dkey_s[head, span, :] += mm(dscores, query, NN)
                term = mm(keys[span, :], dscores, TN)
                dquery = term if dquery is None else dquery + term
                start += size
            extra = []
            for i, first in enumerate(own):
                cols = slice(i * HALF, (i + 1) * HALF)
                span = slice(first, first + HALF)
                probs = jnp.exp(pieces[ntrunk][:, cols] - level[:, cols])
                dprobs = mm(values[span, :], grad[cols], NT)
                dscores = (probs * (dprobs - delta[:, cols])).astype(bf16)
                dvalue_s[span, :] += mm(probs.astype(bf16), grad[cols], NN)
                dkey_s[head, span, :] += mm(dscores, query[cols], NN)
                extra.append(mm(keys[span, :], dscores, TN))
            if own:
                dquery = dquery + jnp.concatenate(extra, axis=1)
            extra = []
            for i, pair in enumerate(leaves):
                cols = slice(i * HALF, (i + 1) * HALF)
                side_value = jnp.concatenate(
                    [value_s[head, parent_rows(parent_ref, leaf), :] for leaf in pair]
                )
                probs = jnp.exp(pieces[ntrunk + 1][:, cols] - level[:, cols])
                dprobs = mm(side_value, grad[cols], NT)
                dscores = (probs * (dprobs - delta[:, cols])).astype(bf16)
                dval = mm(probs.astype(bf16), grad[cols], NN)
                dkey = mm(dscores, query[cols], NN)
                for j, leaf in enumerate(pair):
                    span = parent_rows(parent_ref, leaf)
                    dvalue_s[span, :] += dval[j * SEG : (j + 1) * SEG]
                    dkey_s[head, span, :] += dkey[j * SEG : (j + 1) * SEG]
                extra.append(mm(side[i], dscores, TN))
            if leaves:
                dquery = dquery + jnp.concatenate(extra, axis=1)
            dqueries.append(dquery[half] * 0.125)
        dquery_s[at, :] = jnp.concatenate(dqueries, axis=0).T
    sums = jnp.zeros((1, 384), f32)
    for mask, out_ref in reversed(list(enumerate((o0, o1, o2, o3, o4, o5, o6, o7)))):
        at = pl.ds(pl.multiple_of((place_ref[0] ^ mask) * rows, rows), rows)
        dkey = jnp.where(lane < HID, dkey_s[0, at, :], dkey_s[1, at, :])
        dqkv = jnp.concatenate(
            (dquery_s[at, :].astype(bf16), dkey.astype(bf16), dvalue_s[at, :].astype(bf16)), axis=1
        )
        dqkv_ref[mask] = dqkv
        sums = sums + jnp.sum(dqkv.astype(f32), axis=0, keepdims=True)
        out_ref[...] = mm(dqkv, mat_ref[...], NT).astype(out_ref.dtype)
        leave(out_ref)
    sum_ref[...] = jnp.broadcast_to(sums, (8, 384))


def attention_backward(micro, place, parents, slopes, packed, ctx, grad, logs, mat):
    rows = TREE // GROUP
    width = mat.shape[0]
    result = call(
        partial(backward_kernel, micro),
        [far(x) for x in kinds((rows, width))] + [far(shape((GROUP, rows, 384))), shape((8, 384), f32)],
        [grad, far(packed), ctx, logs, mat],
        "tree_attention_back",
        scalars=(place[None], parents, slopes),
        scratch=[
            pltpu.VMEM((2, TREE, 128), bf16),
            pltpu.VMEM((2, TREE, 128), bf16),
            pltpu.VMEM((2, TREE, 128), bf16),
            pltpu.VMEM((2, TREE, 128), bf16),
            pltpu.VMEM((2, TREE, 128), f32),
            pltpu.VMEM((TREE, 128), f32),
            pltpu.VMEM((TREE, 128), f32),
        ],
        flops=10_000_000_000,
        limit=16,
    )
    return result[:GROUP], result[GROUP], result[GROUP + 1][0]


def project_kernel(p0, p1, x_ref, vec_ref, mat_ref, middle_ref, normed_ref, ctx_ref, total_s):
    micros, rows, width = middle_ref.shape
    for m, part in enumerate((p0, p1)):
        for block in range(GROUP):
            total_s[m * rows : (m + 1) * rows, block * 128 : (block + 1) * 128] = part[block]
    attn = mm(total_s[...], mat_ref[...], NN) + vec_ref[0:1]
    for m in range(micros):
        ctx_ref[m] = total_s[m * rows : (m + 1) * rows]
        middle = x_ref[m].astype(f32) + attn[m * rows : (m + 1) * rows]
        middle_ref[m] = middle
        unit, _ = norm_parts(middle)
        normed_ref[m] = (unit * vec_ref[1:2] + vec_ref[2:3]).astype(bf16)


def project(parts, x, vec, mat):
    dims = dims_of(x)
    return call(
        project_kernel,
        [shape(dims, f32), shape(dims), far(shape(dims))],
        [*parts, x, vec, mat],
        "project",
        scratch=[pltpu.VMEM((dims[0] * dims[1], dims[2]), bf16)],
        flops=2 * dims[0] * dims[1] * dims[2] * dims[2],
        limit=16,
    )


def rows_of(refs):
    if len(refs) == 1:
        micros, rows, width = refs[0].shape
        return refs[0][...].reshape(micros * rows, width)
    return jnp.concatenate([ref[...] for ref in refs])


def ffn_kernel(counts, *refs):
    refs = list(refs)

    def take(number):
        taken = refs[:number]
        del refs[:number]
        return taken

    a_refs = [take(number) for number in counts]
    dy_refs = [take(number) for number in counts]
    up_ref, down_ref, bias_ref = take(3)
    y_refs, da_refs = take(len(counts)), take(len(counts))
    act_ref, du_ref, sum_ref = refs
    sums = jnp.zeros((1, up_ref.shape[1]), f32)
    for i in range(len(counts)):
        upper = mm(rows_of(a_refs[i]), up_ref[...], NN) + bias_ref[...]
        square = upper * upper
        bent = jnp.tanh(upper * (0.7978845608028654 + (0.7978845608028654 * 0.044715) * square))
        half = 0.5 * (1.0 + bent)
        active = (upper * half).astype(bf16)
        slope = half + (0.5 * upper) * (1.0 - bent * bent) * (
            0.7978845608028654 + (3.0 * 0.7978845608028654 * 0.044715) * square
        )
        act_ref[i] = active
        du = mm(rows_of(dy_refs[i]), down_ref[...], NT) * slope
        sums = sums + jnp.sum(du, axis=0, keepdims=True)
        du = du.astype(bf16)
        du_ref[i] = du
        kind = da_refs[i].dtype
        da_refs[i][...] = mm(du, up_ref[...], NT).astype(kind).reshape(da_refs[i].shape)
        y_refs[i][...] = mm(active, down_ref[...], NN).astype(bf16).reshape(y_refs[i].shape)
        leave(y_refs[i], da_refs[i])
    sum_ref[...] = jnp.broadcast_to(sums, sum_ref.shape)


def feed_forward(a, dy, masks, up, down, bias, more):
    counts = tuple(len(a[mask]) for mask in masks)
    micros, (rows, width), units = 2, array_of(a[masks[0]][0]).shape[-2:], up.shape[1]
    dims = (micros, rows, width)
    long = (micros, rows + more, width)
    number = len(masks)
    result = call(
        partial(ffn_kernel, counts),
        [far(shape(long), rows=(0, rows)) for _ in masks]
        + [far(x) for x in kinds(dims, masks)]
        + [far(shape((number, micros * rows, units))) for _ in range(2)]
        + [shape((8, units), f32)],
        [far(x) for mask in masks for x in a[mask]]
        + [far(x, rows=(0, rows)) for mask in masks for x in dy[mask]]
        + [up, down, bias],
        "feed_forward",
        flops=8 * number * micros * rows * width * units,
        limit=18,
    )
    return result[:number], result[number : 2 * number], result[-3], result[-2], result[-1][0]


def flat_rows(groups):
    return jnp.concatenate([rows_of(group) for group in groups])


def take_groups(refs, counts):
    groups, at = [], 0
    for number in counts:
        groups.append(refs[at : at + number])
        at += number
    return groups, refs[at:]


def up_grads_kernel(counts, planes, *refs):
    groups, refs = take_groups(refs, counts)
    *du_refs, out_ref = refs
    units = du_refs[0].shape[-1]
    rows = groups[0][0].shape[-1] // planes
    du = jnp.concatenate([ref[...].reshape(-1, units) for ref in du_refs])
    for plane in range(planes):
        at = slice(plane * rows, (plane + 1) * rows)
        parts = [ref[..., at].reshape(-1, rows) for group in groups for ref in group]
        out_ref[plane] = mm(jnp.concatenate(parts), du, TN)


def down_grads_kernel(counts, planes, *refs):
    groups, refs = take_groups(refs, counts)
    *act_refs, out_ref = refs
    units = act_refs[0].shape[-1]
    frow = units // planes
    dy = flat_rows(groups)
    for plane in range(planes):
        at = slice(plane * frow, (plane + 1) * frow)
        act = jnp.concatenate([ref[:, :, at].reshape(-1, frow) for ref in act_refs])
        down = mm(act, dy, TN)
        out_ref[plane, 0:frow] = down[:, :units]
        out_ref[plane, frow:] = down[:, units:]


def ffn_grads(a, dy, masks, act, du, planes):
    counts = tuple(len(a[mask]) for mask in masks)
    width, units = array_of(a[masks[0]][0]).shape[-1], du[0].shape[-1]
    rows, more = width // planes, 2 * (units // planes)
    total = shape((planes, rows + more, units), f32)
    flops = 4 * TREE * width * units
    (up,) = call(
        partial(up_grads_kernel, counts, planes),
        [far(total, rows=(0, rows))],
        [far(x) for mask in masks for x in a[mask]] + [far(x) for x in du],
        "up_grads",
        flops=flops,
        limit=20,
    )
    yield
    (both,) = call(
        partial(down_grads_kernel, counts, planes),
        [far(total, rows=(rows, more))],
        [far(x, rows=(0, TREE // GROUP)) for mask in masks for x in dy[mask]] + [far(x) for x in act],
        "down_grads",
        flops=flops,
        limit=24,
        into=(up,),
    )
    yield both


def second_back_kernel(
    own_ref, back_ref, first_ref, second_ref, dy_ref, middle_ref, vec_ref, mat_ref,
    dh_ref, dattn_ref, dctx_ref, sum_ref,
):
    micros, rows, width = middle_ref.shape
    sums = []
    for m in range(micros):
        grad = (
            own_ref[m].astype(f32)
            + back_ref[m].astype(f32)
            + first_ref[m].astype(f32)
            + second_ref[m].astype(f32)
        )
        unit, scale = norm_parts(middle_ref[m])
        dy = dy_ref[m].astype(f32)
        dh = dy + norm_back(grad, unit, scale, vec_ref[1:2])
        dh_ref[m] = dh
        dattn = dh.astype(bf16)
        dattn_ref[m] = dattn
        sums.append(
            [
                jnp.sum(value, axis=0, keepdims=True)
                for value in (dattn.astype(f32), dy, grad * unit, grad)
            ]
        )
    leave(dh_ref)
    dattn = dattn_ref[...].reshape(micros * rows, width)
    dctx = mm(dattn, mat_ref[...], NT).astype(bf16)
    for m in range(micros):
        for block in range(GROUP):
            dctx_ref[block, m] = dctx[m * rows : (m + 1) * rows, block * 128 : (block + 1) * 128]
    sum_ref[...] = jnp.concatenate(
        [first + second for first, second in zip(*sums)] + [jnp.zeros((4, width), f32)]
    )


def second_back(addends, dy, middle, vec, mat):
    dims = middle.shape
    return call(
        second_back_kernel,
        [
            far(shape(dims, f32)), shape(dims), shape((GROUP, dims[0], dims[1], 128)),
            shape((8, dims[2]), f32),
        ],
        [*addends, dy, middle, vec, mat],
        "norm2_back",
        flops=2 * middle.size * dims[2],
        limit=16,
    )


def first_back_kernel(*refs):
    groups, (x_ref, dh_ref, vec_ref, out_ref) = (refs[0:4], refs[4:8]), refs[8:]
    for m, group in enumerate(groups):
        grad = group[0][...].astype(f32)
        for ref in group[1:]:
            grad = grad + ref[...].astype(f32)
        unit, scale = norm_parts(x_ref[m].astype(f32))
        out_ref[m] = (dh_ref[m] + norm_back(grad, unit, scale, vec_ref[0:1])).astype(bf16)


def output_kernel(more, planes, plane_ref, own_ref, back_ref, first_ref, second_ref, middle_ref, vec_ref, out_ref, *rest):
    micros, rows, width = middle_ref.shape
    for m in range(micros):
        part = slice(0, rows)
        total = own_ref[m, part].astype(f32) + back_ref[m, part].astype(f32)
        total = total + first_ref[m, part].astype(f32) + second_ref[m, part].astype(f32)
        out_ref[m] = (middle_ref[m] + (total + vec_ref[3:4])).astype(bf16)
    leave(out_ref)
    if more:
        part = slice(rows, rows + more)
        for m in range(micros):
            total = own_ref[m, part].astype(f32) + back_ref[m, part].astype(f32)
            total = total + first_ref[m, part].astype(f32) + second_ref[m, part].astype(f32)
            rest[planes][m * more : (m + 1) * more] = total
        size = micros * more // planes
        for step in range(planes):
            at = pl.ds(pl.multiple_of((plane_ref[0] ^ step) * size, size), size)
            rest[step][...] = rest[planes][at, :].astype(rest[step].dtype)


def out_grads_kernel(planes, place_ref, dattn_ref, ctx_ref, *refs):
    outs, total_s = refs[:GROUP], refs[GROUP]
    total_s[...] = mm(rows_of([ctx_ref]), rows_of([dattn_ref]), TN)
    micros, more, _ = outs[0].shape
    size = micros * more // planes
    for mask in range(GROUP):
        for plane in range(planes):
            start = plane * GROUP * size + (place_ref[0] ^ mask) * size
            m, at = divmod(plane * size, more)
            outs[mask][m, at : at + size, :] = total_s[
                pl.ds(pl.multiple_of(start, size), size), :
            ].astype(bf16)
        leave(outs[mask])


def out_grads(place, ctx, dattn, parts, planes):
    width = dattn.shape[-1]
    rows = dattn.shape[1]
    more = parts[0].shape[1] - rows
    return call(
        partial(out_grads_kernel, planes),
        [far(shape(part.shape), rows=(rows, more)) for part in parts],
        [dattn, far(ctx)],
        "out_grads",
        scalars=(place[None],),
        scratch=[pltpu.VMEM((width, width), f32)],
        limit=16,
        light=True,
        into=parts,
    )


def qkv_grads_kernel(planes, plane_ref, sum_ref, g0, g1, u0, u1, mat_ref, vec_ref, *refs):
    *outs, terms_ref = refs
    rows = mat_ref.shape[0] // planes
    sums = sum_ref[0:1]
    lane = lax.broadcasted_iota(jnp.int32, (rows, 128), 1)
    grads = jnp.concatenate([rows_of_tree(ref) for ref in (g0, g1)])
    u0.ready()
    u1.ready()
    for step in (*range(1, planes), 0):
        plane = plane_ref[0] ^ step
        cols = pl.ds(pl.multiple_of(plane * rows, 128), rows)
        at = pl.ds(pl.multiple_of(plane * rows, rows), rows)
        units = jnp.concatenate([ref.at[:, :, cols][...].reshape(-1, rows) for ref in (u0, u1)])
        product = mm(units, grads, TN)
        mat = mat_ref[at, :].astype(f32)
        total = product * vec_ref[at, 0:1] + vec_ref[at, 1:2] * sums
        outs[step][...] = total.astype(outs[step].dtype)
        gain = jnp.sum(product * mat, axis=1, keepdims=True)
        bias = jnp.sum(mat * sums, axis=1, keepdims=True)
        terms_ref[at, :] = jnp.where(lane == 0, gain, jnp.where(lane == 1, bias, 0.0))


def rows_of_tree(ref):
    blocks, rows, width = ref.shape
    return ref[...].reshape(blocks * rows, width)


def qkv_grads(sums, grads, units, mat, vec_columns, plane, planes):
    width = mat.shape[0]
    return call(
        partial(qkv_grads_kernel, planes),
        [*kinds((width // planes, 384), range(planes)), shape((width, 128), f32)],
        [sums, *[far(x) for x in grads], *[far(x) for x in units], mat, vec_columns],
        "qkv_grads",
        scalars=(plane[None],),
        flops=2 * TREE * 2 * width * 384,
        limit=20,
    )


def pack_kernel(planes, q_ref, k_ref, v_ref, up_ref, *refs):
    *vectors, sent_ref = refs
    frow = up_ref.shape[1] // (planes * GROUP)
    lanes = sent_ref.shape[2] - 128
    row = lax.broadcasted_iota(jnp.int32, (16, 128), 0)
    tile = jnp.zeros((16, 128), f32)
    for at, ref in enumerate(vectors):
        value = ref[...].astype(f32)
        if ref.shape[1] < 128:
            value = jnp.pad(value, ((0, 0), (0, 128 - ref.shape[1])))
        tile = jnp.where(row == at, value, tile)
    for place in range(GROUP):
        for at, ref in enumerate((q_ref, k_ref, v_ref)):
            sent_ref[place, :, at * 128 : (at + 1) * 128] = ref[:, place * 128 : (place + 1) * 128]
        for plane in range(planes):
            start = (plane * GROUP + place) * frow
            sent_ref[place, :, 384 + plane * frow : 384 + (plane + 1) * frow] = up_ref[
                :, start : start + frow
            ]
        sent_ref[place, 0:16, lanes:] = tile.astype(bf16)


def split_kernel(got_ref, out_ref, down_ref, first_ref, second_ref):
    places, size, lanes = got_ref.shape
    rows, wrow, frow = places * size, out_ref.shape[0], down_ref.shape[0]
    for place in range(places):
        for i in range(3):
            at = i * rows + place * size
            first_ref[at : at + size] = got_ref[place, :, i * 128 : (i + 1) * 128]
        second_ref[place * size : (place + 1) * size] = got_ref[place, :, 384 : lanes - 128]
        at = 3 * rows + GROUP * wrow + place * 16
        first_ref[at : at + 16] = got_ref[place, 0:16, lanes - 128 :]
    for i in range(GROUP):
        at = 3 * rows + i * wrow
        first_ref[at : at + wrow] = out_ref[:, i * 128 : (i + 1) * 128]
    half = down_ref.shape[1] // 2
    second_ref[rows : rows + frow] = down_ref[:, 0:half]
    second_ref[rows + frow :] = down_ref[:, half:]


def home_kernel(planes, ffn_ref, *refs):
    mats, (home_ref, down_ref) = refs[:planes], refs[planes:]
    mat = mats[0][...]
    for part in mats[1:]:
        mat = mat + part[...].astype(f32)
    rows, frow = mat.shape[0], down_ref.shape[0]
    size, half = rows // GROUP, down_ref.shape[1] // 2
    for place in range(GROUP):
        at = slice(place * size, (place + 1) * size)
        home_ref[place, :, 0:384] = mat[at]
        home_ref[place, :, 384:] = ffn_ref[at]
    down_ref[:, 0:half] = ffn_ref[rows : rows + frow]
    down_ref[:, half:] = ffn_ref[rows + frow :]


def unpack_kernel(planes, home_ref, q_ref, k_ref, v_ref, up_ref):
    frow = up_ref.shape[1] // (planes * GROUP)
    for place in range(GROUP):
        for at, ref in enumerate((q_ref, k_ref, v_ref)):
            ref[:, place * 128 : (place + 1) * 128] = home_ref[place, :, at * 128 : (at + 1) * 128]
        for plane in range(planes):
            start = (plane * GROUP + place) * frow
            up_ref[:, start : start + frow] = home_ref[
                place, :, 384 + plane * frow : 384 + (plane + 1) * frow
            ]


def on_device(
    tokens, grad_out, w_query, w_key, w_value, b_query, b_value, w_attn_out, b_attn_out,
    w_up, b_up, w_down, b_down, ln1_gain, ln1_bias, ln2_gain, ln2_bias, leaf_parent,
):
    micro_count, row_count, width = tokens.shape
    count = lax.axis_size("dp")
    planes = count // GROUP
    index = lax.axis_index("dp")
    place = index % GROUP
    plane = index // GROUP
    wrow = w_query.shape[0]
    frow = w_down.shape[0]
    head_width = width // GROUP
    unit_width = planes * frow
    lanes = 3 * head_width + unit_width
    both = range(micro_count)
    chain.last = None

    small = (b_query, b_value, b_attn_out, b_down, ln1_gain, ln1_bias, ln2_gain, ln2_bias, b_up)
    if few(planes):
        (sent,) = call(
            partial(pack_kernel, planes),
            [shape((GROUP, wrow, lanes + 128))],
            [far(x) for x in (w_query, w_key, w_value, w_up, *[piece.reshape(1, -1) for piece in small])],
            "pack",
        )
    else:
        qkv_w = [w.reshape(wrow, GROUP, head_width) for w in (w_query, w_key, w_value)]
        up_w = w_up.reshape(wrow, planes, GROUP, frow).transpose(0, 2, 1, 3)
        sent = jnp.concatenate((*qkv_w, up_w.reshape(wrow, GROUP, unit_width)), axis=2)
        sent = sent.transpose(1, 0, 2)
    got = plane_exchange(sent)
    gather_x = Gather(after(tokens, got))

    if few(planes):
        first, second = call(
            split_kernel,
            [
                shape((4 * GROUP * wrow + 16 * GROUP, 128)),
                shape((GROUP * wrow + 2 * frow, unit_width)),
            ],
            [got, far(w_attn_out), far(w_down)],
            "split",
        )
        gather_x.corners(first)
        first_parts = column_parts(first)
        corner_x = gather_x.corner
        blocks_x = gather_x.blocks(first_parts)
        ffn_rows = lax.all_gather(second, "dp", axis=0, axis_index_groups=column_groups())
        mat_qkv, dy_rows, vec_qkv, vec_one, vec_two, vec_up = call(
            partial(order_kernel, wrow),
            [
                shape((width, 3 * head_width)), far(shape((micro_count, row_count + 2 * wrow, width))),
                shape((1, 3 * head_width), f32),
                shape((2, width), f32), shape((4, width), f32), shape((1, unit_width), f32),
            ],
            [after(first_parts[0], *corner_x), *first_parts[1:], far(grad_out)],
            "rows",
            scalars=(plane[None], place[None]),
            scratch=[pltpu.VMEM((16, width), f32)],
        )
    else:
        vector = jnp.stack(
            [jnp.pad(piece.astype(f32), (0, 128 - piece.shape[0])) for piece in small]
        )
        vectors = lax.all_gather(jnp.pad(vector, ((0, 7), (0, 0))), "dp")
        piece = width // count
        long = vectors[:, :8, :piece].transpose(1, 0, 2).reshape(8, width)
        vec_up = lax.dynamic_index_in_dim(
            vectors.reshape(planes, GROUP, 16, 128)[:, :, 8, :frow], place, 1, keepdims=False
        ).reshape(1, -1)
        vec_qkv = lax.dynamic_slice_in_dim(long[:2], place * head_width, head_width, axis=1)
        vec_qkv = jnp.concatenate(
            (vec_qkv[0], jnp.zeros((head_width,), f32), vec_qkv[1])
        )[None]
        vec_one = long[4:6]
        vec_two = jnp.stack((long[2], long[6], long[7], long[3]))
        got = got.reshape(GROUP * wrow, lanes)
        mat_qkv = column_parts(got[:, : 3 * head_width])[0]
        down_rows = jnp.concatenate((w_down[:, :unit_width], w_down[:, unit_width:]))
        ffn_rows = column_parts(jnp.concatenate((got[:, 3 * head_width :], down_rows)))[0]
        ffn_rows = ffn_rows.reshape(planes, -1, unit_width)
        mat_up = ffn_rows[:, : GROUP * wrow].reshape(width, unit_width)
        halves = ffn_rows[:, GROUP * wrow :].reshape(planes, 2, frow, unit_width)
        mat_down = halves.transpose(0, 2, 1, 3).reshape(unit_width, width)
        mat_out = far(lax.all_gather(w_attn_out, "dp", axis=0, tiled=True))
        dy_rows = grad_out
        gather_x.corners()
        blocks_x = gather_x.blocks(())
    gather_dy = Gather(dy_rows)

    parents = lax.dynamic_index_in_dim(leaf_parent, plane, 1, keepdims=False)
    heads = 2 * place + jnp.arange(2, dtype=jnp.int32)
    slopes = jnp.exp2(-8.0 * (heads.astype(f32) + 1.0) / HEADS)
    forward = []
    for m in both:
        blocks = [far(tokens, m)] + [of_micro(blocks_x[mask], m) for mask in range(1, GROUP)]
        forward.append(
            attention_forward(m, place, parents[m], slopes, blocks, vec_one, mat_qkv, vec_qkv)
        )
    plane_ctx = [plane_exchange(forward[m][0]) for m in both]
    gather_dy.corners(chain.last, plane_ctx[0])
    blocks_dy = gather_dy.blocks(plane_ctx[0], plane_ctx[1])
    if few(planes):
        window_of = (row_count, 2 * wrow)
        (mat_out,) = call(
            partial(out_order_kernel, planes),
            [shape((width, width))],
            [far(x, rows=window_of) for mask in range(GROUP) for x in blocks_dy[mask]],
            "attn_out",
            scalars=(place[None],),
        )

    middle, normed2, context = project(
        plane_ctx,
        far(tokens), vec_two, mat_out
    )
    if few(planes):
        mat_up, mat_down = call(
            ffn_order_kernel,
            [shape((width, unit_width)), shape((unit_width, width))],
            [far(ffn_rows)],
            "units",
        )

    more = 2 * wrow if few(planes) else 0
    split = ((0, 1), (2, 4, 3, 5), (6, 7))
    order = [mask for masks in split for mask in masks]
    grad_vec_up = 0.0
    y_parts, a_parts, act, du = [None] * GROUP, [None] * GROUP, [], []
    blocks_a2 = [[normed2], [swap(normed2, 1)]] + [None] * 6
    gather_a2 = Gather(normed2)
    for number, masks in enumerate(split):
        if number == 1:
            gather_a2.side = dict(zip((2, 4), lax.optimization_barrier((*gather_a2.side.values(), chain.last))))
            gather_a2.corners()
            for mask in (2, 4):
                blocks_a2[mask], blocks_a2[mask ^ 1] = [gather_a2.side[mask]], [swap(gather_a2.side[mask], 1)]
        if number == 2:
            corner = lax.optimization_barrier((*gather_a2.corner, chain.last))[:2]
            blocks_a2[6], blocks_a2[7] = list(corner), [swap(c, 1) for c in corner]
        y, da, act_part, du_part, up_sum = feed_forward(
            blocks_a2, blocks_dy, masks, mat_up, mat_down, vec_up, more
        )
        act.append(act_part)
        du.append(du_part)
        grad_vec_up = grad_vec_up + up_sum
        for i, mask in enumerate(masks):
            y_parts[mask] = y[i]
            a_parts[mask] = da[i]
    scatter2 = Scatter(a_parts)
    scatter2.first()
    if few(planes):
        steps = ffn_grads(blocks_a2, blocks_dy, order, act, du, planes)
        next(steps)
    else:
        flat = lambda blocks: jnp.concatenate(
            [x.reshape(-1, width) for mask in order for x in blocks[mask]]
        )
        units_flat = lambda parts: jnp.concatenate([x.reshape(-1, unit_width) for x in parts])
        grad_up = mm(flat(blocks_a2), units_flat(du), TN)
        grad_down = mm(units_flat(act), flat(blocks_dy), TN)
    scatter2.second()
    if few(planes):
        sum_ffn = lax.psum_scatter(
            after(next(steps), *scatter2.sides), "dp", scatter_dimension=0, axis_index_groups=column_groups()
        )
    dh, dattn, dctx, small_own = second_back(
        scatter2.addends(), far(grad_out), middle, vec_two, mat_out
    )
    plane_dctx = plane_exchange(dctx)
    if few(planes):
        y_parts = out_grads(place, context, dattn, y_parts, planes)
    scatter_y = Scatter(y_parts)
    scatter_y.first()

    scatter1, grad_qkv, sum_qkv = [], [], 0.0
    for m in both:
        parts, dqkv, dsum = attention_backward(
            m, place, parents[m], slopes, forward[m][2], forward[m][0], plane_dctx, forward[m][1], mat_qkv
        )
        scatter1.append(ScatterOne(parts, m, (scatter1[0].corner,) if m else scatter_y.corner))
        grad_qkv.append(dqkv)
        sum_qkv = sum_qkv + dsum
        if m == 0:
            scatter1[0].first()
            scatter_y.second()
    sums8 = jnp.broadcast_to(sum_qkv, (8, 384))
    if few(planes):
        own_mat, *others, norm_terms = qkv_grads(
            sums8, grad_qkv, [forward[m][3] for m in both], mat_qkv, vec_one.T, plane, planes
        )
        others = column_send(others)
    else:
        units = jnp.concatenate([forward[m][3].reshape(-1, width) for m in both])
        product = mm(units, jnp.concatenate([g.reshape(-1, 384) for g in grad_qkv]), TN)
        grad_mat = product * vec_one[0][:, None] + vec_one[1][:, None] * sum_qkv[None]
        mat32 = mat_qkv.astype(f32)
        norm_terms = jnp.stack(
            (jnp.sum(product * mat32, axis=1), jnp.sum(mat32 * sum_qkv[None], axis=1)), axis=1
        )
    scatter1[0].second()
    scatter1[1].first(*scatter_y.sides)
    output, *out_parts = call(
        partial(output_kernel, more, planes),
        [far(shape(tokens.shape))] + (kinds((wrow, width), range(planes)) if more else []),
        [*scatter_y.addends(), middle, vec_two],
        "output",
        scalars=(plane[None],),
        scratch=[pltpu.VMEM((2 * more, width), f32)] if more else [],
        limit=16,
    )
    scatter1[1].corner = after(scatter1[1].corner, *scatter1[0].sides)
    scatter1[1].second()
    last = chain.last

    if few(planes):
        home, sum_down = call(
            partial(home_kernel, planes),
            [shape((GROUP, wrow, lanes), f32), far(shape((frow, width), f32))],
            [after(sum_ffn, *scatter1[1].sides), own_mat, *others],
            "home",
        )
        last = home
        home = plane_exchange(home)
        out_sums = column_send(lax.optimization_barrier((out_parts[1:], scatter1[1].sides))[0])
        sum_out = out_parts[0]
        for part in out_sums:
            sum_out = sum_out + part.astype(f32)
    else:

        def scattered(value):
            value = value.reshape(planes, -1, value.shape[1])
            return lax.psum_scatter(
                value, "dp", scatter_dimension=0, axis_index_groups=column_groups()
            )

        home = plane_exchange(
            jnp.concatenate((scattered(grad_mat), scattered(grad_up)), axis=1).reshape(
                GROUP, wrow, lanes
            )
        )
        sum_down = scattered(grad_down)
        grad_out_mat = mm(context.reshape(-1, width), dattn.reshape(-1, width), TN)
        sum_out = lax.psum_scatter(grad_out_mat, "dp", scatter_dimension=0, tiled=True)
    (grad_input,) = call(
        first_back_kernel,
        [far(shape(tokens.shape))],
        [*scatter1[0].addends(), *scatter1[1].addends(), far(tokens), far(dh), vec_one],
        "norm1_back",
    )
    if few(planes):
        *home_qkv, home_up = call(
            partial(unpack_kernel, planes),
            [far(shape((wrow, width), f32))] * 3 + [far(shape((wrow, unit_width * GROUP), f32))],
            [home],
            "unpack",
        )
    else:
        home_up = home[:, :, 3 * head_width :].reshape(GROUP, wrow, planes, frow)
        home_up = home_up.transpose(1, 2, 0, 3).reshape(wrow, -1)
        home_qkv = [
            home[:, :, at * head_width : (at + 1) * head_width].transpose(1, 0, 2).reshape(wrow, width)
            for at in range(3)
        ]

    sum_qkv, small_own, norm_terms, grad_vec_up, _ = lax.optimization_barrier(
        (sum_qkv, small_own, norm_terms, grad_vec_up, last)
    )

    def placed(piece):
        return lax.dynamic_update_slice_in_dim(
            jnp.zeros((width,), f32), piece, place * head_width, 0
        )

    up_terms = lax.dynamic_update_slice_in_dim(
        jnp.zeros((planes, GROUP, frow), f32),
        grad_vec_up.reshape(planes, 1, frow),
        place,
        1,
    )
    terms = jnp.concatenate(
        [
            piece.reshape(count, -1)
            for piece in (
                placed(sum_qkv[:head_width]),
                placed(sum_qkv[2 * head_width :]),
                small_own[0],
                small_own[1],
                norm_terms[:, 0],
                norm_terms[:, 1],
                small_own[2],
                small_own[3],
                up_terms,
            )
        ],
        axis=1,
    )
    sums = jnp.sum(lax.all_to_all(terms, "dp", 0, 0, tiled=True), axis=0)
    bounds = [0]
    for piece in small:
        bounds.append(bounds[-1] + piece.shape[0])
    pieces = [sums[bounds[at] : bounds[at + 1]] for at in range(len(small))]
    return (
        output, grad_input,
        home_qkv[0], home_qkv[1], home_qkv[2], sum_out, home_up, sum_down,
        pieces[0], pieces[1], pieces[2], pieces[8], pieces[3],
        pieces[4], pieces[5], pieces[6], pieces[7],
    )


def solution(mesh):
    row = P("dp", None)
    vec = P("dp")
    tok = P(None, "dp", None)
    return jax.shard_map(
        on_device,
        mesh=mesh,
        in_specs=(
            tok, tok, row, row, row, vec, vec, row, vec, row, vec, row, vec, vec, vec, vec, vec, P(),
        ),
        out_specs=(
            tok, tok, row, row, row, row, row, row, vec, vec, vec, vec, vec, vec, vec, vec, vec,
        ),
        check_vma=False,
    )
```

```python
from functools import partial

import jax
import jax.numpy as jnp
from jax import lax
from jax.experimental import pallas as pl
from jax.experimental.pallas import tpu as pltpu
from jax.sharding import PartitionSpec as P

HEADS = 16
BLK = 32
TRUNK_BLK = 16
SEG_BLK = 2
BRANCHES = 4
LEAVES = 8
TREE_BLK = 40

GROUP = 8
TREE = TREE_BLK * BLK
TRUNK = TRUNK_BLK * BLK
SEG = SEG_BLK * BLK
ROWS = 256
HALF = 128
HID = 64
NEG = -1e30

eps = 1e-05
bf16 = jnp.bfloat16
f32 = jnp.float32


def swap(value, mask):
    count = lax.axis_size("dp")
    pairs = [(source, source ^ mask) for source in range(count)]
    return lax.ppermute(value, "dp", pairs)


def after(value, *others):
    return lax.optimization_barrier((value, *others))[0]


class Chain:
    def __init__(self):
        self.last = None

    def hold(self, value):
        if self.last is None:
            return value
        return after(value, self.last)


chain = Chain()


class Part:
    def __init__(self, array, micro=None, turned=False, far=False, rows=None):
        self.array, self.micro, self.turned, self.far, self.rows = array, micro, turned, far or turned, rows

    def of(self, array):
        return Part(array, self.micro, self.turned, self.far, self.rows)


def far(array, micro=None, rows=None):
    return Part(array, micro, far=True, rows=rows)


def is_far(x):
    return isinstance(x, Part) and x.far


def array_of(x):
    return x.array if isinstance(x, Part) else x


def dims_of(x):
    if not isinstance(x, Part):
        return x.shape
    if x.rows is not None:
        return *x.array.shape[:-2], x.rows[1], x.array.shape[-1]
    if x.micro is None and not x.turned:
        return x.array.shape
    if x.turned:
        places, planes, rows, width = x.array.shape
        return places * planes * rows, width
    return x.array.shape[1:]


def pieces_of(dims, dtype):
    unit = 16 if dtype == bf16 else 8
    size = jnp.dtype(dtype).itemsize
    total = size
    for dim in dims:
        total *= dim
    if len(dims) == 3 and dims[0] >= 4:
        return [(at,) for at in range(dims[0])]
    lead = range(dims[0]) if len(dims) == 3 else [None]
    rows = dims[-2]
    best = 1
    for number in range(1, 9):
        if rows % (number * unit) == 0 and total // len(lead) // number >= 1 << 16:
            best = number
    step = rows // best
    cuts = [slice(at * step, (at + 1) * step) for at in range(best)]
    return [(cut,) if first is None else (first, cut) for first in lead for cut in cuts]


def window(ref, rows):
    return ref.at[pl.ds(*rows)] if len(ref.shape) == 2 else ref.at[:, pl.ds(*rows)]


class Loaded:
    def __init__(self, x, source, target, semaphore):
        self.target, self.copy = target, None
        if x.turned:
            places, planes, rows, _ = x.array.shape
            for place in range(places):
                for plane in range(planes):
                    at = (plane * places + place) * rows
                    pltpu.make_async_copy(
                        source.at[place, plane], target.at[at : at + rows], semaphore
                    ).start()
            self.copy = pltpu.make_async_copy(target, target, semaphore)
            return
        if x.micro is not None:
            source = source.at[x.micro]
        if x.rows is not None:
            source = window(source, x.rows)
        for piece in pieces_of(target.shape, target.dtype):
            pltpu.make_async_copy(source.at[piece], target.at[piece], semaphore).start()
        self.copy = pltpu.make_async_copy(source, target, semaphore)

    def ready(self):
        if self.copy is not None:
            self.copy.wait()
            self.copy = None
        return self.target

    shape = property(lambda self: self.target.shape)
    dtype = property(lambda self: self.target.dtype)
    at = property(lambda self: self.ready().at)

    def __getitem__(self, index):
        return self.ready()[index]


class Stored:
    def __init__(self, x, target, source, semaphore):
        self.source, self.semaphore = source, semaphore
        self.target = target if x.micro is None else target.at[x.micro]
        if x.rows is not None:
            self.target = window(target, x.rows)
        self.gone = False

    shape = property(lambda self: self.source.shape)
    dtype = property(lambda self: self.source.dtype)
    at = property(lambda self: self.source.at)

    def __getitem__(self, index):
        return self.source[index]

    def __setitem__(self, index, value):
        self.source[index] = value

    def leave(self):
        if not self.gone:
            for piece in pieces_of(self.source.shape, self.source.dtype):
                pltpu.make_async_copy(
                    self.source.at[piece], self.target.at[piece], self.semaphore
                ).start()
            self.gone = True

    def done(self):
        pltpu.make_async_copy(self.source, self.target, self.semaphore).wait()


def leave(*refs):
    for ref in refs:
        if isinstance(ref, Stored):
            ref.leave()


def near(x, ref):
    return ref.at[x.micro] if isinstance(x, Part) and x.micro is not None else ref


def call(kernel, outs, args, name, scalars=(), scratch=(), flops=0, ordered=True, into=(), limit=12, light=False):
    args = list(args)
    if ordered:
        first = args[0]
        held = chain.hold(array_of(first))
        args[0] = first.of(held) if isinstance(first, Part) else held
    outside = lambda x: pltpu.with_memory_space_constraint(x, pltpu.HBM)
    arrays = [outside(x.array) if is_far(x) else array_of(x) for x in args]
    arrays += [outside(x) for x in into]
    shapes = [array_of(x) for x in outs]
    colored = [
        pltpu.HBM(x.shape, x.dtype) if is_far(out) else x for out, x in zip(outs, shapes)
    ]
    nscalar, nargs, nouts = len(scalars), len(args), len(outs)
    far_in = [i for i, x in enumerate(args) if is_far(x)]
    far_out = [i for i, x in enumerate(outs) if is_far(x)]

    def body(*refs):
        numbers = refs[:nscalar]
        inputs = list(refs[nscalar : nscalar + nargs])
        outputs = list(refs[nscalar + len(arrays) : nscalar + len(arrays) + nouts])
        rest = list(refs[nscalar + len(arrays) + nouts :])
        sems = rest[-2:]
        loaded = [
            Loaded(args[i], inputs[i], rest[k], sems[0].at[k]) for k, i in enumerate(far_in)
        ]
        stored = [
            Stored(outs[i], outputs[i], rest[len(far_in) + k], sems[1].at[k])
            for k, i in enumerate(far_out)
        ]
        inputs = [near(x, ref) for x, ref in zip(args, inputs)]
        outputs = [near(x, ref) for x, ref in zip(outs, outputs)]
        for k, i in enumerate(far_in):
            inputs[i] = loaded[k]
        for k, i in enumerate(far_out):
            outputs[i] = stored[k]
        kernel(*numbers, *inputs, *outputs, *rest[len(far_in) + len(far_out) : -2])
        for x in loaded:
            x.ready()
        leave(*stored)
        for x in stored:
            x.done()

    bytes_accessed = 0 if light else sum(x.size * x.dtype.itemsize for x in arrays + shapes)
    place = lambda x: pl.BlockSpec(memory_space=pltpu.HBM if is_far(x) else pltpu.VMEM)
    kernel_call = pl.pallas_call(
        body,
        out_shape=tuple(colored),
        in_specs=[pl.BlockSpec(memory_space=pltpu.SMEM)] * nscalar
        + [place(x) for x in args]
        + [pl.BlockSpec(memory_space=pltpu.HBM) for _ in into],
        out_specs=tuple(place(x) for x in outs),
        scratch_shapes=[pltpu.VMEM(dims_of(args[i]), array_of(args[i]).dtype) for i in far_in]
        + [pltpu.VMEM(dims_of(outs[i]), array_of(outs[i]).dtype) for i in far_out]
        + list(scratch)
        + [
            pltpu.SemaphoreType.DMA((max(1, len(far_in)),)),
            pltpu.SemaphoreType.DMA((max(1, len(far_out)),)),
        ],
        input_output_aliases={nscalar + nargs + i: i for i in range(len(into))},
        compiler_params=pltpu.CompilerParams(vmem_limit_bytes=limit << 20),
        cost_estimate=pl.CostEstimate(
            flops=flops, transcendentals=0, bytes_accessed=bytes_accessed
        ),
        name=name,
    )
    result = kernel_call(*scalars, *arrays)
    if ordered:
        chain.last = result[-1]
    return result


def shape(dims, dtype=bf16):
    return jax.ShapeDtypeStruct(dims, dtype)


def kinds(dims, masks=range(GROUP)):
    return [shape(dims, bf16 if mask else f32) for mask in masks]


class Gather:
    def __init__(self, own):
        self.own = own
        self.side = {2: swap(own, 2), 4: swap(own, 4)}

    def corners(self, *gate):
        cut = lax.optimization_barrier(([self.side[2][0], self.side[4][1]], gate))[0]
        self.corner = [swap(cut[0], 4), swap(cut[1], 2)]

    def blocks(self, gate, corner_gate=()):
        even = lax.optimization_barrier(({0: self.own, **self.side}, gate))[0]
        self.corner = lax.optimization_barrier((self.corner, gate, corner_gate))[0]
        blocks = [even[mask] if mask in even else swap(even[mask ^ 1], 1) for mask in range(6)]
        return [[block] for block in blocks] + [self.corner, [swap(c, 1) for c in self.corner]]


def of_micro(blocks, m):
    return far(blocks[0], m) if len(blocks) == 1 else far(blocks[m])


def add_kernel(plan, *refs):
    ninputs = len(refs) - len(plan)
    for out_ref, rows in zip(refs[ninputs:], plan):
        for lead, addends in enumerate(rows):
            total = None
            for number, at in addends:
                value = (refs[number][...] if at is None else refs[number][at]).astype(f32)
                total = value if total is None else total + value
            if len(rows) == 1:
                out_ref[...] = total.astype(out_ref.dtype)
            else:
                out_ref[lead] = total.astype(out_ref.dtype)


def swap_back(parts, others=()):
    masks = (6, 2, 4, 0)
    odd = lax.optimization_barrier(([parts[mask ^ 1] for mask in masks], others))[0]
    return dict(zip(masks, lax.optimization_barrier([swap(part, 1) for part in odd])))


class Scatter:
    def __init__(self, parts):
        self.parts = parts
        self.back = swap_back(parts)

    def first(self):
        dims = self.parts[6].shape[1:]
        plan = [[[(0, m), (1, m)]] for m in range(2)]
        total = call(
            partial(add_kernel, plan), [shape(dims)] * 2, [far(self.back[6]), far(self.parts[6])], "corner", light=True
        )
        self.corner = swap(total[0], 4), swap(total[1], 2)

    def second(self):
        dims = self.parts[2].shape
        plan = [
            [[(0, 0), (1, 0), (4, None)], [(0, 1), (1, 1)]],
            [[(2, 0), (3, 0)], [(2, 1), (3, 1), (5, None)]],
        ]
        total = call(
            partial(add_kernel, plan), [shape(dims)] * 2,
            [far(x) for x in (self.back[2], self.parts[2], self.back[4], self.parts[4], *self.corner)],
            "sides", light=True,
        )
        self.sides = swap(total[0], 2), swap(total[1], 4)

    def addends(self):
        return [far(x) for x in (self.parts[0], self.back[0], *self.sides)]


class ScatterOne:
    def __init__(self, parts, micro, others):
        self.parts = parts
        self.via = 4 if micro == 0 else 2
        self.back = swap_back(parts, others)

    def first(self, *gate):
        total = call(
            partial(add_kernel, [[[(0, None), (1, None)]]]), [shape(self.parts[6].shape)],
            [far(after(self.back[6], *gate)), far(self.parts[6])], "corner", light=True,
        )[0]
        self.corner = swap(total, self.via)

    def second(self):
        via = self.via
        plan = [[[(0, None), (1, None)]], [[(2, None), (3, None), (4, None)]]]
        total = call(
            partial(add_kernel, plan), [shape(self.parts[6].shape)] * 2,
            [
                far(x)
                for x in (self.back[via], self.parts[via], self.back[6 ^ via], self.parts[6 ^ via], self.corner)
            ],
            "sides", light=True,
        )
        self.sides = swap(total[0], via), swap(total[1], 6 ^ via)

    def addends(self):
        return [far(x) for x in (self.parts[0], self.back[0], *self.sides)]


def plane_groups():
    count = lax.axis_size("dp")
    return [list(range(first, first + GROUP)) for first in range(0, count, GROUP)]


def column_groups():
    count = lax.axis_size("dp")
    return [list(range(place, count, GROUP)) for place in range(GROUP)]


def plane_exchange(value):
    return lax.all_to_all(value, "dp", 0, 0, tiled=True, axis_index_groups=plane_groups())


def column_parts(value):
    planes = lax.axis_size("dp") // GROUP
    if planes > 4:
        return [
            lax.all_gather(value, "dp", axis=0, axis_index_groups=column_groups(), tiled=True)
        ]
    return [value] + [swap(value, GROUP * step) for step in range(1, planes)]


def column_send(parts):
    return [swap(part, GROUP * (step + 1)) for step, part in enumerate(parts)]


def few(planes):
    return planes <= 4


def order_kernel(wrow, plane_ref, place_ref, *refs):
    *parts, dy_ref, mat_ref, long_ref, qkv_ref, one_ref, two_ref, up_ref, long_s = refs
    for m in range(2):
        long_ref[m, 0 : dy_ref.shape[1]] = dy_ref[m]
    planes = len(parts)
    rows = mat_ref.shape[0] // planes
    piece = mat_ref.shape[0] // (planes * GROUP)
    source = lax.broadcasted_iota(jnp.int32, (128, 128), 0)
    target = lax.broadcasted_iota(jnp.int32, (128, 128), 1)
    each = 128 // piece
    for step, part in enumerate(parts):
        plane = plane_ref[0] ^ step
        at = pl.ds(pl.multiple_of(plane * rows, rows), rows)
        for i in range(3):
            mat_ref[at, i * 128 : (i + 1) * 128] = part[i * rows : (i + 1) * rows]
        start = 3 * rows
        for i in range(GROUP):
            value = part[start + i * wrow : start + (i + 1) * wrow]
            at = pl.ds(pl.multiple_of(dy_ref.shape[1] + (plane % (planes // 2)) * wrow, wrow), wrow)
            long_ref.at[plane // (planes // 2), at, i * 128 : (i + 1) * 128][...] = value
        start += GROUP * wrow
        for first in range(0, GROUP, each):
            total = jnp.zeros((16, 128), f32)
            for i in range(each):
                chosen = (source < piece) & (source + i * piece == target)
                tile = part[start + (first + i) * 16 : start + (first + i + 1) * 16]
                total = total + mm(tile, jnp.where(chosen, 1.0, 0.0).astype(bf16), NN)
            lane = (plane * GROUP + first) * piece
            long_s[:, pl.ds(pl.multiple_of(lane, 128), 128)] = total
        frow = up_ref.shape[1] // planes
        tile = part[pl.ds(pl.multiple_of(start + place_ref[0] * 16, 16), 16), :].astype(f32)
        up_ref[0:1, pl.ds(pl.multiple_of(plane * frow, 128), frow)] = tile[8:9]
    at = pl.ds(pl.multiple_of(place_ref[0] * 128, 128), 128)
    heads = long_s[0:8, at]
    qkv_ref[...] = jnp.concatenate((heads[0:1], jnp.zeros((1, 128), f32), heads[1:2]), axis=1)
    one_ref[...] = long_s[4:6]
    two_ref[0:1] = long_s[2:3]
    two_ref[1:3] = long_s[6:8]
    two_ref[3:4] = long_s[3:4]


def ffn_order_kernel(rows_ref, up_ref, down_ref):
    planes = rows_ref.shape[0]
    rows, units = up_ref.shape[0] // planes, up_ref.shape[1]
    frow = units // planes
    for plane in range(planes):
        up_ref[plane * rows : (plane + 1) * rows] = rows_ref[plane, 0:rows]
        down_ref[plane * frow : (plane + 1) * frow, 0:units] = rows_ref[plane, rows : rows + frow]
        down_ref[plane * frow : (plane + 1) * frow, units:] = rows_ref[plane, rows + frow :]


def out_order_kernel(planes, place_ref, *refs):
    *blocks, out_ref = refs
    size = out_ref.shape[0] // (planes * GROUP)
    half = planes // 2
    at = 0
    for mask in range(GROUP):
        for plane in range(planes):
            m, step = divmod(plane, half)
            ref = blocks[mask] if mask < 6 else blocks[6 + (mask - 6) * 2 + m]
            value = ref[m, step * size : (step + 1) * size] if mask < 6 else ref[step * size : (step + 1) * size]
            start = plane * GROUP * size + (place_ref[0] ^ mask) * size
            out_ref[pl.ds(pl.multiple_of(start, size), size), :] = value


def mm(left, right, contract):
    return lax.dot_general(left, right, (contract, ((), ())), preferred_element_type=f32)


NN = ((1,), (0,))
NT = ((1,), (1,))
TN = ((0,), (0,))


def split3(values):
    high = values.astype(bf16)
    rest = values - high.astype(f32)
    middle = rest.astype(bf16)
    low = (rest - middle.astype(f32)).astype(bf16)
    return high, middle, low


def norm_parts(values):
    center = values - jnp.mean(values, axis=-1, keepdims=True)
    spread = jnp.mean(center * center, axis=-1, keepdims=True)
    scale = lax.rsqrt(spread + eps)
    return center * scale, scale


def norm_back(grad, unit, scale, gain):
    scaled = grad * gain
    return scale * (
        scaled
        - jnp.mean(scaled, axis=-1, keepdims=True)
        - unit * jnp.mean(scaled * unit, axis=-1, keepdims=True)
    )


def fill_heads(query, key, slope_ref, query_s, key_s, place, start, rows):
    lane = lax.broadcasted_iota(jnp.int32, (rows, 128), 1)
    one = jnp.ones((rows, 128), bf16)
    zero = jnp.zeros((rows, 128), bf16)
    at = pl.ds(start, rows)
    for head in range(2):
        mine = (lane < HID) if head == 0 else (lane >= HID)
        base = HID if head == 0 else 0
        high, middle, low = split3(place * slope_ref[head])
        extra = jnp.where(
            lane == base,
            high,
            jnp.where(lane == base + 1, middle, jnp.where(lane == base + 2, low, zero)),
        )
        ones = jnp.where((lane >= base) & (lane < base + 3), one, zero)
        query_s[head, at, :] = jnp.where(mine, query, ones)
        key_s[head, at, :] = jnp.where(mine, key, extra)


def positions(start, rows):
    row = lax.broadcasted_iota(jnp.int32, (rows, 128), 0) + start
    after_trunk = row - TRUNK
    inside = after_trunk & (SEG - 1)
    return jnp.where(
        row < TRUNK, row, TRUNK + inside + jnp.where(after_trunk < BRANCHES * SEG, 0, SEG)
    ).astype(f32)


def tile_masks():
    row = lax.broadcasted_iota(jnp.int32, (HALF, HALF), 1)
    col = lax.broadcasted_iota(jnp.int32, (HALF, HALF), 0)
    same = (row // SEG) == (col // SEG)
    segment = jnp.where(same & (col <= row), 0.0, NEG)
    parent = jnp.where(same, 0.0, NEG)
    trow = lax.broadcasted_iota(jnp.int32, (ROWS, ROWS), 1)
    tcol = lax.broadcasted_iota(jnp.int32, (ROWS, ROWS), 0)
    causal = jnp.where(tcol <= trow, 0.0, NEG)
    return segment, parent, causal


def parent_rows(parent_ref, leaf):
    start = TRUNK + (parent_ref[leaf] - 1) * SEG
    return pl.ds(pl.multiple_of(start, SEG), SEG)


def tile_pieces(tile):
    if tile < TRUNK // ROWS:
        return (tile + 1) * ROWS, True, [], []
    start = tile * ROWS
    own = [start, start + HALF]
    first_leaf = TRUNK + BRANCHES * SEG
    leaves = []
    if start >= first_leaf:
        leaf = (start - first_leaf) // SEG
        leaves = [(leaf, leaf + 1), (leaf + 2, leaf + 3)]
    return TRUNK, False, own, leaves


def tile_scores(tile, key_ref, query, masks, side):
    segment, parent, causal = masks
    trunk, last, own, leaves = tile_pieces(tile)
    scores = mm(key_ref[0:trunk, :], query, NT)
    pieces = []
    if last:
        if trunk > ROWS:
            pieces.append(scores[: trunk - ROWS])
        pieces.append(scores[trunk - ROWS :] + causal)
    else:
        pieces.append(scores)
    if own:
        pieces.append(
            jnp.concatenate(
                [
                    mm(key_ref[at : at + HALF, :], query[i * HALF : (i + 1) * HALF], NT) + segment
                    for i, at in enumerate(own)
                ],
                axis=1,
            )
        )
    if leaves:
        pieces.append(
            jnp.concatenate(
                [
                    mm(rows, query[i * HALF : (i + 1) * HALF], NT) + parent
                    for i, rows in enumerate(side)
                ],
                axis=1,
            )
        )
    return pieces


def forward_kernel(
    micro, place_ref, parent_ref, slope_ref,
    a0, a1, a2, a3, a4, a5, a6, a7, vec_ref, mat_ref, bias_ref,
    ctx_ref, log_ref, packed_ref, unit_ref,
    query_s, key_s, value_s, ctx_s,
):
    rows = TREE // GROUP
    for mask, block_ref in zip((1, 2, 3, 4, 5, 0, 6, 7), (a1, a2, a3, a4, a5, a0, a6, a7)):
        start = pl.multiple_of((place_ref[0] ^ mask) * rows, rows)
        unit, _ = norm_parts(block_ref[...].astype(f32))
        unit_ref[mask] = unit.astype(bf16)
        normed = (unit * vec_ref[0:1] + vec_ref[1:2]).astype(bf16)
        part = (mm(normed, mat_ref[...], NN) + bias_ref[...]).astype(bf16)
        packed_ref.source[pl.ds(start, rows), :] = part
        value_s[pl.ds(start, rows), :] = part[:, 256:384]
        fill_heads(
            part[:, 0:128] * jnp.asarray(0.125, bf16), part[:, 128:256],
            slope_ref, query_s, key_s, positions(start, rows), start, rows,
        )
    leave(unit_ref, packed_ref)
    masks = tile_masks()
    for tile in range(TREE // ROWS):
        trunk, last, own, leaves = tile_pieces(tile)
        at = slice(tile * ROWS, (tile + 1) * ROWS)
        contexts = []
        side_values = [
            jnp.concatenate([value_s[parent_rows(parent_ref, leaf), :] for leaf in pair])
            for pair in leaves
        ]
        for head in range(2):
            query = query_s[head, at, :]
            side = [
                jnp.concatenate([key_s[head, parent_rows(parent_ref, leaf), :] for leaf in pair])
                for pair in leaves
            ]
            pieces = tile_scores(tile, key_s.at[head], query, masks, side)
            peak = pieces[0].max(axis=0, keepdims=True)
            for piece in pieces[1:]:
                peak = jnp.maximum(peak, piece.max(axis=0, keepdims=True))
            probs = [jnp.exp(piece - peak) for piece in pieces]
            total = probs[0].sum(axis=0, keepdims=True)
            for piece in probs[1:]:
                total = total + piece.sum(axis=0, keepdims=True)
            probs = [piece.astype(bf16) for piece in probs]
            ntrunk = len(probs) - bool(own) - bool(leaves)
            start = 0
            context = None
            for piece in probs[:ntrunk]:
                term = mm(value_s[start : start + piece.shape[0], :], piece, TN)
                context = term if context is None else context + term
                start += piece.shape[0]
            if own:
                context = context + jnp.concatenate(
                    [
                        mm(value_s[first : first + HALF, :], probs[ntrunk][:, i * HALF : (i + 1) * HALF], TN)
                        for i, first in enumerate(own)
                    ],
                    axis=1,
                )
            if leaves:
                context = context + jnp.concatenate(
                    [
                        mm(side_values[i], probs[ntrunk + 1][:, i * HALF : (i + 1) * HALF], TN)
                        for i in range(2)
                    ],
                    axis=1,
                )
            half = slice(head * HID, (head + 1) * HID)
            contexts.append(context[half] / total)
            log_ref[head : head + 1, at] = peak + jnp.log(total)
        ctx_s[at, :] = jnp.concatenate(contexts, axis=0).T.astype(bf16)
    for block in range(GROUP):
        ctx_ref[block] = ctx_s[block * rows : (block + 1) * rows, :]


def attention_forward(micro, place, parents, slopes, blocks, vec, mat, bias):
    rows, width = TREE // GROUP, mat.shape[0]
    return call(
        partial(forward_kernel, micro),
        [
            shape((GROUP, rows, 128)), shape((8, TREE), f32),
            far(shape((TREE, 384))), far(shape((GROUP, rows, width))),
        ],
        [*blocks, vec, mat, bias],
        "tree_attention",
        scalars=(place[None], parents, slopes),
        scratch=[
            pltpu.VMEM((2, TREE, 128), bf16),
            pltpu.VMEM((2, TREE, 128), bf16),
            pltpu.VMEM((TREE, 128), bf16),
            pltpu.VMEM((TREE, 128), bf16),
        ],
        flops=4_000_000_000,
        limit=14,
    )


def backward_kernel(
    micro, place_ref, parent_ref, slope_ref,
    grad_ref, packed_ref, ctx_ref, log_ref, mat_ref,
    o0, o1, o2, o3, o4, o5, o6, o7, dqkv_ref, sum_ref,
    query_s, key_s, value_s, grad_s, dkey_s, dvalue_s, dquery_s,
):
    rows = TREE // GROUP
    lane = lax.broadcasted_iota(jnp.int32, (rows, 128), 1)
    zero = jnp.zeros((rows, 128), bf16)
    for block in range(GROUP):
        start = block * rows
        at = pl.ds(start, rows)
        part = packed_ref[at, :]
        fill_heads(
            part[:, 0:128] * jnp.asarray(0.125, bf16), part[:, 128:256],
            slope_ref, query_s, key_s, positions(start, rows), start, rows,
        )
        value = part[:, 256:384]
        grad = grad_ref[block, micro]
        for head in range(2):
            mine = (lane < HID) if head == 0 else (lane >= HID)
            value_s[head, at, :] = jnp.where(mine, value, zero)
            grad_s[head, at, :] = jnp.where(mine, grad, zero)
        dquery_s[at, :] = grad.astype(f32) * ctx_ref[block].astype(f32)
    dkey_s[...] = jnp.zeros_like(dkey_s)
    dvalue_s[...] = jnp.zeros_like(dvalue_s)
    masks = tile_masks()
    for tile in range(TREE // ROWS):
        trunk, last, own, leaves = tile_pieces(tile)
        at = slice(tile * ROWS, (tile + 1) * ROWS)
        deltas = dquery_s[at, :].T
        dqueries = []
        for head in range(2):
            half = slice(head * HID, (head + 1) * HID)
            query = query_s[head, at, :]
            grad = grad_s[head, at, :]
            keys = key_s.at[head]
            values = value_s.at[head]
            side = [
                jnp.concatenate([key_s[head, parent_rows(parent_ref, leaf), :] for leaf in pair])
                for pair in leaves
            ]
            pieces = tile_scores(tile, keys, query, masks, side)
            level = log_ref[head : head + 1, at]
            delta = deltas[half].sum(axis=0, keepdims=True)
            ntrunk = len(pieces) - bool(own) - bool(leaves)
            dquery = None
            start = 0
            for piece in pieces[:ntrunk]:
                size = piece.shape[0]
                span = slice(start, start + size)
                probs = jnp.exp(piece - level)
                dprobs = mm(values[span, :], grad, NT)
                dscores = (probs * (dprobs - delta)).astype(bf16)
                dvalue_s[span, :] += mm(probs.astype(bf16), grad, NN)
                dkey_s[head, span, :] += mm(dscores, query, NN)
                term = mm(keys[span, :], dscores, TN)
                dquery = term if dquery is None else dquery + term
                start += size
            extra = []
            for i, first in enumerate(own):
                cols = slice(i * HALF, (i + 1) * HALF)
                span = slice(first, first + HALF)
                probs = jnp.exp(pieces[ntrunk][:, cols] - level[:, cols])
                dprobs = mm(values[span, :], grad[cols], NT)
                dscores = (probs * (dprobs - delta[:, cols])).astype(bf16)
                dvalue_s[span, :] += mm(probs.astype(bf16), grad[cols], NN)
                dkey_s[head, span, :] += mm(dscores, query[cols], NN)
                extra.append(mm(keys[span, :], dscores, TN))
            if own:
                dquery = dquery + jnp.concatenate(extra, axis=1)
            extra = []
            for i, pair in enumerate(leaves):
                cols = slice(i * HALF, (i + 1) * HALF)
                side_value = jnp.concatenate(
                    [value_s[head, parent_rows(parent_ref, leaf), :] for leaf in pair]
                )
                probs = jnp.exp(pieces[ntrunk + 1][:, cols] - level[:, cols])
                dprobs = mm(side_value, grad[cols], NT)
                dscores = (probs * (dprobs - delta[:, cols])).astype(bf16)
                dval = mm(probs.astype(bf16), grad[cols], NN)
                dkey = mm(dscores, query[cols], NN)
                for j, leaf in enumerate(pair):
                    span = parent_rows(parent_ref, leaf)
                    dvalue_s[span, :] += dval[j * SEG : (j + 1) * SEG]
                    dkey_s[head, span, :] += dkey[j * SEG : (j + 1) * SEG]
                extra.append(mm(side[i], dscores, TN))
            if leaves:
                dquery = dquery + jnp.concatenate(extra, axis=1)
            dqueries.append(dquery[half] * 0.125)
        dquery_s[at, :] = jnp.concatenate(dqueries, axis=0).T
    sums = jnp.zeros((1, 384), f32)
    for mask, out_ref in reversed(list(enumerate((o0, o1, o2, o3, o4, o5, o6, o7)))):
        at = pl.ds(pl.multiple_of((place_ref[0] ^ mask) * rows, rows), rows)
        dkey = jnp.where(lane < HID, dkey_s[0, at, :], dkey_s[1, at, :])
        dqkv = jnp.concatenate(
            (dquery_s[at, :].astype(bf16), dkey.astype(bf16), dvalue_s[at, :].astype(bf16)), axis=1
        )
        dqkv_ref[mask] = dqkv
        sums = sums + jnp.sum(dqkv.astype(f32), axis=0, keepdims=True)
        out_ref[...] = mm(dqkv, mat_ref[...], NT).astype(out_ref.dtype)
        leave(out_ref)
    sum_ref[...] = jnp.broadcast_to(sums, (8, 384))


def attention_backward(micro, place, parents, slopes, packed, ctx, grad, logs, mat):
    rows = TREE // GROUP
    width = mat.shape[0]
    result = call(
        partial(backward_kernel, micro),
        [far(x) for x in kinds((rows, width))] + [far(shape((GROUP, rows, 384))), shape((8, 384), f32)],
        [grad, far(packed), ctx, logs, mat],
        "tree_attention_back",
        scalars=(place[None], parents, slopes),
        scratch=[
            pltpu.VMEM((2, TREE, 128), bf16),
            pltpu.VMEM((2, TREE, 128), bf16),
            pltpu.VMEM((2, TREE, 128), bf16),
            pltpu.VMEM((2, TREE, 128), bf16),
            pltpu.VMEM((2, TREE, 128), f32),
            pltpu.VMEM((TREE, 128), f32),
            pltpu.VMEM((TREE, 128), f32),
        ],
        flops=10_000_000_000,
        limit=16,
    )
    return result[:GROUP], result[GROUP], result[GROUP + 1][0]


def project_kernel(p0, p1, x_ref, vec_ref, mat_ref, middle_ref, normed_ref, ctx_ref, total_s):
    micros, rows, width = middle_ref.shape
    for m, part in enumerate((p0, p1)):
        for block in range(GROUP):
            total_s[m * rows : (m + 1) * rows, block * 128 : (block + 1) * 128] = part[block]
    attn = mm(total_s[...], mat_ref[...], NN) + vec_ref[0:1]
    for m in range(micros):
        ctx_ref[m] = total_s[m * rows : (m + 1) * rows]
        middle = x_ref[m].astype(f32) + attn[m * rows : (m + 1) * rows]
        middle_ref[m] = middle
        unit, _ = norm_parts(middle)
        normed_ref[m] = (unit * vec_ref[1:2] + vec_ref[2:3]).astype(bf16)


def project(parts, x, vec, mat):
    dims = dims_of(x)
    return call(
        project_kernel,
        [shape(dims, f32), shape(dims), far(shape(dims))],
        [*parts, x, vec, mat],
        "project",
        scratch=[pltpu.VMEM((dims[0] * dims[1], dims[2]), bf16)],
        flops=2 * dims[0] * dims[1] * dims[2] * dims[2],
        limit=16,
    )


def rows_of(refs):
    if len(refs) == 1:
        micros, rows, width = refs[0].shape
        return refs[0][...].reshape(micros * rows, width)
    return jnp.concatenate([ref[...] for ref in refs])


def ffn_kernel(counts, *refs):
    refs = list(refs)

    def take(number):
        taken = refs[:number]
        del refs[:number]
        return taken

    a_refs = [take(number) for number in counts]
    dy_refs = [take(number) for number in counts]
    up_ref, down_ref, bias_ref = take(3)
    y_refs, da_refs = take(len(counts)), take(len(counts))
    act_ref, du_ref, sum_ref = refs
    sums = jnp.zeros((1, up_ref.shape[1]), f32)
    for i in range(len(counts)):
        upper = mm(rows_of(a_refs[i]), up_ref[...], NN) + bias_ref[...]
        square = upper * upper
        bent = jnp.tanh(upper * (0.7978845608028654 + (0.7978845608028654 * 0.044715) * square))
        half = 0.5 * (1.0 + bent)
        active = (upper * half).astype(bf16)
        slope = half + (0.5 * upper) * (1.0 - bent * bent) * (
            0.7978845608028654 + (3.0 * 0.7978845608028654 * 0.044715) * square
        )
        act_ref[i] = active
        du = mm(rows_of(dy_refs[i]), down_ref[...], NT) * slope
        sums = sums + jnp.sum(du, axis=0, keepdims=True)
        du = du.astype(bf16)
        du_ref[i] = du
        kind = da_refs[i].dtype
        da_refs[i][...] = mm(du, up_ref[...], NT).astype(kind).reshape(da_refs[i].shape)
        y_refs[i][...] = mm(active, down_ref[...], NN).astype(bf16).reshape(y_refs[i].shape)
        leave(y_refs[i], da_refs[i])
    sum_ref[...] = jnp.broadcast_to(sums, sum_ref.shape)


def feed_forward(a, dy, masks, up, down, bias, more):
    counts = tuple(len(a[mask]) for mask in masks)
    micros, (rows, width), units = 2, array_of(a[masks[0]][0]).shape[-2:], up.shape[1]
    dims = (micros, rows, width)
    long = (micros, rows + more, width)
    number = len(masks)
    result = call(
        partial(ffn_kernel, counts),
        [far(shape(long), rows=(0, rows)) for _ in masks]
        + [far(x) for x in kinds(dims, masks)]
        + [far(shape((number, micros * rows, units))) for _ in range(2)]
        + [shape((8, units), f32)],
        [far(x) for mask in masks for x in a[mask]]
        + [far(x, rows=(0, rows)) for mask in masks for x in dy[mask]]
        + [up, down, bias],
        "feed_forward",
        flops=8 * number * micros * rows * width * units,
        limit=18,
    )
    return result[:number], result[number : 2 * number], result[-3], result[-2], result[-1][0]


def flat_rows(groups):
    return jnp.concatenate([rows_of(group) for group in groups])


def take_groups(refs, counts):
    groups, at = [], 0
    for number in counts:
        groups.append(refs[at : at + number])
        at += number
    return groups, refs[at:]


def up_grads_kernel(counts, planes, *refs):
    groups, refs = take_groups(refs, counts)
    *du_refs, out_ref = refs
    units = du_refs[0].shape[-1]
    rows = groups[0][0].shape[-1] // planes
    du = jnp.concatenate([ref[...].reshape(-1, units) for ref in du_refs])
    for plane in range(planes):
        at = slice(plane * rows, (plane + 1) * rows)
        parts = [ref[..., at].reshape(-1, rows) for group in groups for ref in group]
        out_ref[plane] = mm(jnp.concatenate(parts), du, TN)


def down_grads_kernel(counts, planes, *refs):
    groups, refs = take_groups(refs, counts)
    *act_refs, out_ref = refs
    units = act_refs[0].shape[-1]
    frow = units // planes
    dy = flat_rows(groups)
    for plane in range(planes):
        at = slice(plane * frow, (plane + 1) * frow)
        act = jnp.concatenate([ref[:, :, at].reshape(-1, frow) for ref in act_refs])
        down = mm(act, dy, TN)
        out_ref[plane, 0:frow] = down[:, :units]
        out_ref[plane, frow:] = down[:, units:]


def ffn_grads(a, dy, masks, act, du, planes):
    counts = tuple(len(a[mask]) for mask in masks)
    width, units = array_of(a[masks[0]][0]).shape[-1], du[0].shape[-1]
    rows, more = width // planes, 2 * (units // planes)
    total = shape((planes, rows + more, units), f32)
    flops = 4 * TREE * width * units
    (up,) = call(
        partial(up_grads_kernel, counts, planes),
        [far(total, rows=(0, rows))],
        [far(x) for mask in masks for x in a[mask]] + [far(x) for x in du],
        "up_grads",
        flops=flops,
        limit=20,
    )
    yield
    (both,) = call(
        partial(down_grads_kernel, counts, planes),
        [far(total, rows=(rows, more))],
        [far(x, rows=(0, TREE // GROUP)) for mask in masks for x in dy[mask]] + [far(x) for x in act],
        "down_grads",
        flops=flops,
        limit=24,
        into=(up,),
    )
    yield both


def second_back_kernel(
    own_ref, back_ref, first_ref, second_ref, dy_ref, middle_ref, vec_ref, mat_ref,
    dh_ref, dattn_ref, dctx_ref, sum_ref,
):
    micros, rows, width = middle_ref.shape
    sums = []
    for m in range(micros):
        grad = (
            own_ref[m].astype(f32)
            + back_ref[m].astype(f32)
            + first_ref[m].astype(f32)
            + second_ref[m].astype(f32)
        )
        unit, scale = norm_parts(middle_ref[m])
        dy = dy_ref[m].astype(f32)
        dh = dy + norm_back(grad, unit, scale, vec_ref[1:2])
        dh_ref[m] = dh
        dattn = dh.astype(bf16)
        dattn_ref[m] = dattn
        sums.append(
            [
                jnp.sum(value, axis=0, keepdims=True)
                for value in (dattn.astype(f32), dy, grad * unit, grad)
            ]
        )
    leave(dh_ref)
    dattn = dattn_ref[...].reshape(micros * rows, width)
    dctx = mm(dattn, mat_ref[...], NT).astype(bf16)
    for m in range(micros):
        for block in range(GROUP):
            dctx_ref[block, m] = dctx[m * rows : (m + 1) * rows, block * 128 : (block + 1) * 128]
    sum_ref[...] = jnp.concatenate(
        [first + second for first, second in zip(*sums)] + [jnp.zeros((4, width), f32)]
    )


def second_back(addends, dy, middle, vec, mat):
    dims = middle.shape
    return call(
        second_back_kernel,
        [
            far(shape(dims, f32)), shape(dims), shape((GROUP, dims[0], dims[1], 128)),
            shape((8, dims[2]), f32),
        ],
        [*addends, dy, middle, vec, mat],
        "norm2_back",
        flops=2 * middle.size * dims[2],
        limit=16,
    )


def first_back_kernel(*refs):
    groups, (x_ref, dh_ref, vec_ref, out_ref) = (refs[0:4], refs[4:8]), refs[8:]
    for m, group in enumerate(groups):
        grad = group[0][...].astype(f32)
        for ref in group[1:]:
            grad = grad + ref[...].astype(f32)
        unit, scale = norm_parts(x_ref[m].astype(f32))
        out_ref[m] = (dh_ref[m] + norm_back(grad, unit, scale, vec_ref[0:1])).astype(bf16)


def output_kernel(more, planes, plane_ref, own_ref, back_ref, first_ref, second_ref, middle_ref, vec_ref, out_ref, *rest):
    micros, rows, width = middle_ref.shape
    for m in range(micros):
        part = slice(0, rows)
        total = own_ref[m, part].astype(f32) + back_ref[m, part].astype(f32)
        total = total + first_ref[m, part].astype(f32) + second_ref[m, part].astype(f32)
        out_ref[m] = (middle_ref[m] + (total + vec_ref[3:4])).astype(bf16)
    leave(out_ref)
    if more:
        part = slice(rows, rows + more)
        for m in range(micros):
            total = own_ref[m, part].astype(f32) + back_ref[m, part].astype(f32)
            total = total + first_ref[m, part].astype(f32) + second_ref[m, part].astype(f32)
            rest[planes][m * more : (m + 1) * more] = total
        size = micros * more // planes
        for step in range(planes):
            at = pl.ds(pl.multiple_of((plane_ref[0] ^ step) * size, size), size)
            rest[step][...] = rest[planes][at, :].astype(rest[step].dtype)


def out_grads_kernel(planes, place_ref, dattn_ref, ctx_ref, *refs):
    outs, total_s = refs[:GROUP], refs[GROUP]
    total_s[...] = mm(rows_of([ctx_ref]), rows_of([dattn_ref]), TN)
    micros, more, _ = outs[0].shape
    size = micros * more // planes
    for mask in range(GROUP):
        for plane in range(planes):
            start = plane * GROUP * size + (place_ref[0] ^ mask) * size
            m, at = divmod(plane * size, more)
            outs[mask][m, at : at + size, :] = total_s[
                pl.ds(pl.multiple_of(start, size), size), :
            ].astype(bf16)
        leave(outs[mask])


def out_grads(place, ctx, dattn, parts, planes):
    width = dattn.shape[-1]
    rows = dattn.shape[1]
    more = parts[0].shape[1] - rows
    return call(
        partial(out_grads_kernel, planes),
        [far(shape(part.shape), rows=(rows, more)) for part in parts],
        [dattn, far(ctx)],
        "out_grads",
        scalars=(place[None],),
        scratch=[pltpu.VMEM((width, width), f32)],
        limit=16,
        light=True,
        into=parts,
    )


def qkv_grads_kernel(planes, plane_ref, sum_ref, g0, g1, u0, u1, mat_ref, vec_ref, *refs):
    *outs, terms_ref = refs
    rows = mat_ref.shape[0] // planes
    sums = sum_ref[0:1]
    lane = lax.broadcasted_iota(jnp.int32, (rows, 128), 1)
    grads = jnp.concatenate([rows_of_tree(ref) for ref in (g0, g1)])
    u0.ready()
    u1.ready()
    for step in (*range(1, planes), 0):
        plane = plane_ref[0] ^ step
        cols = pl.ds(pl.multiple_of(plane * rows, 128), rows)
        at = pl.ds(pl.multiple_of(plane * rows, rows), rows)
        units = jnp.concatenate([ref.at[:, :, cols][...].reshape(-1, rows) for ref in (u0, u1)])
        product = mm(units, grads, TN)
        mat = mat_ref[at, :].astype(f32)
        total = product * vec_ref[at, 0:1] + vec_ref[at, 1:2] * sums
        outs[step][...] = total.astype(outs[step].dtype)
        gain = jnp.sum(product * mat, axis=1, keepdims=True)
        bias = jnp.sum(mat * sums, axis=1, keepdims=True)
        terms_ref[at, :] = jnp.where(lane == 0, gain, jnp.where(lane == 1, bias, 0.0))


def rows_of_tree(ref):
    blocks, rows, width = ref.shape
    return ref[...].reshape(blocks * rows, width)


def qkv_grads(sums, grads, units, mat, vec_columns, plane, planes):
    width = mat.shape[0]
    return call(
        partial(qkv_grads_kernel, planes),
        [*kinds((width // planes, 384), range(planes)), shape((width, 128), f32)],
        [sums, *[far(x) for x in grads], *[far(x) for x in units], mat, vec_columns],
        "qkv_grads",
        scalars=(plane[None],),
        flops=2 * TREE * 2 * width * 384,
        limit=20,
    )


def pack_kernel(planes, q_ref, k_ref, v_ref, up_ref, *refs):
    *vectors, sent_ref = refs
    frow = up_ref.shape[1] // (planes * GROUP)
    lanes = sent_ref.shape[2] - 128
    row = lax.broadcasted_iota(jnp.int32, (16, 128), 0)
    tile = jnp.zeros((16, 128), f32)
    for at, ref in enumerate(vectors):
        value = ref[...].astype(f32)
        if ref.shape[1] < 128:
            value = jnp.pad(value, ((0, 0), (0, 128 - ref.shape[1])))
        tile = jnp.where(row == at, value, tile)
    for place in range(GROUP):
        for at, ref in enumerate((q_ref, k_ref, v_ref)):
            sent_ref[place, :, at * 128 : (at + 1) * 128] = ref[:, place * 128 : (place + 1) * 128]
        for plane in range(planes):
            start = (plane * GROUP + place) * frow
            sent_ref[place, :, 384 + plane * frow : 384 + (plane + 1) * frow] = up_ref[
                :, start : start + frow
            ]
        sent_ref[place, 0:16, lanes:] = tile.astype(bf16)


def split_kernel(got_ref, out_ref, down_ref, first_ref, second_ref):
    places, size, lanes = got_ref.shape
    rows, wrow, frow = places * size, out_ref.shape[0], down_ref.shape[0]
    for place in range(places):
        for i in range(3):
            at = i * rows + place * size
            first_ref[at : at + size] = got_ref[place, :, i * 128 : (i + 1) * 128]
        second_ref[place * size : (place + 1) * size] = got_ref[place, :, 384 : lanes - 128]
        at = 3 * rows + GROUP * wrow + place * 16
        first_ref[at : at + 16] = got_ref[place, 0:16, lanes - 128 :]
    for i in range(GROUP):
        at = 3 * rows + i * wrow
        first_ref[at : at + wrow] = out_ref[:, i * 128 : (i + 1) * 128]
    half = down_ref.shape[1] // 2
    second_ref[rows : rows + frow] = down_ref[:, 0:half]
    second_ref[rows + frow :] = down_ref[:, half:]


def home_kernel(planes, ffn_ref, *refs):
    mats, (home_ref, down_ref) = refs[:planes], refs[planes:]
    mat = mats[0][...]
    for part in mats[1:]:
        mat = mat + part[...].astype(f32)
    rows, frow = mat.shape[0], down_ref.shape[0]
    size, half = rows // GROUP, down_ref.shape[1] // 2
    for place in range(GROUP):
        at = slice(place * size, (place + 1) * size)
        home_ref[place, :, 0:384] = mat[at]
        home_ref[place, :, 384:] = ffn_ref[at]
    down_ref[:, 0:half] = ffn_ref[rows : rows + frow]
    down_ref[:, half:] = ffn_ref[rows + frow :]


def unpack_kernel(planes, home_ref, q_ref, k_ref, v_ref, up_ref):
    frow = up_ref.shape[1] // (planes * GROUP)
    for place in range(GROUP):
        for at, ref in enumerate((q_ref, k_ref, v_ref)):
            ref[:, place * 128 : (place + 1) * 128] = home_ref[place, :, at * 128 : (at + 1) * 128]
        for plane in range(planes):
            start = (plane * GROUP + place) * frow
            up_ref[:, start : start + frow] = home_ref[
                place, :, 384 + plane * frow : 384 + (plane + 1) * frow
            ]


def on_device(
    tokens, grad_out, w_query, w_key, w_value, b_query, b_value, w_attn_out, b_attn_out,
    w_up, b_up, w_down, b_down, ln1_gain, ln1_bias, ln2_gain, ln2_bias, leaf_parent,
):
    micro_count, row_count, width = tokens.shape
    count = lax.axis_size("dp")
    planes = count // GROUP
    index = lax.axis_index("dp")
    place = index % GROUP
    plane = index // GROUP
    wrow = w_query.shape[0]
    frow = w_down.shape[0]
    head_width = width // GROUP
    unit_width = planes * frow
    lanes = 3 * head_width + unit_width
    both = range(micro_count)
    chain.last = None

    small = (b_query, b_value, b_attn_out, b_down, ln1_gain, ln1_bias, ln2_gain, ln2_bias, b_up)
    if few(planes):
        (sent,) = call(
            partial(pack_kernel, planes),
            [shape((GROUP, wrow, lanes + 128))],
            [far(x) for x in (w_query, w_key, w_value, w_up, *[piece.reshape(1, -1) for piece in small])],
            "pack",
        )
    else:
        qkv_w = [w.reshape(wrow, GROUP, head_width) for w in (w_query, w_key, w_value)]
        up_w = w_up.reshape(wrow, planes, GROUP, frow).transpose(0, 2, 1, 3)
        sent = jnp.concatenate((*qkv_w, up_w.reshape(wrow, GROUP, unit_width)), axis=2)
        sent = sent.transpose(1, 0, 2)
    got = plane_exchange(sent)
    gather_x = Gather(after(tokens, got))

    if few(planes):
        first, second = call(
            split_kernel,
            [
                shape((4 * GROUP * wrow + 16 * GROUP, 128)),
                shape((GROUP * wrow + 2 * frow, unit_width)),
            ],
            [got, far(w_attn_out), far(w_down)],
            "split",
        )
        gather_x.corners(first)
        first_parts = column_parts(first)
        corner_x = gather_x.corner
        blocks_x = gather_x.blocks(first_parts)
        ffn_rows = lax.all_gather(second, "dp", axis=0, axis_index_groups=column_groups())
        mat_qkv, dy_rows, vec_qkv, vec_one, vec_two, vec_up = call(
            partial(order_kernel, wrow),
            [
                shape((width, 3 * head_width)), far(shape((micro_count, row_count + 2 * wrow, width))),
                shape((1, 3 * head_width), f32),
                shape((2, width), f32), shape((4, width), f32), shape((1, unit_width), f32),
            ],
            [after(first_parts[0], *corner_x), *first_parts[1:], far(grad_out)],
            "rows",
            scalars=(plane[None], place[None]),
            scratch=[pltpu.VMEM((16, width), f32)],
        )
    else:
        vector = jnp.stack(
            [jnp.pad(piece.astype(f32), (0, 128 - piece.shape[0])) for piece in small]
        )
        vectors = lax.all_gather(jnp.pad(vector, ((0, 7), (0, 0))), "dp")
        piece = width // count
        long = vectors[:, :8, :piece].transpose(1, 0, 2).reshape(8, width)
        vec_up = lax.dynamic_index_in_dim(
            vectors.reshape(planes, GROUP, 16, 128)[:, :, 8, :frow], place, 1, keepdims=False
        ).reshape(1, -1)
        vec_qkv = lax.dynamic_slice_in_dim(long[:2], place * head_width, head_width, axis=1)
        vec_qkv = jnp.concatenate(
            (vec_qkv[0], jnp.zeros((head_width,), f32), vec_qkv[1])
        )[None]
        vec_one = long[4:6]
        vec_two = jnp.stack((long[2], long[6], long[7], long[3]))
        got = got.reshape(GROUP * wrow, lanes)
        mat_qkv = column_parts(got[:, : 3 * head_width])[0]
        down_rows = jnp.concatenate((w_down[:, :unit_width], w_down[:, unit_width:]))
        ffn_rows = column_parts(jnp.concatenate((got[:, 3 * head_width :], down_rows)))[0]
        ffn_rows = ffn_rows.reshape(planes, -1, unit_width)
        mat_up = ffn_rows[:, : GROUP * wrow].reshape(width, unit_width)
        halves = ffn_rows[:, GROUP * wrow :].reshape(planes, 2, frow, unit_width)
        mat_down = halves.transpose(0, 2, 1, 3).reshape(unit_width, width)
        mat_out = far(lax.all_gather(w_attn_out, "dp", axis=0, tiled=True))
        dy_rows = grad_out
        gather_x.corners()
        blocks_x = gather_x.blocks(())
    gather_dy = Gather(dy_rows)

    parents = lax.dynamic_index_in_dim(leaf_parent, plane, 1, keepdims=False)
    heads = 2 * place + jnp.arange(2, dtype=jnp.int32)
    slopes = jnp.exp2(-8.0 * (heads.astype(f32) + 1.0) / HEADS)
    forward = []
    for m in both:
        blocks = [far(tokens, m)] + [of_micro(blocks_x[mask], m) for mask in range(1, GROUP)]
        forward.append(
            attention_forward(m, place, parents[m], slopes, blocks, vec_one, mat_qkv, vec_qkv)
        )
    plane_ctx = [plane_exchange(forward[m][0]) for m in both]
    gather_dy.corners(chain.last, plane_ctx[0])
    blocks_dy = gather_dy.blocks(plane_ctx[0], plane_ctx[1])
    if few(planes):
        window_of = (row_count, 2 * wrow)
        (mat_out,) = call(
            partial(out_order_kernel, planes),
            [shape((width, width))],
            [far(x, rows=window_of) for mask in range(GROUP) for x in blocks_dy[mask]],
            "attn_out",
            scalars=(place[None],),
        )

    middle, normed2, context = project(
        plane_ctx,
        far(tokens), vec_two, mat_out
    )
    if few(planes):
        mat_up, mat_down = call(
            ffn_order_kernel,
            [shape((width, unit_width)), shape((unit_width, width))],
            [far(ffn_rows)],
            "units",
        )

    more = 2 * wrow if few(planes) else 0
    split = ((0, 1), (2, 4, 3, 5), (6, 7))
    order = [mask for masks in split for mask in masks]
    grad_vec_up = 0.0
    y_parts, a_parts, act, du = [None] * GROUP, [None] * GROUP, [], []
    blocks_a2 = [[normed2], [swap(normed2, 1)]] + [None] * 6
    gather_a2 = Gather(normed2)
    for number, masks in enumerate(split):
        if number == 1:
            gather_a2.side = dict(zip((2, 4), lax.optimization_barrier((*gather_a2.side.values(), chain.last))))
            gather_a2.corners()
            for mask in (2, 4):
                blocks_a2[mask], blocks_a2[mask ^ 1] = [gather_a2.side[mask]], [swap(gather_a2.side[mask], 1)]
        if number == 2:
            corner = lax.optimization_barrier((*gather_a2.corner, chain.last))[:2]
            blocks_a2[6], blocks_a2[7] = list(corner), [swap(c, 1) for c in corner]
        y, da, act_part, du_part, up_sum = feed_forward(
            blocks_a2, blocks_dy, masks, mat_up, mat_down, vec_up, more
        )
        act.append(act_part)
        du.append(du_part)
        grad_vec_up = grad_vec_up + up_sum
        for i, mask in enumerate(masks):
            y_parts[mask] = y[i]
            a_parts[mask] = da[i]
    scatter2 = Scatter(a_parts)
    scatter2.first()
    if few(planes):
        steps = ffn_grads(blocks_a2, blocks_dy, order, act, du, planes)
        next(steps)
    else:
        flat = lambda blocks: jnp.concatenate(
            [x.reshape(-1, width) for mask in order for x in blocks[mask]]
        )
        units_flat = lambda parts: jnp.concatenate([x.reshape(-1, unit_width) for x in parts])
        grad_up = mm(flat(blocks_a2), units_flat(du), TN)
        grad_down = mm(units_flat(act), flat(blocks_dy), TN)
    scatter2.second()
    if few(planes):
        sum_ffn = lax.psum_scatter(
            after(next(steps), *scatter2.sides), "dp", scatter_dimension=0, axis_index_groups=column_groups()
        )
    dh, dattn, dctx, small_own = second_back(
        scatter2.addends(), far(grad_out), middle, vec_two, mat_out
    )
    plane_dctx = plane_exchange(dctx)
    if few(planes):
        y_parts = out_grads(place, context, dattn, y_parts, planes)
    scatter_y = Scatter(y_parts)
    scatter_y.first()

    scatter1, grad_qkv, sum_qkv = [], [], 0.0
    for m in both:
        parts, dqkv, dsum = attention_backward(
            m, place, parents[m], slopes, forward[m][2], forward[m][0], plane_dctx, forward[m][1], mat_qkv
        )
        scatter1.append(ScatterOne(parts, m, (scatter1[0].corner,) if m else scatter_y.corner))
        grad_qkv.append(dqkv)
        sum_qkv = sum_qkv + dsum
        if m == 0:
            scatter1[0].first()
            scatter_y.second()
    scatter1[0].second()
    scatter1[1].first(*scatter_y.sides)
    sums8 = jnp.broadcast_to(sum_qkv, (8, 384))
    if few(planes):
        own_mat, *others, norm_terms = qkv_grads(
            sums8, grad_qkv, [forward[m][3] for m in both], mat_qkv, vec_one.T, plane, planes
        )
        others = column_send(lax.optimization_barrier((others, scatter1[0].sides))[0])
    else:
        units = jnp.concatenate([forward[m][3].reshape(-1, width) for m in both])
        product = mm(units, jnp.concatenate([g.reshape(-1, 384) for g in grad_qkv]), TN)
        grad_mat = product * vec_one[0][:, None] + vec_one[1][:, None] * sum_qkv[None]
        mat32 = mat_qkv.astype(f32)
        norm_terms = jnp.stack(
            (jnp.sum(product * mat32, axis=1), jnp.sum(mat32 * sum_qkv[None], axis=1)), axis=1
        )
    scatter1[1].second()
    output, *out_parts = call(
        partial(output_kernel, more, planes),
        [far(shape(tokens.shape))] + (kinds((wrow, width), range(planes)) if more else []),
        [*scatter_y.addends(), middle, vec_two],
        "output",
        scalars=(plane[None],),
        scratch=[pltpu.VMEM((2 * more, width), f32)] if more else [],
        light=True,
        limit=16,
    )
    last = output

    if few(planes):
        home, sum_down = call(
            partial(home_kernel, planes),
            [shape((GROUP, wrow, lanes), f32), far(shape((frow, width), f32))],
            [after(sum_ffn, *scatter1[1].sides), own_mat, *others],
            "home",
            light=True,
        )
        home = plane_exchange(home)
        out_sums = column_send(lax.optimization_barrier((out_parts[1:], others))[0])
        sum_out = out_parts[0]
        for part in out_sums:
            sum_out = sum_out + part.astype(f32)
    else:

        def scattered(value):
            value = value.reshape(planes, -1, value.shape[1])
            return lax.psum_scatter(
                value, "dp", scatter_dimension=0, axis_index_groups=column_groups()
            )

        home = plane_exchange(
            jnp.concatenate((scattered(grad_mat), scattered(grad_up)), axis=1).reshape(
                GROUP, wrow, lanes
            )
        )
        sum_down = scattered(grad_down)
        grad_out_mat = mm(context.reshape(-1, width), dattn.reshape(-1, width), TN)
        sum_out = lax.psum_scatter(grad_out_mat, "dp", scatter_dimension=0, tiled=True)
    (grad_input,) = call(
        first_back_kernel,
        [far(shape(tokens.shape))],
        [*scatter1[0].addends(), *scatter1[1].addends(), far(tokens), far(dh), vec_one],
        "norm1_back",
    )
    if few(planes):
        *home_qkv, home_up = call(
            partial(unpack_kernel, planes),
            [far(shape((wrow, width), f32))] * 3 + [far(shape((wrow, unit_width * GROUP), f32))],
            [home],
            "unpack",
        )
    else:
        home_up = home[:, :, 3 * head_width :].reshape(GROUP, wrow, planes, frow)
        home_up = home_up.transpose(1, 2, 0, 3).reshape(wrow, -1)
        home_qkv = [
            home[:, :, at * head_width : (at + 1) * head_width].transpose(1, 0, 2).reshape(wrow, width)
            for at in range(3)
        ]

    sum_qkv, small_own, norm_terms, grad_vec_up, _ = lax.optimization_barrier(
        (sum_qkv, small_own, norm_terms, grad_vec_up, last)
    )

    def placed(piece):
        return lax.dynamic_update_slice_in_dim(
            jnp.zeros((width,), f32), piece, place * head_width, 0
        )

    up_terms = lax.dynamic_update_slice_in_dim(
        jnp.zeros((planes, GROUP, frow), f32),
        grad_vec_up.reshape(planes, 1, frow),
        place,
        1,
    )
    terms = jnp.concatenate(
        [
            piece.reshape(count, -1)
            for piece in (
                placed(sum_qkv[:head_width]),
                placed(sum_qkv[2 * head_width :]),
                small_own[0],
                small_own[1],
                norm_terms[:, 0],
                norm_terms[:, 1],
                small_own[2],
                small_own[3],
                up_terms,
            )
        ],
        axis=1,
    )
    sums = jnp.sum(lax.all_to_all(terms, "dp", 0, 0, tiled=True), axis=0)
    bounds = [0]
    for piece in small:
        bounds.append(bounds[-1] + piece.shape[0])
    pieces = [sums[bounds[at] : bounds[at + 1]] for at in range(len(small))]
    return (
        output, grad_input,
        home_qkv[0], home_qkv[1], home_qkv[2], sum_out, home_up, sum_down,
        pieces[0], pieces[1], pieces[2], pieces[8], pieces[3],
        pieces[4], pieces[5], pieces[6], pieces[7],
    )


def solution(mesh):
    row = P("dp", None)
    vec = P("dp")
    tok = P(None, "dp", None)
    return jax.shard_map(
        on_device,
        mesh=mesh,
        in_specs=(
            tok, tok, row, row, row, vec, vec, row, vec, row, vec, row, vec, vec, vec, vec, vec, P(),
        ),
        out_specs=(
            tok, tok, row, row, row, row, row, row, vec, vec, vec, vec, vec, vec, vec, vec, vec,
        ),
        check_vma=False,
    )
```

```python
from functools import partial

import jax
import jax.numpy as jnp
from jax import lax
from jax.experimental import pallas as pl
from jax.experimental.pallas import tpu as pltpu
from jax.sharding import PartitionSpec as P

HEADS = 16
BLK = 32
TRUNK_BLK = 16
SEG_BLK = 2
BRANCHES = 4
LEAVES = 8
TREE_BLK = 40

GROUP = 8
TREE = TREE_BLK * BLK
TRUNK = TRUNK_BLK * BLK
SEG = SEG_BLK * BLK
ROWS = 256
HALF = 128
HID = 64
NEG = -1e30

eps = 1e-05
bf16 = jnp.bfloat16
f32 = jnp.float32


def swap(value, mask):
    count = lax.axis_size("dp")
    pairs = [(source, source ^ mask) for source in range(count)]
    return lax.ppermute(value, "dp", pairs)


def after(value, *others):
    return lax.optimization_barrier((value, *others))[0]


class Chain:
    def __init__(self):
        self.last = None

    def hold(self, value):
        if self.last is None:
            return value
        return after(value, self.last)


chain = Chain()


class Part:
    def __init__(self, array, micro=None, turned=False, far=False, rows=None):
        self.array, self.micro, self.turned, self.far, self.rows = array, micro, turned, far or turned, rows

    def of(self, array):
        return Part(array, self.micro, self.turned, self.far, self.rows)


def far(array, micro=None, rows=None):
    return Part(array, micro, far=True, rows=rows)


def is_far(x):
    return isinstance(x, Part) and x.far


def array_of(x):
    return x.array if isinstance(x, Part) else x


def dims_of(x):
    if not isinstance(x, Part):
        return x.shape
    if x.rows is not None:
        return *x.array.shape[:-2], x.rows[1], x.array.shape[-1]
    if x.micro is None and not x.turned:
        return x.array.shape
    if x.turned:
        places, planes, rows, width = x.array.shape
        return places * planes * rows, width
    return x.array.shape[1:]


def pieces_of(dims, dtype):
    unit = 16 if dtype == bf16 else 8
    size = jnp.dtype(dtype).itemsize
    total = size
    for dim in dims:
        total *= dim
    if len(dims) == 3 and dims[0] >= 4:
        return [(at,) for at in range(dims[0])]
    lead = range(dims[0]) if len(dims) == 3 else [None]
    rows = dims[-2]
    best = 1
    for number in range(1, 9):
        if rows % (number * unit) == 0 and total // len(lead) // number >= 1 << 16:
            best = number
    step = rows // best
    cuts = [slice(at * step, (at + 1) * step) for at in range(best)]
    return [(cut,) if first is None else (first, cut) for first in lead for cut in cuts]


def window(ref, rows):
    return ref.at[pl.ds(*rows)] if len(ref.shape) == 2 else ref.at[:, pl.ds(*rows)]


class Loaded:
    def __init__(self, x, source, target, semaphore):
        self.target, self.copy = target, None
        if x.turned:
            places, planes, rows, _ = x.array.shape
            for place in range(places):
                for plane in range(planes):
                    at = (plane * places + place) * rows
                    pltpu.make_async_copy(
                        source.at[place, plane], target.at[at : at + rows], semaphore
                    ).start()
            self.copy = pltpu.make_async_copy(target, target, semaphore)
            return
        if x.micro is not None:
            source = source.at[x.micro]
        if x.rows is not None:
            source = window(source, x.rows)
        for piece in pieces_of(target.shape, target.dtype):
            pltpu.make_async_copy(source.at[piece], target.at[piece], semaphore).start()
        self.copy = pltpu.make_async_copy(source, target, semaphore)

    def ready(self):
        if self.copy is not None:
            self.copy.wait()
            self.copy = None
        return self.target

    shape = property(lambda self: self.target.shape)
    dtype = property(lambda self: self.target.dtype)
    at = property(lambda self: self.ready().at)

    def __getitem__(self, index):
        return self.ready()[index]


class Stored:
    def __init__(self, x, target, source, semaphore):
        self.source, self.semaphore = source, semaphore
        self.target = target if x.micro is None else target.at[x.micro]
        if x.rows is not None:
            self.target = window(target, x.rows)
        self.gone = False

    shape = property(lambda self: self.source.shape)
    dtype = property(lambda self: self.source.dtype)
    at = property(lambda self: self.source.at)

    def __getitem__(self, index):
        return self.source[index]

    def __setitem__(self, index, value):
        self.source[index] = value

    def leave(self):
        if not self.gone:
            for piece in pieces_of(self.source.shape, self.source.dtype):
                pltpu.make_async_copy(
                    self.source.at[piece], self.target.at[piece], self.semaphore
                ).start()
            self.gone = True

    def done(self):
        pltpu.make_async_copy(self.source, self.target, self.semaphore).wait()


def leave(*refs):
    for ref in refs:
        if isinstance(ref, Stored):
            ref.leave()


def near(x, ref):
    return ref.at[x.micro] if isinstance(x, Part) and x.micro is not None else ref


def call(kernel, outs, args, name, scalars=(), scratch=(), flops=0, ordered=True, into=(), limit=12, light=False):
    args = list(args)
    if ordered:
        first = args[0]
        held = chain.hold(array_of(first))
        args[0] = first.of(held) if isinstance(first, Part) else held
    outside = lambda x: pltpu.with_memory_space_constraint(x, pltpu.HBM)
    arrays = [outside(x.array) if is_far(x) else array_of(x) for x in args]
    arrays += [outside(x) for x in into]
    shapes = [array_of(x) for x in outs]
    colored = [
        pltpu.HBM(x.shape, x.dtype) if is_far(out) else x for out, x in zip(outs, shapes)
    ]
    nscalar, nargs, nouts = len(scalars), len(args), len(outs)
    far_in = [i for i, x in enumerate(args) if is_far(x)]
    far_out = [i for i, x in enumerate(outs) if is_far(x)]

    def body(*refs):
        numbers = refs[:nscalar]
        inputs = list(refs[nscalar : nscalar + nargs])
        outputs = list(refs[nscalar + len(arrays) : nscalar + len(arrays) + nouts])
        rest = list(refs[nscalar + len(arrays) + nouts :])
        sems = rest[-2:]
        loaded = [
            Loaded(args[i], inputs[i], rest[k], sems[0].at[k]) for k, i in enumerate(far_in)
        ]
        stored = [
            Stored(outs[i], outputs[i], rest[len(far_in) + k], sems[1].at[k])
            for k, i in enumerate(far_out)
        ]
        inputs = [near(x, ref) for x, ref in zip(args, inputs)]
        outputs = [near(x, ref) for x, ref in zip(outs, outputs)]
        for k, i in enumerate(far_in):
            inputs[i] = loaded[k]
        for k, i in enumerate(far_out):
            outputs[i] = stored[k]
        kernel(*numbers, *inputs, *outputs, *rest[len(far_in) + len(far_out) : -2])
        for x in loaded:
            x.ready()
        leave(*stored)
        for x in stored:
            x.done()

    bytes_accessed = 0 if light else sum(x.size * x.dtype.itemsize for x in arrays + shapes)
    place = lambda x: pl.BlockSpec(memory_space=pltpu.HBM if is_far(x) else pltpu.VMEM)
    kernel_call = pl.pallas_call(
        body,
        out_shape=tuple(colored),
        in_specs=[pl.BlockSpec(memory_space=pltpu.SMEM)] * nscalar
        + [place(x) for x in args]
        + [pl.BlockSpec(memory_space=pltpu.HBM) for _ in into],
        out_specs=tuple(place(x) for x in outs),
        scratch_shapes=[pltpu.VMEM(dims_of(args[i]), array_of(args[i]).dtype) for i in far_in]
        + [pltpu.VMEM(dims_of(outs[i]), array_of(outs[i]).dtype) for i in far_out]
        + list(scratch)
        + [
            pltpu.SemaphoreType.DMA((max(1, len(far_in)),)),
            pltpu.SemaphoreType.DMA((max(1, len(far_out)),)),
        ],
        input_output_aliases={nscalar + nargs + i: i for i in range(len(into))},
        compiler_params=pltpu.CompilerParams(vmem_limit_bytes=limit << 20),
        cost_estimate=pl.CostEstimate(
            flops=flops, transcendentals=0, bytes_accessed=bytes_accessed
        ),
        name=name,
    )
    result = kernel_call(*scalars, *arrays)
    if ordered:
        chain.last = result[-1]
    return result


def shape(dims, dtype=bf16):
    return jax.ShapeDtypeStruct(dims, dtype)


def kinds(dims, masks=range(GROUP)):
    return [shape(dims, bf16 if mask else f32) for mask in masks]


class Gather:
    def __init__(self, own):
        self.own = own
        self.side = {2: swap(own, 2), 4: swap(own, 4)}

    def corners(self, *gate):
        cut = lax.optimization_barrier(([self.side[2][0], self.side[4][1]], gate))[0]
        self.corner = [swap(cut[0], 4), swap(cut[1], 2)]

    def blocks(self, gate, corner_gate=()):
        even = lax.optimization_barrier(({0: self.own, **self.side}, gate))[0]
        self.corner = lax.optimization_barrier((self.corner, gate, corner_gate))[0]
        blocks = [even[mask] if mask in even else swap(even[mask ^ 1], 1) for mask in range(6)]
        return [[block] for block in blocks] + [self.corner, [swap(c, 1) for c in self.corner]]


def of_micro(blocks, m):
    return far(blocks[0], m) if len(blocks) == 1 else far(blocks[m])


def add_kernel(plan, *refs):
    ninputs = len(refs) - len(plan)
    for out_ref, rows in zip(refs[ninputs:], plan):
        for lead, addends in enumerate(rows):
            total = None
            for number, at in addends:
                value = (refs[number][...] if at is None else refs[number][at]).astype(f32)
                total = value if total is None else total + value
            if len(rows) == 1:
                out_ref[...] = total.astype(out_ref.dtype)
            else:
                out_ref[lead] = total.astype(out_ref.dtype)


def swap_back(parts, others=()):
    masks = (6, 2, 4, 0)
    odd = lax.optimization_barrier(([parts[mask ^ 1] for mask in masks], others))[0]
    return dict(zip(masks, lax.optimization_barrier([swap(part, 1) for part in odd])))


class Scatter:
    def __init__(self, parts):
        self.parts = parts
        self.back = {mask: swap(parts[mask ^ 1], 1) for mask in (6, 2, 4, 0)}

    def first(self):
        dims = self.parts[6].shape[1:]
        plan = [[[(0, m), (1, m)]] for m in range(2)]
        total = call(
            partial(add_kernel, plan), [shape(dims)] * 2, [far(self.back[6]), far(self.parts[6])], "corner", light=True
        )
        self.corner = swap(total[0], 4), swap(total[1], 2)

    def second(self):
        self.back[0], self.back[2], self.back[4] = lax.optimization_barrier([self.back[mask] for mask in (0, 2, 4)])
        dims = self.parts[2].shape
        plan = [
            [[(0, 0), (1, 0), (4, None)], [(0, 1), (1, 1)]],
            [[(2, 0), (3, 0)], [(2, 1), (3, 1), (5, None)]],
        ]
        total = call(
            partial(add_kernel, plan), [shape(dims)] * 2,
            [far(x) for x in (self.back[2], self.parts[2], self.back[4], self.parts[4], *self.corner)],
            "sides", light=True,
        )
        self.sides = swap(total[0], 2), swap(total[1], 4)

    def addends(self):
        return [far(x) for x in (self.parts[0], self.back[0], *self.sides)]


class ScatterOne:
    def __init__(self, parts, micro, others):
        self.parts = parts
        self.via = 4 if micro == 0 else 2
        self.back = swap_back(parts, others)

    def first(self, *gate):
        total = call(
            partial(add_kernel, [[[(0, None), (1, None)]]]), [shape(self.parts[6].shape)],
            [far(after(self.back[6], *gate)), far(self.parts[6])], "corner", light=True,
        )[0]
        self.corner = swap(total, self.via)

    def second(self):
        via = self.via
        plan = [[[(0, None), (1, None)]], [[(2, None), (3, None), (4, None)]]]
        total = call(
            partial(add_kernel, plan), [shape(self.parts[6].shape)] * 2,
            [
                far(x)
                for x in (self.back[via], self.parts[via], self.back[6 ^ via], self.parts[6 ^ via], self.corner)
            ],
            "sides", light=True,
        )
        self.sides = swap(total[0], via), swap(total[1], 6 ^ via)

    def addends(self):
        return [far(x) for x in (self.parts[0], self.back[0], *self.sides)]


def plane_groups():
    count = lax.axis_size("dp")
    return [list(range(first, first + GROUP)) for first in range(0, count, GROUP)]


def column_groups():
    count = lax.axis_size("dp")
    return [list(range(place, count, GROUP)) for place in range(GROUP)]


def plane_exchange(value):
    return lax.all_to_all(value, "dp", 0, 0, tiled=True, axis_index_groups=plane_groups())


def column_parts(value):
    planes = lax.axis_size("dp") // GROUP
    if planes > 4:
        return [
            lax.all_gather(value, "dp", axis=0, axis_index_groups=column_groups(), tiled=True)
        ]
    return [value] + [swap(value, GROUP * step) for step in range(1, planes)]


def column_send(parts):
    return [swap(part, GROUP * (step + 1)) for step, part in enumerate(parts)]


def few(planes):
    return planes <= 4


def order_kernel(wrow, plane_ref, place_ref, *refs):
    *parts, dy_ref, mat_ref, long_ref, qkv_ref, one_ref, two_ref, up_ref, long_s = refs
    for m in range(2):
        long_ref[m, 0 : dy_ref.shape[1]] = dy_ref[m]
    planes = len(parts)
    rows = mat_ref.shape[0] // planes
    piece = mat_ref.shape[0] // (planes * GROUP)
    source = lax.broadcasted_iota(jnp.int32, (128, 128), 0)
    target = lax.broadcasted_iota(jnp.int32, (128, 128), 1)
    each = 128 // piece
    for step, part in enumerate(parts):
        plane = plane_ref[0] ^ step
        at = pl.ds(pl.multiple_of(plane * rows, rows), rows)
        for i in range(3):
            mat_ref[at, i * 128 : (i + 1) * 128] = part[i * rows : (i + 1) * rows]
        start = 3 * rows
        for i in range(GROUP):
            value = part[start + i * wrow : start + (i + 1) * wrow]
            at = pl.ds(pl.multiple_of(dy_ref.shape[1] + (plane % (planes // 2)) * wrow, wrow), wrow)
            long_ref.at[plane // (planes // 2), at, i * 128 : (i + 1) * 128][...] = value
        start += GROUP * wrow
        for first in range(0, GROUP, each):
            total = jnp.zeros((16, 128), f32)
            for i in range(each):
                chosen = (source < piece) & (source + i * piece == target)
                tile = part[start + (first + i) * 16 : start + (first + i + 1) * 16]
                total = total + mm(tile, jnp.where(chosen, 1.0, 0.0).astype(bf16), NN)
            lane = (plane * GROUP + first) * piece
            long_s[:, pl.ds(pl.multiple_of(lane, 128), 128)] = total
        frow = up_ref.shape[1] // planes
        tile = part[pl.ds(pl.multiple_of(start + place_ref[0] * 16, 16), 16), :].astype(f32)
        up_ref[0:1, pl.ds(pl.multiple_of(plane * frow, 128), frow)] = tile[8:9]
    at = pl.ds(pl.multiple_of(place_ref[0] * 128, 128), 128)
    heads = long_s[0:8, at]
    qkv_ref[...] = jnp.concatenate((heads[0:1], jnp.zeros((1, 128), f32), heads[1:2]), axis=1)
    one_ref[...] = long_s[4:6]
    two_ref[0:1] = long_s[2:3]
    two_ref[1:3] = long_s[6:8]
    two_ref[3:4] = long_s[3:4]


def ffn_order_kernel(rows_ref, up_ref, down_ref):
    planes = rows_ref.shape[0]
    rows, units = up_ref.shape[0] // planes, up_ref.shape[1]
    frow = units // planes
    for plane in range(planes):
        up_ref[plane * rows : (plane + 1) * rows] = rows_ref[plane, 0:rows]
        down_ref[plane * frow : (plane + 1) * frow, 0:units] = rows_ref[plane, rows : rows + frow]
        down_ref[plane * frow : (plane + 1) * frow, units:] = rows_ref[plane, rows + frow :]


def out_order_kernel(planes, place_ref, *refs):
    *blocks, out_ref = refs
    size = out_ref.shape[0] // (planes * GROUP)
    half = planes // 2
    at = 0
    for mask in range(GROUP):
        for plane in range(planes):
            m, step = divmod(plane, half)
            ref = blocks[mask] if mask < 6 else blocks[6 + (mask - 6) * 2 + m]
            value = ref[m, step * size : (step + 1) * size] if mask < 6 else ref[step * size : (step + 1) * size]
            start = plane * GROUP * size + (place_ref[0] ^ mask) * size
            out_ref[pl.ds(pl.multiple_of(start, size), size), :] = value


def mm(left, right, contract):
    return lax.dot_general(left, right, (contract, ((), ())), preferred_element_type=f32)


NN = ((1,), (0,))
NT = ((1,), (1,))
TN = ((0,), (0,))


def split3(values):
    high = values.astype(bf16)
    rest = values - high.astype(f32)
    middle = rest.astype(bf16)
    low = (rest - middle.astype(f32)).astype(bf16)
    return high, middle, low


def norm_parts(values):
    center = values - jnp.mean(values, axis=-1, keepdims=True)
    spread = jnp.mean(center * center, axis=-1, keepdims=True)
    scale = lax.rsqrt(spread + eps)
    return center * scale, scale


def norm_back(grad, unit, scale, gain):
    scaled = grad * gain
    return scale * (
        scaled
        - jnp.mean(scaled, axis=-1, keepdims=True)
        - unit * jnp.mean(scaled * unit, axis=-1, keepdims=True)
    )


def fill_heads(query, key, slope_ref, query_s, key_s, place, start, rows):
    lane = lax.broadcasted_iota(jnp.int32, (rows, 128), 1)
    one = jnp.ones((rows, 128), bf16)
    zero = jnp.zeros((rows, 128), bf16)
    at = pl.ds(start, rows)
    for head in range(2):
        mine = (lane < HID) if head == 0 else (lane >= HID)
        base = HID if head == 0 else 0
        high, middle, low = split3(place * slope_ref[head])
        extra = jnp.where(
            lane == base,
            high,
            jnp.where(lane == base + 1, middle, jnp.where(lane == base + 2, low, zero)),
        )
        ones = jnp.where((lane >= base) & (lane < base + 3), one, zero)
        query_s[head, at, :] = jnp.where(mine, query, ones)
        key_s[head, at, :] = jnp.where(mine, key, extra)


def positions(start, rows):
    row = lax.broadcasted_iota(jnp.int32, (rows, 128), 0) + start
    after_trunk = row - TRUNK
    inside = after_trunk & (SEG - 1)
    return jnp.where(
        row < TRUNK, row, TRUNK + inside + jnp.where(after_trunk < BRANCHES * SEG, 0, SEG)
    ).astype(f32)


def tile_masks():
    row = lax.broadcasted_iota(jnp.int32, (HALF, HALF), 1)
    col = lax.broadcasted_iota(jnp.int32, (HALF, HALF), 0)
    same = (row // SEG) == (col // SEG)
    segment = jnp.where(same & (col <= row), 0.0, NEG)
    parent = jnp.where(same, 0.0, NEG)
    trow = lax.broadcasted_iota(jnp.int32, (ROWS, ROWS), 1)
    tcol = lax.broadcasted_iota(jnp.int32, (ROWS, ROWS), 0)
    causal = jnp.where(tcol <= trow, 0.0, NEG)
    return segment, parent, causal


def parent_rows(parent_ref, leaf):
    start = TRUNK + (parent_ref[leaf] - 1) * SEG
    return pl.ds(pl.multiple_of(start, SEG), SEG)


def tile_pieces(tile):
    if tile < TRUNK // ROWS:
        return (tile + 1) * ROWS, True, [], []
    start = tile * ROWS
    own = [start, start + HALF]
    first_leaf = TRUNK + BRANCHES * SEG
    leaves = []
    if start >= first_leaf:
        leaf = (start - first_leaf) // SEG
        leaves = [(leaf, leaf + 1), (leaf + 2, leaf + 3)]
    return TRUNK, False, own, leaves


def tile_scores(tile, key_ref, query, masks, side):
    segment, parent, causal = masks
    trunk, last, own, leaves = tile_pieces(tile)
    scores = mm(key_ref[0:trunk, :], query, NT)
    pieces = []
    if last:
        if trunk > ROWS:
            pieces.append(scores[: trunk - ROWS])
        pieces.append(scores[trunk - ROWS :] + causal)
    else:
        pieces.append(scores)
    if own:
        pieces.append(
            jnp.concatenate(
                [
                    mm(key_ref[at : at + HALF, :], query[i * HALF : (i + 1) * HALF], NT) + segment
                    for i, at in enumerate(own)
                ],
                axis=1,
            )
        )
    if leaves:
        pieces.append(
            jnp.concatenate(
                [
                    mm(rows, query[i * HALF : (i + 1) * HALF], NT) + parent
                    for i, rows in enumerate(side)
                ],
                axis=1,
            )
        )
    return pieces


def forward_kernel(
    micro, place_ref, parent_ref, slope_ref,
    a0, a1, a2, a3, a4, a5, a6, a7, vec_ref, mat_ref, bias_ref,
    ctx_ref, log_ref, packed_ref, unit_ref,
    query_s, key_s, value_s, ctx_s,
):
    rows = TREE // GROUP
    for mask, block_ref in zip((1, 2, 3, 4, 5, 0, 6, 7), (a1, a2, a3, a4, a5, a0, a6, a7)):
        start = pl.multiple_of((place_ref[0] ^ mask) * rows, rows)
        unit, _ = norm_parts(block_ref[...].astype(f32))
        unit_ref[mask] = unit.astype(bf16)
        normed = (unit * vec_ref[0:1] + vec_ref[1:2]).astype(bf16)
        part = (mm(normed, mat_ref[...], NN) + bias_ref[...]).astype(bf16)
        packed_ref.source[pl.ds(start, rows), :] = part
        value_s[pl.ds(start, rows), :] = part[:, 256:384]
        fill_heads(
            part[:, 0:128] * jnp.asarray(0.125, bf16), part[:, 128:256],
            slope_ref, query_s, key_s, positions(start, rows), start, rows,
        )
    leave(unit_ref, packed_ref)
    masks = tile_masks()
    for tile in range(TREE // ROWS):
        trunk, last, own, leaves = tile_pieces(tile)
        at = slice(tile * ROWS, (tile + 1) * ROWS)
        contexts = []
        side_values = [
            jnp.concatenate([value_s[parent_rows(parent_ref, leaf), :] for leaf in pair])
            for pair in leaves
        ]
        for head in range(2):
            query = query_s[head, at, :]
            side = [
                jnp.concatenate([key_s[head, parent_rows(parent_ref, leaf), :] for leaf in pair])
                for pair in leaves
            ]
            pieces = tile_scores(tile, key_s.at[head], query, masks, side)
            peak = pieces[0].max(axis=0, keepdims=True)
            for piece in pieces[1:]:
                peak = jnp.maximum(peak, piece.max(axis=0, keepdims=True))
            probs = [jnp.exp(piece - peak) for piece in pieces]
            total = probs[0].sum(axis=0, keepdims=True)
            for piece in probs[1:]:
                total = total + piece.sum(axis=0, keepdims=True)
            probs = [piece.astype(bf16) for piece in probs]
            ntrunk = len(probs) - bool(own) - bool(leaves)
            start = 0
            context = None
            for piece in probs[:ntrunk]:
                term = mm(value_s[start : start + piece.shape[0], :], piece, TN)
                context = term if context is None else context + term
                start += piece.shape[0]
            if own:
                context = context + jnp.concatenate(
                    [
                        mm(value_s[first : first + HALF, :], probs[ntrunk][:, i * HALF : (i + 1) * HALF], TN)
                        for i, first in enumerate(own)
                    ],
                    axis=1,
                )
            if leaves:
                context = context + jnp.concatenate(
                    [
                        mm(side_values[i], probs[ntrunk + 1][:, i * HALF : (i + 1) * HALF], TN)
                        for i in range(2)
                    ],
                    axis=1,
                )
            half = slice(head * HID, (head + 1) * HID)
            contexts.append(context[half] / total)
            log_ref[head : head + 1, at] = peak + jnp.log(total)
        ctx_s[at, :] = jnp.concatenate(contexts, axis=0).T.astype(bf16)
    for block in range(GROUP):
        ctx_ref[block] = ctx_s[block * rows : (block + 1) * rows, :]


def attention_forward(micro, place, parents, slopes, blocks, vec, mat, bias):
    rows, width = TREE // GROUP, mat.shape[0]
    return call(
        partial(forward_kernel, micro),
        [
            shape((GROUP, rows, 128)), shape((8, TREE), f32),
            far(shape((TREE, 384))), far(shape((GROUP, rows, width))),
        ],
        [*blocks, vec, mat, bias],
        "tree_attention",
        scalars=(place[None], parents, slopes),
        scratch=[
            pltpu.VMEM((2, TREE, 128), bf16),
            pltpu.VMEM((2, TREE, 128), bf16),
            pltpu.VMEM((TREE, 128), bf16),
            pltpu.VMEM((TREE, 128), bf16),
        ],
        flops=4_000_000_000,
        limit=14,
    )


def backward_kernel(
    micro, place_ref, parent_ref, slope_ref,
    grad_ref, packed_ref, ctx_ref, log_ref, mat_ref,
    o0, o1, o2, o3, o4, o5, o6, o7, dqkv_ref, sum_ref,
    query_s, key_s, value_s, grad_s, dkey_s, dvalue_s, dquery_s,
):
    rows = TREE // GROUP
    lane = lax.broadcasted_iota(jnp.int32, (rows, 128), 1)
    zero = jnp.zeros((rows, 128), bf16)
    for block in range(GROUP):
        start = block * rows
        at = pl.ds(start, rows)
        part = packed_ref[at, :]
        fill_heads(
            part[:, 0:128] * jnp.asarray(0.125, bf16), part[:, 128:256],
            slope_ref, query_s, key_s, positions(start, rows), start, rows,
        )
        value = part[:, 256:384]
        grad = grad_ref[block, micro]
        for head in range(2):
            mine = (lane < HID) if head == 0 else (lane >= HID)
            value_s[head, at, :] = jnp.where(mine, value, zero)
            grad_s[head, at, :] = jnp.where(mine, grad, zero)
        dquery_s[at, :] = grad.astype(f32) * ctx_ref[block].astype(f32)
    dkey_s[...] = jnp.zeros_like(dkey_s)
    dvalue_s[...] = jnp.zeros_like(dvalue_s)
    masks = tile_masks()
    for tile in range(TREE // ROWS):
        trunk, last, own, leaves = tile_pieces(tile)
        at = slice(tile * ROWS, (tile + 1) * ROWS)
        deltas = dquery_s[at, :].T
        dqueries = []
        for head in range(2):
            half = slice(head * HID, (head + 1) * HID)
            query = query_s[head, at, :]
            grad = grad_s[head, at, :]
            keys = key_s.at[head]
            values = value_s.at[head]
            side = [
                jnp.concatenate([key_s[head, parent_rows(parent_ref, leaf), :] for leaf in pair])
                for pair in leaves
            ]
            pieces = tile_scores(tile, keys, query, masks, side)
            level = log_ref[head : head + 1, at]
            delta = deltas[half].sum(axis=0, keepdims=True)
            ntrunk = len(pieces) - bool(own) - bool(leaves)
            dquery = None
            start = 0
            for piece in pieces[:ntrunk]:
                size = piece.shape[0]
                span = slice(start, start + size)
                probs = jnp.exp(piece - level)
                dprobs = mm(values[span, :], grad, NT)
                dscores = (probs * (dprobs - delta)).astype(bf16)
                dvalue_s[span, :] += mm(probs.astype(bf16), grad, NN)
                dkey_s[head, span, :] += mm(dscores, query, NN)
                term = mm(keys[span, :], dscores, TN)
                dquery = term if dquery is None else dquery + term
                start += size
            extra = []
            for i, first in enumerate(own):
                cols = slice(i * HALF, (i + 1) * HALF)
                span = slice(first, first + HALF)
                probs = jnp.exp(pieces[ntrunk][:, cols] - level[:, cols])
                dprobs = mm(values[span, :], grad[cols], NT)
                dscores = (probs * (dprobs - delta[:, cols])).astype(bf16)
                dvalue_s[span, :] += mm(probs.astype(bf16), grad[cols], NN)
                dkey_s[head, span, :] += mm(dscores, query[cols], NN)
                extra.append(mm(keys[span, :], dscores, TN))
            if own:
                dquery = dquery + jnp.concatenate(extra, axis=1)
            extra = []
            for i, pair in enumerate(leaves):
                cols = slice(i * HALF, (i + 1) * HALF)
                side_value = jnp.concatenate(
                    [value_s[head, parent_rows(parent_ref, leaf), :] for leaf in pair]
                )
                probs = jnp.exp(pieces[ntrunk + 1][:, cols] - level[:, cols])
                dprobs = mm(side_value, grad[cols], NT)
                dscores = (probs * (dprobs - delta[:, cols])).astype(bf16)
                dval = mm(probs.astype(bf16), grad[cols], NN)
                dkey = mm(dscores, query[cols], NN)
                for j, leaf in enumerate(pair):
                    span = parent_rows(parent_ref, leaf)
                    dvalue_s[span, :] += dval[j * SEG : (j + 1) * SEG]
                    dkey_s[head, span, :] += dkey[j * SEG : (j + 1) * SEG]
                extra.append(mm(side[i], dscores, TN))
            if leaves:
                dquery = dquery + jnp.concatenate(extra, axis=1)
            dqueries.append(dquery[half] * 0.125)
        dquery_s[at, :] = jnp.concatenate(dqueries, axis=0).T
    sums = jnp.zeros((1, 384), f32)
    for mask, out_ref in reversed(list(enumerate((o0, o1, o2, o3, o4, o5, o6, o7)))):
        at = pl.ds(pl.multiple_of((place_ref[0] ^ mask) * rows, rows), rows)
        dkey = jnp.where(lane < HID, dkey_s[0, at, :], dkey_s[1, at, :])
        dqkv = jnp.concatenate(
            (dquery_s[at, :].astype(bf16), dkey.astype(bf16), dvalue_s[at, :].astype(bf16)), axis=1
        )
        dqkv_ref[mask] = dqkv
        sums = sums + jnp.sum(dqkv.astype(f32), axis=0, keepdims=True)
        out_ref[...] = mm(dqkv, mat_ref[...], NT).astype(out_ref.dtype)
        leave(out_ref)
    sum_ref[...] = jnp.broadcast_to(sums, (8, 384))


def attention_backward(micro, place, parents, slopes, packed, ctx, grad, logs, mat):
    rows = TREE // GROUP
    width = mat.shape[0]
    result = call(
        partial(backward_kernel, micro),
        [far(x) for x in kinds((rows, width))] + [far(shape((GROUP, rows, 384))), shape((8, 384), f32)],
        [grad, far(packed), ctx, logs, mat],
        "tree_attention_back",
        scalars=(place[None], parents, slopes),
        scratch=[
            pltpu.VMEM((2, TREE, 128), bf16),
            pltpu.VMEM((2, TREE, 128), bf16),
            pltpu.VMEM((2, TREE, 128), bf16),
            pltpu.VMEM((2, TREE, 128), bf16),
            pltpu.VMEM((2, TREE, 128), f32),
            pltpu.VMEM((TREE, 128), f32),
            pltpu.VMEM((TREE, 128), f32),
        ],
        flops=10_000_000_000,
        limit=16,
    )
    return result[:GROUP], result[GROUP], result[GROUP + 1][0]


def project_kernel(p0, p1, x_ref, vec_ref, mat_ref, middle_ref, normed_ref, ctx_ref, total_s):
    micros, rows, width = middle_ref.shape
    for m, part in enumerate((p0, p1)):
        for block in range(GROUP):
            total_s[m * rows : (m + 1) * rows, block * 128 : (block + 1) * 128] = part[block]
    attn = mm(total_s[...], mat_ref[...], NN) + vec_ref[0:1]
    for m in range(micros):
        ctx_ref[m] = total_s[m * rows : (m + 1) * rows]
        middle = x_ref[m].astype(f32) + attn[m * rows : (m + 1) * rows]
        middle_ref[m] = middle
        unit, _ = norm_parts(middle)
        normed_ref[m] = (unit * vec_ref[1:2] + vec_ref[2:3]).astype(bf16)


def project(parts, x, vec, mat):
    dims = dims_of(x)
    return call(
        project_kernel,
        [shape(dims, f32), shape(dims), far(shape(dims))],
        [*parts, x, vec, mat],
        "project",
        scratch=[pltpu.VMEM((dims[0] * dims[1], dims[2]), bf16)],
        flops=2 * dims[0] * dims[1] * dims[2] * dims[2],
        limit=16,
    )


def rows_of(refs):
    if len(refs) == 1:
        micros, rows, width = refs[0].shape
        return refs[0][...].reshape(micros * rows, width)
    return jnp.concatenate([ref[...] for ref in refs])


def ffn_kernel(counts, *refs):
    refs = list(refs)

    def take(number):
        taken = refs[:number]
        del refs[:number]
        return taken

    a_refs = [take(number) for number in counts]
    dy_refs = [take(number) for number in counts]
    up_ref, down_ref, bias_ref = take(3)
    y_refs, da_refs = take(len(counts)), take(len(counts))
    act_ref, du_ref, sum_ref = refs
    sums = jnp.zeros((1, up_ref.shape[1]), f32)
    for i in range(len(counts)):
        upper = mm(rows_of(a_refs[i]), up_ref[...], NN) + bias_ref[...]
        square = upper * upper
        bent = jnp.tanh(upper * (0.7978845608028654 + (0.7978845608028654 * 0.044715) * square))
        half = 0.5 * (1.0 + bent)
        active = (upper * half).astype(bf16)
        slope = half + (0.5 * upper) * (1.0 - bent * bent) * (
            0.7978845608028654 + (3.0 * 0.7978845608028654 * 0.044715) * square
        )
        act_ref[i] = active
        du = mm(rows_of(dy_refs[i]), down_ref[...], NT) * slope
        sums = sums + jnp.sum(du, axis=0, keepdims=True)
        du = du.astype(bf16)
        du_ref[i] = du
        kind = da_refs[i].dtype
        da_refs[i][...] = mm(du, up_ref[...], NT).astype(kind).reshape(da_refs[i].shape)
        y_refs[i][...] = mm(active, down_ref[...], NN).astype(bf16).reshape(y_refs[i].shape)
        leave(y_refs[i], da_refs[i])
    sum_ref[...] = jnp.broadcast_to(sums, sum_ref.shape)


def feed_forward(a, dy, masks, up, down, bias, more):
    counts = tuple(len(a[mask]) for mask in masks)
    micros, (rows, width), units = 2, array_of(a[masks[0]][0]).shape[-2:], up.shape[1]
    dims = (micros, rows, width)
    long = (micros, rows + more, width)
    number = len(masks)
    result = call(
        partial(ffn_kernel, counts),
        [far(shape(long), rows=(0, rows)) for _ in masks]
        + [far(x) for x in kinds(dims, masks)]
        + [far(shape((number, micros * rows, units))) for _ in range(2)]
        + [shape((8, units), f32)],
        [far(x) for mask in masks for x in a[mask]]
        + [far(x, rows=(0, rows)) for mask in masks for x in dy[mask]]
        + [up, down, bias],
        "feed_forward",
        flops=8 * number * micros * rows * width * units,
        limit=18,
    )
    return result[:number], result[number : 2 * number], result[-3], result[-2], result[-1][0]


def flat_rows(groups):
    return jnp.concatenate([rows_of(group) for group in groups])


def take_groups(refs, counts):
    groups, at = [], 0
    for number in counts:
        groups.append(refs[at : at + number])
        at += number
    return groups, refs[at:]


def up_grads_kernel(counts, planes, *refs):
    groups, refs = take_groups(refs, counts)
    *du_refs, out_ref = refs
    units = du_refs[0].shape[-1]
    rows = groups[0][0].shape[-1] // planes
    du = jnp.concatenate([ref[...].reshape(-1, units) for ref in du_refs])
    for plane in range(planes):
        at = slice(plane * rows, (plane + 1) * rows)
        parts = [ref[..., at].reshape(-1, rows) for group in groups for ref in group]
        out_ref[plane] = mm(jnp.concatenate(parts), du, TN)


def down_grads_kernel(counts, planes, *refs):
    groups, refs = take_groups(refs, counts)
    *act_refs, out_ref = refs
    units = act_refs[0].shape[-1]
    frow = units // planes
    dy = flat_rows(groups)
    for plane in range(planes):
        at = slice(plane * frow, (plane + 1) * frow)
        act = jnp.concatenate([ref[:, :, at].reshape(-1, frow) for ref in act_refs])
        down = mm(act, dy, TN)
        out_ref[plane, 0:frow] = down[:, :units]
        out_ref[plane, frow:] = down[:, units:]


def ffn_grads(a, dy, masks, act, du, planes):
    counts = tuple(len(a[mask]) for mask in masks)
    width, units = array_of(a[masks[0]][0]).shape[-1], du[0].shape[-1]
    rows, more = width // planes, 2 * (units // planes)
    total = shape((planes, rows + more, units), f32)
    flops = 4 * TREE * width * units
    (up,) = call(
        partial(up_grads_kernel, counts, planes),
        [far(total, rows=(0, rows))],
        [far(x) for mask in masks for x in a[mask]] + [far(x) for x in du],
        "up_grads",
        flops=flops,
        limit=20,
    )
    yield
    (both,) = call(
        partial(down_grads_kernel, counts, planes),
        [far(total, rows=(rows, more))],
        [far(x, rows=(0, TREE // GROUP)) for mask in masks for x in dy[mask]] + [far(x) for x in act],
        "down_grads",
        flops=flops,
        limit=24,
        into=(up,),
    )
    yield both


def second_back_kernel(
    own_ref, back_ref, first_ref, second_ref, dy_ref, middle_ref, vec_ref, mat_ref,
    dh_ref, dattn_ref, dctx_ref, sum_ref,
):
    micros, rows, width = middle_ref.shape
    sums = []
    for m in range(micros):
        grad = (
            own_ref[m].astype(f32)
            + back_ref[m].astype(f32)
            + first_ref[m].astype(f32)
            + second_ref[m].astype(f32)
        )
        unit, scale = norm_parts(middle_ref[m])
        dy = dy_ref[m].astype(f32)
        dh = dy + norm_back(grad, unit, scale, vec_ref[1:2])
        dh_ref[m] = dh
        dattn = dh.astype(bf16)
        dattn_ref[m] = dattn
        sums.append(
            [
                jnp.sum(value, axis=0, keepdims=True)
                for value in (dattn.astype(f32), dy, grad * unit, grad)
            ]
        )
    leave(dh_ref)
    dattn = dattn_ref[...].reshape(micros * rows, width)
    dctx = mm(dattn, mat_ref[...], NT).astype(bf16)
    for m in range(micros):
        for block in range(GROUP):
            dctx_ref[block, m] = dctx[m * rows : (m + 1) * rows, block * 128 : (block + 1) * 128]
    sum_ref[...] = jnp.concatenate(
        [first + second for first, second in zip(*sums)] + [jnp.zeros((4, width), f32)]
    )


def second_back(addends, dy, middle, vec, mat):
    dims = middle.shape
    return call(
        second_back_kernel,
        [
            far(shape(dims, f32)), shape(dims), shape((GROUP, dims[0], dims[1], 128)),
            shape((8, dims[2]), f32),
        ],
        [*addends, dy, middle, vec, mat],
        "norm2_back",
        flops=2 * middle.size * dims[2],
        limit=16,
    )


def first_back_kernel(*refs):
    groups, (x_ref, dh_ref, vec_ref, out_ref) = (refs[0:4], refs[4:8]), refs[8:]
    for m, group in enumerate(groups):
        grad = group[0][...].astype(f32)
        for ref in group[1:]:
            grad = grad + ref[...].astype(f32)
        unit, scale = norm_parts(x_ref[m].astype(f32))
        out_ref[m] = (dh_ref[m] + norm_back(grad, unit, scale, vec_ref[0:1])).astype(bf16)


def output_kernel(more, planes, plane_ref, own_ref, back_ref, first_ref, second_ref, middle_ref, vec_ref, out_ref, *rest):
    micros, rows, width = middle_ref.shape
    for m in range(micros):
        part = slice(0, rows)
        total = own_ref[m, part].astype(f32) + back_ref[m, part].astype(f32)
        total = total + first_ref[m, part].astype(f32) + second_ref[m, part].astype(f32)
        out_ref[m] = (middle_ref[m] + (total + vec_ref[3:4])).astype(bf16)
    leave(out_ref)
    if more:
        part = slice(rows, rows + more)
        for m in range(micros):
            total = own_ref[m, part].astype(f32) + back_ref[m, part].astype(f32)
            total = total + first_ref[m, part].astype(f32) + second_ref[m, part].astype(f32)
            rest[planes][m * more : (m + 1) * more] = total
        size = micros * more // planes
        for step in range(planes):
            at = pl.ds(pl.multiple_of((plane_ref[0] ^ step) * size, size), size)
            rest[step][...] = rest[planes][at, :].astype(rest[step].dtype)


def out_grads_kernel(planes, place_ref, dattn_ref, ctx_ref, *refs):
    outs, total_s = refs[:GROUP], refs[GROUP]
    total_s[...] = mm(rows_of([ctx_ref]), rows_of([dattn_ref]), TN)
    micros, more, _ = outs[0].shape
    size = micros * more // planes
    for mask in range(GROUP):
        for plane in range(planes):
            start = plane * GROUP * size + (place_ref[0] ^ mask) * size
            m, at = divmod(plane * size, more)
            outs[mask][m, at : at + size, :] = total_s[
                pl.ds(pl.multiple_of(start, size), size), :
            ].astype(bf16)
        leave(outs[mask])


def out_grads(place, ctx, dattn, parts, planes):
    width = dattn.shape[-1]
    rows = dattn.shape[1]
    more = parts[0].shape[1] - rows
    return call(
        partial(out_grads_kernel, planes),
        [far(shape(part.shape), rows=(rows, more)) for part in parts],
        [dattn, far(ctx)],
        "out_grads",
        scalars=(place[None],),
        scratch=[pltpu.VMEM((width, width), f32)],
        limit=16,
        light=True,
        into=parts,
    )


def qkv_grads_kernel(planes, plane_ref, sum_ref, g0, g1, u0, u1, mat_ref, vec_ref, *refs):
    *outs, terms_ref = refs
    rows = mat_ref.shape[0] // planes
    sums = sum_ref[0:1]
    lane = lax.broadcasted_iota(jnp.int32, (rows, 128), 1)
    grads = jnp.concatenate([rows_of_tree(ref) for ref in (g0, g1)])
    u0.ready()
    u1.ready()
    for step in (*range(1, planes), 0):
        plane = plane_ref[0] ^ step
        cols = pl.ds(pl.multiple_of(plane * rows, 128), rows)
        at = pl.ds(pl.multiple_of(plane * rows, rows), rows)
        units = jnp.concatenate([ref.at[:, :, cols][...].reshape(-1, rows) for ref in (u0, u1)])
        product = mm(units, grads, TN)
        mat = mat_ref[at, :].astype(f32)
        total = product * vec_ref[at, 0:1] + vec_ref[at, 1:2] * sums
        outs[step][...] = total.astype(outs[step].dtype)
        gain = jnp.sum(product * mat, axis=1, keepdims=True)
        bias = jnp.sum(mat * sums, axis=1, keepdims=True)
        terms_ref[at, :] = jnp.where(lane == 0, gain, jnp.where(lane == 1, bias, 0.0))


def rows_of_tree(ref):
    blocks, rows, width = ref.shape
    return ref[...].reshape(blocks * rows, width)


def qkv_grads(sums, grads, units, mat, vec_columns, plane, planes):
    width = mat.shape[0]
    return call(
        partial(qkv_grads_kernel, planes),
        [*kinds((width // planes, 384), range(planes)), shape((width, 128), f32)],
        [sums, *[far(x) for x in grads], *[far(x) for x in units], mat, vec_columns],
        "qkv_grads",
        scalars=(plane[None],),
        flops=2 * TREE * 2 * width * 384,
        limit=20,
    )


def pack_kernel(planes, q_ref, k_ref, v_ref, up_ref, *refs):
    *vectors, sent_ref = refs
    frow = up_ref.shape[1] // (planes * GROUP)
    lanes = sent_ref.shape[2] - 128
    row = lax.broadcasted_iota(jnp.int32, (16, 128), 0)
    tile = jnp.zeros((16, 128), f32)
    for at, ref in enumerate(vectors):
        value = ref[...].astype(f32)
        if ref.shape[1] < 128:
            value = jnp.pad(value, ((0, 0), (0, 128 - ref.shape[1])))
        tile = jnp.where(row == at, value, tile)
    for place in range(GROUP):
        for at, ref in enumerate((q_ref, k_ref, v_ref)):
            sent_ref[place, :, at * 128 : (at + 1) * 128] = ref[:, place * 128 : (place + 1) * 128]
        for plane in range(planes):
            start = (plane * GROUP + place) * frow
            sent_ref[place, :, 384 + plane * frow : 384 + (plane + 1) * frow] = up_ref[
                :, start : start + frow
            ]
        sent_ref[place, 0:16, lanes:] = tile.astype(bf16)


def split_kernel(got_ref, out_ref, down_ref, first_ref, second_ref):
    places, size, lanes = got_ref.shape
    rows, wrow, frow = places * size, out_ref.shape[0], down_ref.shape[0]
    for place in range(places):
        for i in range(3):
            at = i * rows + place * size
            first_ref[at : at + size] = got_ref[place, :, i * 128 : (i + 1) * 128]
        second_ref[place * size : (place + 1) * size] = got_ref[place, :, 384 : lanes - 128]
        at = 3 * rows + GROUP * wrow + place * 16
        first_ref[at : at + 16] = got_ref[place, 0:16, lanes - 128 :]
    for i in range(GROUP):
        at = 3 * rows + i * wrow
        first_ref[at : at + wrow] = out_ref[:, i * 128 : (i + 1) * 128]
    half = down_ref.shape[1] // 2
    second_ref[rows : rows + frow] = down_ref[:, 0:half]
    second_ref[rows + frow :] = down_ref[:, half:]


def home_kernel(planes, ffn_ref, *refs):
    mats, (home_ref, down_ref) = refs[:planes], refs[planes:]
    mat = mats[0][...]
    for part in mats[1:]:
        mat = mat + part[...].astype(f32)
    rows, frow = mat.shape[0], down_ref.shape[0]
    size, half = rows // GROUP, down_ref.shape[1] // 2
    for place in range(GROUP):
        at = slice(place * size, (place + 1) * size)
        home_ref[place, :, 0:384] = mat[at]
        home_ref[place, :, 384:] = ffn_ref[at]
    down_ref[:, 0:half] = ffn_ref[rows : rows + frow]
    down_ref[:, half:] = ffn_ref[rows + frow :]


def unpack_kernel(planes, home_ref, q_ref, k_ref, v_ref, up_ref):
    frow = up_ref.shape[1] // (planes * GROUP)
    for place in range(GROUP):
        for at, ref in enumerate((q_ref, k_ref, v_ref)):
            ref[:, place * 128 : (place + 1) * 128] = home_ref[place, :, at * 128 : (at + 1) * 128]
        for plane in range(planes):
            start = (plane * GROUP + place) * frow
            up_ref[:, start : start + frow] = home_ref[
                place, :, 384 + plane * frow : 384 + (plane + 1) * frow
            ]


def on_device(
    tokens, grad_out, w_query, w_key, w_value, b_query, b_value, w_attn_out, b_attn_out,
    w_up, b_up, w_down, b_down, ln1_gain, ln1_bias, ln2_gain, ln2_bias, leaf_parent,
):
    micro_count, row_count, width = tokens.shape
    count = lax.axis_size("dp")
    planes = count // GROUP
    index = lax.axis_index("dp")
    place = index % GROUP
    plane = index // GROUP
    wrow = w_query.shape[0]
    frow = w_down.shape[0]
    head_width = width // GROUP
    unit_width = planes * frow
    lanes = 3 * head_width + unit_width
    both = range(micro_count)
    chain.last = None

    small = (b_query, b_value, b_attn_out, b_down, ln1_gain, ln1_bias, ln2_gain, ln2_bias, b_up)
    if few(planes):
        (sent,) = call(
            partial(pack_kernel, planes),
            [shape((GROUP, wrow, lanes + 128))],
            [far(x) for x in (w_query, w_key, w_value, w_up, *[piece.reshape(1, -1) for piece in small])],
            "pack",
        )
    else:
        qkv_w = [w.reshape(wrow, GROUP, head_width) for w in (w_query, w_key, w_value)]
        up_w = w_up.reshape(wrow, planes, GROUP, frow).transpose(0, 2, 1, 3)
        sent = jnp.concatenate((*qkv_w, up_w.reshape(wrow, GROUP, unit_width)), axis=2)
        sent = sent.transpose(1, 0, 2)
    got = plane_exchange(sent)
    gather_x = Gather(after(tokens, got))

    if few(planes):
        first, second = call(
            split_kernel,
            [
                shape((4 * GROUP * wrow + 16 * GROUP, 128)),
                shape((GROUP * wrow + 2 * frow, unit_width)),
            ],
            [got, far(w_attn_out), far(w_down)],
            "split",
        )
        gather_x.corners(first)
        first_parts = column_parts(first)
        corner_x = gather_x.corner
        blocks_x = gather_x.blocks(first_parts)
        ffn_rows = lax.all_gather(second, "dp", axis=0, axis_index_groups=column_groups())
        mat_qkv, dy_rows, vec_qkv, vec_one, vec_two, vec_up = call(
            partial(order_kernel, wrow),
            [
                shape((width, 3 * head_width)), far(shape((micro_count, row_count + 2 * wrow, width))),
                shape((1, 3 * head_width), f32),
                shape((2, width), f32), shape((4, width), f32), shape((1, unit_width), f32),
            ],
            [after(first_parts[0], *corner_x), *first_parts[1:], far(grad_out)],
            "rows",
            scalars=(plane[None], place[None]),
            scratch=[pltpu.VMEM((16, width), f32)],
        )
    else:
        vector = jnp.stack(
            [jnp.pad(piece.astype(f32), (0, 128 - piece.shape[0])) for piece in small]
        )
        vectors = lax.all_gather(jnp.pad(vector, ((0, 7), (0, 0))), "dp")
        piece = width // count
        long = vectors[:, :8, :piece].transpose(1, 0, 2).reshape(8, width)
        vec_up = lax.dynamic_index_in_dim(
            vectors.reshape(planes, GROUP, 16, 128)[:, :, 8, :frow], place, 1, keepdims=False
        ).reshape(1, -1)
        vec_qkv = lax.dynamic_slice_in_dim(long[:2], place * head_width, head_width, axis=1)
        vec_qkv = jnp.concatenate(
            (vec_qkv[0], jnp.zeros((head_width,), f32), vec_qkv[1])
        )[None]
        vec_one = long[4:6]
        vec_two = jnp.stack((long[2], long[6], long[7], long[3]))
        got = got.reshape(GROUP * wrow, lanes)
        mat_qkv = column_parts(got[:, : 3 * head_width])[0]
        down_rows = jnp.concatenate((w_down[:, :unit_width], w_down[:, unit_width:]))
        ffn_rows = column_parts(jnp.concatenate((got[:, 3 * head_width :], down_rows)))[0]
        ffn_rows = ffn_rows.reshape(planes, -1, unit_width)
        mat_up = ffn_rows[:, : GROUP * wrow].reshape(width, unit_width)
        halves = ffn_rows[:, GROUP * wrow :].reshape(planes, 2, frow, unit_width)
        mat_down = halves.transpose(0, 2, 1, 3).reshape(unit_width, width)
        mat_out = far(lax.all_gather(w_attn_out, "dp", axis=0, tiled=True))
        dy_rows = grad_out
        gather_x.corners()
        blocks_x = gather_x.blocks(())
    gather_dy = Gather(dy_rows)

    parents = lax.dynamic_index_in_dim(leaf_parent, plane, 1, keepdims=False)
    heads = 2 * place + jnp.arange(2, dtype=jnp.int32)
    slopes = jnp.exp2(-8.0 * (heads.astype(f32) + 1.0) / HEADS)
    forward = []
    for m in both:
        blocks = [far(tokens, m)] + [of_micro(blocks_x[mask], m) for mask in range(1, GROUP)]
        forward.append(
            attention_forward(m, place, parents[m], slopes, blocks, vec_one, mat_qkv, vec_qkv)
        )
    plane_ctx = [plane_exchange(forward[m][0]) for m in both]
    gather_dy.corners(chain.last, plane_ctx[0])
    blocks_dy = gather_dy.blocks(plane_ctx[0], plane_ctx[1])
    if few(planes):
        window_of = (row_count, 2 * wrow)
        (mat_out,) = call(
            partial(out_order_kernel, planes),
            [shape((width, width))],
            [far(x, rows=window_of) for mask in range(GROUP) for x in blocks_dy[mask]],
            "attn_out",
            scalars=(place[None],),
        )

    middle, normed2, context = project(
        plane_ctx,
        far(tokens), vec_two, mat_out
    )
    if few(planes):
        mat_up, mat_down = call(
            ffn_order_kernel,
            [shape((width, unit_width)), shape((unit_width, width))],
            [far(ffn_rows)],
            "units",
        )

    more = 2 * wrow if few(planes) else 0
    split = ((0, 1), (2, 4, 3, 5), (6, 7))
    order = [mask for masks in split for mask in masks]
    grad_vec_up = 0.0
    y_parts, a_parts, act, du = [None] * GROUP, [None] * GROUP, [], []
    blocks_a2 = [[normed2], [swap(normed2, 1)]] + [None] * 6
    gather_a2 = Gather(normed2)
    for number, masks in enumerate(split):
        if number == 1:
            gather_a2.side = dict(zip((2, 4), lax.optimization_barrier((*gather_a2.side.values(), chain.last))))
            gather_a2.corners()
            for mask in (2, 4):
                blocks_a2[mask], blocks_a2[mask ^ 1] = [gather_a2.side[mask]], [swap(gather_a2.side[mask], 1)]
        if number == 2:
            corner = lax.optimization_barrier((*gather_a2.corner, chain.last))[:2]
            blocks_a2[6], blocks_a2[7] = list(corner), [swap(c, 1) for c in corner]
        y, da, act_part, du_part, up_sum = feed_forward(
            blocks_a2, blocks_dy, masks, mat_up, mat_down, vec_up, more
        )
        act.append(act_part)
        du.append(du_part)
        grad_vec_up = grad_vec_up + up_sum
        for i, mask in enumerate(masks):
            y_parts[mask] = y[i]
            a_parts[mask] = da[i]
    scatter2 = Scatter(a_parts)
    scatter2.first()
    if few(planes):
        steps = ffn_grads(blocks_a2, blocks_dy, order, act, du, planes)
        next(steps)
    else:
        flat = lambda blocks: jnp.concatenate(
            [x.reshape(-1, width) for mask in order for x in blocks[mask]]
        )
        units_flat = lambda parts: jnp.concatenate([x.reshape(-1, unit_width) for x in parts])
        grad_up = mm(flat(blocks_a2), units_flat(du), TN)
        grad_down = mm(units_flat(act), flat(blocks_dy), TN)
    scatter2.second()
    if few(planes):
        sum_ffn = lax.psum_scatter(
            after(next(steps), *scatter2.sides), "dp", scatter_dimension=0, axis_index_groups=column_groups()
        )
    dh, dattn, dctx, small_own = second_back(
        scatter2.addends(), far(grad_out), middle, vec_two, mat_out
    )
    plane_dctx = plane_exchange(dctx)
    if few(planes):
        y_parts = out_grads(place, context, dattn, y_parts, planes)
    scatter_y = Scatter(y_parts)
    scatter_y.first()

    scatter1, grad_qkv, sum_qkv = [], [], 0.0
    for m in both:
        parts, dqkv, dsum = attention_backward(
            m, place, parents[m], slopes, forward[m][2], forward[m][0], plane_dctx, forward[m][1], mat_qkv
        )
        scatter1.append(ScatterOne(parts, m, (scatter1[0].corner,) if m else scatter_y.corner))
        grad_qkv.append(dqkv)
        sum_qkv = sum_qkv + dsum
        if m == 0:
            scatter1[0].first()
            scatter_y.second()
    scatter1[0].second()
    scatter1[1].first(*scatter_y.sides)
    sums8 = jnp.broadcast_to(sum_qkv, (8, 384))
    if few(planes):
        own_mat, *others, norm_terms = qkv_grads(
            sums8, grad_qkv, [forward[m][3] for m in both], mat_qkv, vec_one.T, plane, planes
        )
        others = column_send(lax.optimization_barrier((others, scatter1[0].sides))[0])
    else:
        units = jnp.concatenate([forward[m][3].reshape(-1, width) for m in both])
        product = mm(units, jnp.concatenate([g.reshape(-1, 384) for g in grad_qkv]), TN)
        grad_mat = product * vec_one[0][:, None] + vec_one[1][:, None] * sum_qkv[None]
        mat32 = mat_qkv.astype(f32)
        norm_terms = jnp.stack(
            (jnp.sum(product * mat32, axis=1), jnp.sum(mat32 * sum_qkv[None], axis=1)), axis=1
        )
    scatter1[1].second()
    last = chain.last
    output, *out_parts = call(
        partial(output_kernel, more, planes),
        [far(shape(tokens.shape))] + (kinds((wrow, width), range(planes)) if more else []),
        [*scatter_y.addends(), middle, vec_two],
        "output",
        scalars=(plane[None],),
        scratch=[pltpu.VMEM((2 * more, width), f32)] if more else [],
        light=True,
        limit=16,
    )

    if few(planes):
        home, sum_down = call(
            partial(home_kernel, planes),
            [shape((GROUP, wrow, lanes), f32), far(shape((frow, width), f32))],
            [far(after(sum_ffn, *scatter1[1].sides)), own_mat, *others],
            "home",
            light=True,
        )
        home = plane_exchange(home)
        out_sums = column_send(lax.optimization_barrier((out_parts[1:], others))[0])
    else:

        def scattered(value):
            value = value.reshape(planes, -1, value.shape[1])
            return lax.psum_scatter(
                value, "dp", scatter_dimension=0, axis_index_groups=column_groups()
            )

        home = plane_exchange(
            jnp.concatenate((scattered(grad_mat), scattered(grad_up)), axis=1).reshape(
                GROUP, wrow, lanes
            )
        )
        sum_down = scattered(grad_down)
        grad_out_mat = mm(context.reshape(-1, width), dattn.reshape(-1, width), TN)
        sum_out = lax.psum_scatter(grad_out_mat, "dp", scatter_dimension=0, tiled=True)
    (grad_input,) = call(
        first_back_kernel,
        [far(shape(tokens.shape))],
        [*scatter1[0].addends(), *scatter1[1].addends(), far(tokens), far(dh), vec_one],
        "norm1_back",
    )
    if few(planes):
        sum_out = after(out_parts[0], grad_input)
        for part in out_sums:
            sum_out = sum_out + part.astype(f32)
    if few(planes):
        *home_qkv, home_up = call(
            partial(unpack_kernel, planes),
            [far(shape((wrow, width), f32))] * 3 + [far(shape((wrow, unit_width * GROUP), f32))],
            [home],
            "unpack",
        )
    else:
        home_up = home[:, :, 3 * head_width :].reshape(GROUP, wrow, planes, frow)
        home_up = home_up.transpose(1, 2, 0, 3).reshape(wrow, -1)
        home_qkv = [
            home[:, :, at * head_width : (at + 1) * head_width].transpose(1, 0, 2).reshape(wrow, width)
            for at in range(3)
        ]

    sum_qkv, small_own, norm_terms, grad_vec_up, _ = lax.optimization_barrier(
        (sum_qkv, small_own, norm_terms, grad_vec_up, last)
    )

    def placed(piece):
        return lax.dynamic_update_slice_in_dim(
            jnp.zeros((width,), f32), piece, place * head_width, 0
        )

    up_terms = lax.dynamic_update_slice_in_dim(
        jnp.zeros((planes, GROUP, frow), f32),
        grad_vec_up.reshape(planes, 1, frow),
        place,
        1,
    )
    terms = jnp.concatenate(
        [
            piece.reshape(count, -1)
            for piece in (
                placed(sum_qkv[:head_width]),
                placed(sum_qkv[2 * head_width :]),
                small_own[0],
                small_own[1],
                norm_terms[:, 0],
                norm_terms[:, 1],
                small_own[2],
                small_own[3],
                up_terms,
            )
        ],
        axis=1,
    )
    sums = jnp.sum(lax.all_to_all(terms, "dp", 0, 0, tiled=True), axis=0)
    bounds = [0]
    for piece in small:
        bounds.append(bounds[-1] + piece.shape[0])
    pieces = [sums[bounds[at] : bounds[at + 1]] for at in range(len(small))]
    return (
        output, grad_input,
        home_qkv[0], home_qkv[1], home_qkv[2], sum_out, home_up, sum_down,
        pieces[0], pieces[1], pieces[2], pieces[8], pieces[3],
        pieces[4], pieces[5], pieces[6], pieces[7],
    )


def solution(mesh):
    row = P("dp", None)
    vec = P("dp")
    tok = P(None, "dp", None)
    return jax.shard_map(
        on_device,
        mesh=mesh,
        in_specs=(
            tok, tok, row, row, row, vec, vec, row, vec, row, vec, row, vec, vec, vec, vec, vec, P(),
        ),
        out_specs=(
            tok, tok, row, row, row, row, row, row, vec, vec, vec, vec, vec, vec, vec, vec, vec,
        ),
        check_vma=False,
    )
```

```python
from functools import partial

import jax
import jax.numpy as jnp
from jax import lax
from jax.experimental import pallas as pl
from jax.experimental.pallas import tpu as pltpu
from jax.sharding import PartitionSpec as P

HEADS = 16
BLK = 32
TRUNK_BLK = 16
SEG_BLK = 2
BRANCHES = 4
LEAVES = 8
TREE_BLK = 40

GROUP = 8
TREE = TREE_BLK * BLK
TRUNK = TRUNK_BLK * BLK
SEG = SEG_BLK * BLK
ROWS = 256
HALF = 128
HID = 64
NEG = -1e30

eps = 1e-05
bf16 = jnp.bfloat16
f32 = jnp.float32


def swap(value, mask):
    count = lax.axis_size("dp")
    pairs = [(source, source ^ mask) for source in range(count)]
    return lax.ppermute(value, "dp", pairs)


def after(value, *others):
    return lax.optimization_barrier((value, *others))[0]


class Chain:
    def __init__(self):
        self.last = None

    def hold(self, value):
        if self.last is None:
            return value
        return after(value, self.last)


chain = Chain()


class Part:
    def __init__(self, array, micro=None, turned=False, far=False, rows=None):
        self.array, self.micro, self.turned, self.far, self.rows = array, micro, turned, far or turned, rows

    def of(self, array):
        return Part(array, self.micro, self.turned, self.far, self.rows)


def far(array, micro=None, rows=None):
    return Part(array, micro, far=True, rows=rows)


def is_far(x):
    return isinstance(x, Part) and x.far


def array_of(x):
    return x.array if isinstance(x, Part) else x


def dims_of(x):
    if not isinstance(x, Part):
        return x.shape
    if x.rows is not None:
        return *x.array.shape[:-2], x.rows[1], x.array.shape[-1]
    if x.micro is None and not x.turned:
        return x.array.shape
    if x.turned:
        places, planes, rows, width = x.array.shape
        return places * planes * rows, width
    return x.array.shape[1:]


def pieces_of(dims, dtype):
    unit = 16 if dtype == bf16 else 8
    size = jnp.dtype(dtype).itemsize
    total = size
    for dim in dims:
        total *= dim
    if len(dims) == 3 and dims[0] >= 4:
        return [(at,) for at in range(dims[0])]
    lead = range(dims[0]) if len(dims) == 3 else [None]
    rows = dims[-2]
    best = 1
    for number in range(1, 9):
        if rows % (number * unit) == 0 and total // len(lead) // number >= 1 << 16:
            best = number
    step = rows // best
    cuts = [slice(at * step, (at + 1) * step) for at in range(best)]
    return [(cut,) if first is None else (first, cut) for first in lead for cut in cuts]


def window(ref, rows):
    return ref.at[pl.ds(*rows)] if len(ref.shape) == 2 else ref.at[:, pl.ds(*rows)]


class Loaded:
    def __init__(self, x, source, target, semaphore):
        self.target, self.copy = target, None
        if x.turned:
            places, planes, rows, _ = x.array.shape
            for place in range(places):
                for plane in range(planes):
                    at = (plane * places + place) * rows
                    pltpu.make_async_copy(
                        source.at[place, plane], target.at[at : at + rows], semaphore
                    ).start()
            self.copy = pltpu.make_async_copy(target, target, semaphore)
            return
        if x.micro is not None:
            source = source.at[x.micro]
        if x.rows is not None:
            source = window(source, x.rows)
        for piece in pieces_of(target.shape, target.dtype):
            pltpu.make_async_copy(source.at[piece], target.at[piece], semaphore).start()
        self.copy = pltpu.make_async_copy(source, target, semaphore)

    def ready(self):
        if self.copy is not None:
            self.copy.wait()
            self.copy = None
        return self.target

    shape = property(lambda self: self.target.shape)
    dtype = property(lambda self: self.target.dtype)
    at = property(lambda self: self.ready().at)

    def __getitem__(self, index):
        return self.ready()[index]


class Stored:
    def __init__(self, x, target, source, semaphore):
        self.source, self.semaphore = source, semaphore
        self.target = target if x.micro is None else target.at[x.micro]
        if x.rows is not None:
            self.target = window(target, x.rows)
        self.gone = False

    shape = property(lambda self: self.source.shape)
    dtype = property(lambda self: self.source.dtype)
    at = property(lambda self: self.source.at)

    def __getitem__(self, index):
        return self.source[index]

    def __setitem__(self, index, value):
        self.source[index] = value

    def leave(self):
        if not self.gone:
            for piece in pieces_of(self.source.shape, self.source.dtype):
                pltpu.make_async_copy(
                    self.source.at[piece], self.target.at[piece], self.semaphore
                ).start()
            self.gone = True

    def done(self):
        pltpu.make_async_copy(self.source, self.target, self.semaphore).wait()


def leave(*refs):
    for ref in refs:
        if isinstance(ref, Stored):
            ref.leave()


def near(x, ref):
    return ref.at[x.micro] if isinstance(x, Part) and x.micro is not None else ref


def call(kernel, outs, args, name, scalars=(), scratch=(), flops=0, ordered=True, into=(), limit=12, light=False):
    args = list(args)
    if ordered:
        first = args[0]
        held = chain.hold(array_of(first))
        args[0] = first.of(held) if isinstance(first, Part) else held
    outside = lambda x: pltpu.with_memory_space_constraint(x, pltpu.HBM)
    arrays = [outside(x.array) if is_far(x) else array_of(x) for x in args]
    arrays += [outside(x) for x in into]
    shapes = [array_of(x) for x in outs]
    colored = [
        pltpu.HBM(x.shape, x.dtype) if is_far(out) else x for out, x in zip(outs, shapes)
    ]
    nscalar, nargs, nouts = len(scalars), len(args), len(outs)
    far_in = [i for i, x in enumerate(args) if is_far(x)]
    far_out = [i for i, x in enumerate(outs) if is_far(x)]

    def body(*refs):
        numbers = refs[:nscalar]
        inputs = list(refs[nscalar : nscalar + nargs])
        outputs = list(refs[nscalar + len(arrays) : nscalar + len(arrays) + nouts])
        rest = list(refs[nscalar + len(arrays) + nouts :])
        sems = rest[-2:]
        loaded = [
            Loaded(args[i], inputs[i], rest[k], sems[0].at[k]) for k, i in enumerate(far_in)
        ]
        stored = [
            Stored(outs[i], outputs[i], rest[len(far_in) + k], sems[1].at[k])
            for k, i in enumerate(far_out)
        ]
        inputs = [near(x, ref) for x, ref in zip(args, inputs)]
        outputs = [near(x, ref) for x, ref in zip(outs, outputs)]
        for k, i in enumerate(far_in):
            inputs[i] = loaded[k]
        for k, i in enumerate(far_out):
            outputs[i] = stored[k]
        kernel(*numbers, *inputs, *outputs, *rest[len(far_in) + len(far_out) : -2])
        for x in loaded:
            x.ready()
        leave(*stored)
        for x in stored:
            x.done()

    bytes_accessed = 0 if light else sum(x.size * x.dtype.itemsize for x in arrays + shapes)
    place = lambda x: pl.BlockSpec(memory_space=pltpu.HBM if is_far(x) else pltpu.VMEM)
    kernel_call = pl.pallas_call(
        body,
        out_shape=tuple(colored),
        in_specs=[pl.BlockSpec(memory_space=pltpu.SMEM)] * nscalar
        + [place(x) for x in args]
        + [pl.BlockSpec(memory_space=pltpu.HBM) for _ in into],
        out_specs=tuple(place(x) for x in outs),
        scratch_shapes=[pltpu.VMEM(dims_of(args[i]), array_of(args[i]).dtype) for i in far_in]
        + [pltpu.VMEM(dims_of(outs[i]), array_of(outs[i]).dtype) for i in far_out]
        + list(scratch)
        + [
            pltpu.SemaphoreType.DMA((max(1, len(far_in)),)),
            pltpu.SemaphoreType.DMA((max(1, len(far_out)),)),
        ],
        input_output_aliases={nscalar + nargs + i: i for i in range(len(into))},
        compiler_params=pltpu.CompilerParams(vmem_limit_bytes=limit << 20),
        cost_estimate=pl.CostEstimate(
            flops=flops, transcendentals=0, bytes_accessed=bytes_accessed
        ),
        name=name,
    )
    result = kernel_call(*scalars, *arrays)
    if ordered:
        chain.last = result[-1]
    return result


def shape(dims, dtype=bf16):
    return jax.ShapeDtypeStruct(dims, dtype)


def kinds(dims, masks=range(GROUP)):
    return [shape(dims, bf16 if mask else f32) for mask in masks]


class Gather:
    def __init__(self, own):
        self.own = own
        self.side = {2: swap(own, 2), 4: swap(own, 4)}

    def corners(self, *gate):
        cut = lax.optimization_barrier(([self.side[2][0], self.side[4][1]], gate))[0]
        self.corner = [swap(cut[0], 4), swap(cut[1], 2)]

    def blocks(self, gate, corner_gate=()):
        even = lax.optimization_barrier(({0: self.own, **self.side}, gate))[0]
        self.corner = lax.optimization_barrier((self.corner, gate, corner_gate))[0]
        blocks = [even[mask] if mask in even else swap(even[mask ^ 1], 1) for mask in range(6)]
        return [[block] for block in blocks] + [self.corner, [swap(c, 1) for c in self.corner]]


def of_micro(blocks, m):
    return far(blocks[0], m) if len(blocks) == 1 else far(blocks[m])


def add_kernel(plan, *refs):
    ninputs = len(refs) - len(plan)
    for out_ref, rows in zip(refs[ninputs:], plan):
        for lead, addends in enumerate(rows):
            total = None
            for number, at in addends:
                value = (refs[number][...] if at is None else refs[number][at]).astype(f32)
                total = value if total is None else total + value
            if len(rows) == 1:
                out_ref[...] = total.astype(out_ref.dtype)
            else:
                out_ref[lead] = total.astype(out_ref.dtype)


def swap_back(parts, others=()):
    masks = (6, 2, 4, 0)
    odd = lax.optimization_barrier(([parts[mask ^ 1] for mask in masks], others))[0]
    return dict(zip(masks, lax.optimization_barrier([swap(part, 1) for part in odd])))


class Scatter:
    def __init__(self, parts):
        self.parts = parts
        self.back = {mask: swap(parts[mask ^ 1], 1) for mask in (6, 2, 4, 0)}

    def first(self):
        dims = self.parts[6].shape[1:]
        plan = [[[(0, m), (1, m)]] for m in range(2)]
        total = call(
            partial(add_kernel, plan), [shape(dims)] * 2, [far(self.back[6]), far(self.parts[6])], "corner", light=True
        )
        self.corner = swap(total[0], 4), swap(total[1], 2)

    def second(self):
        self.back[0], self.back[2], self.back[4] = lax.optimization_barrier([self.back[mask] for mask in (0, 2, 4)])
        dims = self.parts[2].shape
        plan = [
            [[(0, 0), (1, 0), (4, None)], [(0, 1), (1, 1)]],
            [[(2, 0), (3, 0)], [(2, 1), (3, 1), (5, None)]],
        ]
        total = call(
            partial(add_kernel, plan), [shape(dims)] * 2,
            [far(x) for x in (self.back[2], self.parts[2], self.back[4], self.parts[4], *self.corner)],
            "sides", light=True,
        )
        self.sides = swap(total[0], 2), swap(total[1], 4)

    def addends(self):
        return [far(x) for x in (self.parts[0], self.back[0], *self.sides)]


class ScatterOne:
    def __init__(self, parts, micro, others):
        self.parts = parts
        self.via = 4 if micro == 0 else 2
        self.back = swap_back(parts, others)

    def first(self, *gate):
        total = call(
            partial(add_kernel, [[[(0, None), (1, None)]]]), [shape(self.parts[6].shape)],
            [far(after(self.back[6], *gate)), far(self.parts[6])], "corner", light=True,
        )[0]
        self.corner = swap(total, self.via)

    def second(self):
        via = self.via
        plan = [[[(0, None), (1, None)]], [[(2, None), (3, None), (4, None)]]]
        total = call(
            partial(add_kernel, plan), [shape(self.parts[6].shape)] * 2,
            [
                far(x)
                for x in (self.back[via], self.parts[via], self.back[6 ^ via], self.parts[6 ^ via], self.corner)
            ],
            "sides", light=True,
        )
        self.sides = swap(total[0], via), swap(total[1], 6 ^ via)

    def addends(self):
        return [far(x) for x in (self.parts[0], self.back[0], *self.sides)]


def plane_groups():
    count = lax.axis_size("dp")
    return [list(range(first, first + GROUP)) for first in range(0, count, GROUP)]


def column_groups():
    count = lax.axis_size("dp")
    return [list(range(place, count, GROUP)) for place in range(GROUP)]


def plane_exchange(value):
    return lax.all_to_all(value, "dp", 0, 0, tiled=True, axis_index_groups=plane_groups())


def column_parts(value):
    planes = lax.axis_size("dp") // GROUP
    if planes > 4:
        return [
            lax.all_gather(value, "dp", axis=0, axis_index_groups=column_groups(), tiled=True)
        ]
    return [value] + [swap(value, GROUP * step) for step in range(1, planes)]


def column_send(parts):
    return [swap(part, GROUP * (step + 1)) for step, part in enumerate(parts)]


def few(planes):
    return planes <= 4


def order_kernel(wrow, plane_ref, place_ref, *refs):
    *parts, dy_ref, mat_ref, long_ref, qkv_ref, one_ref, two_ref, up_ref, long_s = refs
    for m in range(2):
        long_ref[m, 0 : dy_ref.shape[1]] = dy_ref[m]
    planes = len(parts)
    rows = mat_ref.shape[0] // planes
    piece = mat_ref.shape[0] // (planes * GROUP)
    source = lax.broadcasted_iota(jnp.int32, (128, 128), 0)
    target = lax.broadcasted_iota(jnp.int32, (128, 128), 1)
    each = 128 // piece
    for step, part in enumerate(parts):
        plane = plane_ref[0] ^ step
        at = pl.ds(pl.multiple_of(plane * rows, rows), rows)
        for i in range(3):
            mat_ref[at, i * 128 : (i + 1) * 128] = part[i * rows : (i + 1) * rows]
        start = 3 * rows
        for i in range(GROUP):
            value = part[start + i * wrow : start + (i + 1) * wrow]
            at = pl.ds(pl.multiple_of(dy_ref.shape[1] + (plane % (planes // 2)) * wrow, wrow), wrow)
            long_ref.at[plane // (planes // 2), at, i * 128 : (i + 1) * 128][...] = value
        start += GROUP * wrow
        for first in range(0, GROUP, each):
            total = jnp.zeros((16, 128), f32)
            for i in range(each):
                chosen = (source < piece) & (source + i * piece == target)
                tile = part[start + (first + i) * 16 : start + (first + i + 1) * 16]
                total = total + mm(tile, jnp.where(chosen, 1.0, 0.0).astype(bf16), NN)
            lane = (plane * GROUP + first) * piece
            long_s[:, pl.ds(pl.multiple_of(lane, 128), 128)] = total
        frow = up_ref.shape[1] // planes
        tile = part[pl.ds(pl.multiple_of(start + place_ref[0] * 16, 16), 16), :].astype(f32)
        up_ref[0:1, pl.ds(pl.multiple_of(plane * frow, 128), frow)] = tile[8:9]
    at = pl.ds(pl.multiple_of(place_ref[0] * 128, 128), 128)
    heads = long_s[0:8, at]
    qkv_ref[...] = jnp.concatenate((heads[0:1], jnp.zeros((1, 128), f32), heads[1:2]), axis=1)
    one_ref[...] = long_s[4:6]
    two_ref[0:1] = long_s[2:3]
    two_ref[1:3] = long_s[6:8]
    two_ref[3:4] = long_s[3:4]


def ffn_order_kernel(rows_ref, up_ref, down_ref):
    planes = rows_ref.shape[0]
    rows, units = up_ref.shape[0] // planes, up_ref.shape[1]
    frow = units // planes
    for plane in range(planes):
        up_ref[plane * rows : (plane + 1) * rows] = rows_ref[plane, 0:rows]
        down_ref[plane * frow : (plane + 1) * frow, 0:units] = rows_ref[plane, rows : rows + frow]
        down_ref[plane * frow : (plane + 1) * frow, units:] = rows_ref[plane, rows + frow :]


def out_order_kernel(planes, place_ref, *refs):
    *blocks, out_ref = refs
    size = out_ref.shape[0] // (planes * GROUP)
    half = planes // 2
    at = 0
    for mask in range(GROUP):
        for plane in range(planes):
            m, step = divmod(plane, half)
            ref = blocks[mask] if mask < 6 else blocks[6 + (mask - 6) * 2 + m]
            value = ref[m, step * size : (step + 1) * size] if mask < 6 else ref[step * size : (step + 1) * size]
            start = plane * GROUP * size + (place_ref[0] ^ mask) * size
            out_ref[pl.ds(pl.multiple_of(start, size), size), :] = value


def mm(left, right, contract):
    return lax.dot_general(left, right, (contract, ((), ())), preferred_element_type=f32)


NN = ((1,), (0,))
NT = ((1,), (1,))
TN = ((0,), (0,))


def split3(values):
    high = values.astype(bf16)
    rest = values - high.astype(f32)
    middle = rest.astype(bf16)
    low = (rest - middle.astype(f32)).astype(bf16)
    return high, middle, low


def norm_parts(values):
    center = values - jnp.mean(values, axis=-1, keepdims=True)
    spread = jnp.mean(center * center, axis=-1, keepdims=True)
    scale = lax.rsqrt(spread + eps)
    return center * scale, scale


def norm_back(grad, unit, scale, gain):
    scaled = grad * gain
    return scale * (
        scaled
        - jnp.mean(scaled, axis=-1, keepdims=True)
        - unit * jnp.mean(scaled * unit, axis=-1, keepdims=True)
    )


def fill_heads(query, key, slope_ref, query_s, key_s, place, start, rows):
    lane = lax.broadcasted_iota(jnp.int32, (rows, 128), 1)
    one = jnp.ones((rows, 128), bf16)
    zero = jnp.zeros((rows, 128), bf16)
    at = pl.ds(start, rows)
    for head in range(2):
        mine = (lane < HID) if head == 0 else (lane >= HID)
        base = HID if head == 0 else 0
        high, middle, low = split3(place * slope_ref[head])
        extra = jnp.where(
            lane == base,
            high,
            jnp.where(lane == base + 1, middle, jnp.where(lane == base + 2, low, zero)),
        )
        ones = jnp.where((lane >= base) & (lane < base + 3), one, zero)
        query_s[head, at, :] = jnp.where(mine, query, ones)
        key_s[head, at, :] = jnp.where(mine, key, extra)


def positions(start, rows):
    row = lax.broadcasted_iota(jnp.int32, (rows, 128), 0) + start
    after_trunk = row - TRUNK
    inside = after_trunk & (SEG - 1)
    return jnp.where(
        row < TRUNK, row, TRUNK + inside + jnp.where(after_trunk < BRANCHES * SEG, 0, SEG)
    ).astype(f32)


def tile_masks():
    row = lax.broadcasted_iota(jnp.int32, (HALF, HALF), 1)
    col = lax.broadcasted_iota(jnp.int32, (HALF, HALF), 0)
    same = (row // SEG) == (col // SEG)
    segment = jnp.where(same & (col <= row), 0.0, NEG)
    parent = jnp.where(same, 0.0, NEG)
    trow = lax.broadcasted_iota(jnp.int32, (ROWS, ROWS), 1)
    tcol = lax.broadcasted_iota(jnp.int32, (ROWS, ROWS), 0)
    causal = jnp.where(tcol <= trow, 0.0, NEG)
    return segment, parent, causal


def parent_rows(parent_ref, leaf):
    start = TRUNK + (parent_ref[leaf] - 1) * SEG
    return pl.ds(pl.multiple_of(start, SEG), SEG)


def tile_pieces(tile):
    if tile < TRUNK // ROWS:
        return (tile + 1) * ROWS, True, [], []
    start = tile * ROWS
    own = [start, start + HALF]
    first_leaf = TRUNK + BRANCHES * SEG
    leaves = []
    if start >= first_leaf:
        leaf = (start - first_leaf) // SEG
        leaves = [(leaf, leaf + 1), (leaf + 2, leaf + 3)]
    return TRUNK, False, own, leaves


def tile_scores(tile, key_ref, query, masks, side):
    segment, parent, causal = masks
    trunk, last, own, leaves = tile_pieces(tile)
    scores = mm(key_ref[0:trunk, :], query, NT)
    pieces = []
    if last:
        if trunk > ROWS:
            pieces.append(scores[: trunk - ROWS])
        pieces.append(scores[trunk - ROWS :] + causal)
    else:
        pieces.append(scores)
    if own:
        pieces.append(
            jnp.concatenate(
                [
                    mm(key_ref[at : at + HALF, :], query[i * HALF : (i + 1) * HALF], NT) + segment
                    for i, at in enumerate(own)
                ],
                axis=1,
            )
        )
    if leaves:
        pieces.append(
            jnp.concatenate(
                [
                    mm(rows, query[i * HALF : (i + 1) * HALF], NT) + parent
                    for i, rows in enumerate(side)
                ],
                axis=1,
            )
        )
    return pieces


def forward_kernel(
    micro, place_ref, parent_ref, slope_ref,
    a0, a1, a2, a3, a4, a5, a6, a7, vec_ref, mat_ref, bias_ref,
    ctx_ref, log_ref, packed_ref, unit_ref,
    query_s, key_s, value_s, ctx_s,
):
    rows = TREE // GROUP
    for mask, block_ref in zip((1, 2, 3, 4, 5, 0, 6, 7), (a1, a2, a3, a4, a5, a0, a6, a7)):
        start = pl.multiple_of((place_ref[0] ^ mask) * rows, rows)
        unit, _ = norm_parts(block_ref[...].astype(f32))
        unit_ref[mask] = unit.astype(bf16)
        normed = (unit * vec_ref[0:1] + vec_ref[1:2]).astype(bf16)
        part = (mm(normed, mat_ref[...], NN) + bias_ref[...]).astype(bf16)
        packed_ref.source[pl.ds(start, rows), :] = part
        value_s[pl.ds(start, rows), :] = part[:, 256:384]
        fill_heads(
            part[:, 0:128] * jnp.asarray(0.125, bf16), part[:, 128:256],
            slope_ref, query_s, key_s, positions(start, rows), start, rows,
        )
    leave(unit_ref, packed_ref)
    masks = tile_masks()
    for tile in range(TREE // ROWS):
        trunk, last, own, leaves = tile_pieces(tile)
        at = slice(tile * ROWS, (tile + 1) * ROWS)
        contexts = []
        side_values = [
            jnp.concatenate([value_s[parent_rows(parent_ref, leaf), :] for leaf in pair])
            for pair in leaves
        ]
        for head in range(2):
            query = query_s[head, at, :]
            side = [
                jnp.concatenate([key_s[head, parent_rows(parent_ref, leaf), :] for leaf in pair])
                for pair in leaves
            ]
            pieces = tile_scores(tile, key_s.at[head], query, masks, side)
            peak = pieces[0].max(axis=0, keepdims=True)
            for piece in pieces[1:]:
                peak = jnp.maximum(peak, piece.max(axis=0, keepdims=True))
            probs = [jnp.exp(piece - peak) for piece in pieces]
            total = probs[0].sum(axis=0, keepdims=True)
            for piece in probs[1:]:
                total = total + piece.sum(axis=0, keepdims=True)
            probs = [piece.astype(bf16) for piece in probs]
            ntrunk = len(probs) - bool(own) - bool(leaves)
            start = 0
            context = None
            for piece in probs[:ntrunk]:
                term = mm(value_s[start : start + piece.shape[0], :], piece, TN)
                context = term if context is None else context + term
                start += piece.shape[0]
            if own:
                context = context + jnp.concatenate(
                    [
                        mm(value_s[first : first + HALF, :], probs[ntrunk][:, i * HALF : (i + 1) * HALF], TN)
                        for i, first in enumerate(own)
                    ],
                    axis=1,
                )
            if leaves:
                context = context + jnp.concatenate(
                    [
                        mm(side_values[i], probs[ntrunk + 1][:, i * HALF : (i + 1) * HALF], TN)
                        for i in range(2)
                    ],
                    axis=1,
                )
            half = slice(head * HID, (head + 1) * HID)
            contexts.append(context[half] / total)
            log_ref[head : head + 1, at] = peak + jnp.log(total)
        ctx_s[at, :] = jnp.concatenate(contexts, axis=0).T.astype(bf16)
    for block in range(GROUP):
        ctx_ref[block] = ctx_s[block * rows : (block + 1) * rows, :]


def attention_forward(micro, place, parents, slopes, blocks, vec, mat, bias):
    rows, width = TREE // GROUP, mat.shape[0]
    return call(
        partial(forward_kernel, micro),
        [
            shape((GROUP, rows, 128)), shape((8, TREE), f32),
            far(shape((TREE, 384))), far(shape((GROUP, rows, width))),
        ],
        [*blocks, vec, mat, bias],
        "tree_attention",
        scalars=(place[None], parents, slopes),
        scratch=[
            pltpu.VMEM((2, TREE, 128), bf16),
            pltpu.VMEM((2, TREE, 128), bf16),
            pltpu.VMEM((TREE, 128), bf16),
            pltpu.VMEM((TREE, 128), bf16),
        ],
        flops=4_000_000_000,
        limit=14,
    )


def backward_kernel(
    micro, place_ref, parent_ref, slope_ref,
    grad_ref, packed_ref, ctx_ref, log_ref, mat_ref,
    o0, o1, o2, o3, o4, o5, o6, o7, dqkv_ref, sum_ref,
    query_s, key_s, value_s, grad_s, dkey_s, dvalue_s, dquery_s,
):
    rows = TREE // GROUP
    lane = lax.broadcasted_iota(jnp.int32, (rows, 128), 1)
    zero = jnp.zeros((rows, 128), bf16)
    for block in range(GROUP):
        start = block * rows
        at = pl.ds(start, rows)
        part = packed_ref[at, :]
        fill_heads(
            part[:, 0:128] * jnp.asarray(0.125, bf16), part[:, 128:256],
            slope_ref, query_s, key_s, positions(start, rows), start, rows,
        )
        value = part[:, 256:384]
        grad = grad_ref[block, micro]
        for head in range(2):
            mine = (lane < HID) if head == 0 else (lane >= HID)
            value_s[head, at, :] = jnp.where(mine, value, zero)
            grad_s[head, at, :] = jnp.where(mine, grad, zero)
        dquery_s[at, :] = grad.astype(f32) * ctx_ref[block].astype(f32)
    dkey_s[...] = jnp.zeros_like(dkey_s)
    dvalue_s[...] = jnp.zeros_like(dvalue_s)
    masks = tile_masks()
    for tile in range(TREE // ROWS):
        trunk, last, own, leaves = tile_pieces(tile)
        at = slice(tile * ROWS, (tile + 1) * ROWS)
        deltas = dquery_s[at, :].T
        dqueries = []
        for head in range(2):
            half = slice(head * HID, (head + 1) * HID)
            query = query_s[head, at, :]
            grad = grad_s[head, at, :]
            keys = key_s.at[head]
            values = value_s.at[head]
            side = [
                jnp.concatenate([key_s[head, parent_rows(parent_ref, leaf), :] for leaf in pair])
                for pair in leaves
            ]
            pieces = tile_scores(tile, keys, query, masks, side)
            level = log_ref[head : head + 1, at]
            delta = deltas[half].sum(axis=0, keepdims=True)
            ntrunk = len(pieces) - bool(own) - bool(leaves)
            dquery = None
            start = 0
            for piece in pieces[:ntrunk]:
                size = piece.shape[0]
                span = slice(start, start + size)
                probs = jnp.exp(piece - level)
                dprobs = mm(values[span, :], grad, NT)
                dscores = (probs * (dprobs - delta)).astype(bf16)
                dvalue_s[span, :] += mm(probs.astype(bf16), grad, NN)
                dkey_s[head, span, :] += mm(dscores, query, NN)
                term = mm(keys[span, :], dscores, TN)
                dquery = term if dquery is None else dquery + term
                start += size
            extra = []
            for i, first in enumerate(own):
                cols = slice(i * HALF, (i + 1) * HALF)
                span = slice(first, first + HALF)
                probs = jnp.exp(pieces[ntrunk][:, cols] - level[:, cols])
                dprobs = mm(values[span, :], grad[cols], NT)
                dscores = (probs * (dprobs - delta[:, cols])).astype(bf16)
                dvalue_s[span, :] += mm(probs.astype(bf16), grad[cols], NN)
                dkey_s[head, span, :] += mm(dscores, query[cols], NN)
                extra.append(mm(keys[span, :], dscores, TN))
            if own:
                dquery = dquery + jnp.concatenate(extra, axis=1)
            extra = []
            for i, pair in enumerate(leaves):
                cols = slice(i * HALF, (i + 1) * HALF)
                side_value = jnp.concatenate(
                    [value_s[head, parent_rows(parent_ref, leaf), :] for leaf in pair]
                )
                probs = jnp.exp(pieces[ntrunk + 1][:, cols] - level[:, cols])
                dprobs = mm(side_value, grad[cols], NT)
                dscores = (probs * (dprobs - delta[:, cols])).astype(bf16)
                dval = mm(probs.astype(bf16), grad[cols], NN)
                dkey = mm(dscores, query[cols], NN)
                for j, leaf in enumerate(pair):
                    span = parent_rows(parent_ref, leaf)
                    dvalue_s[span, :] += dval[j * SEG : (j + 1) * SEG]
                    dkey_s[head, span, :] += dkey[j * SEG : (j + 1) * SEG]
                extra.append(mm(side[i], dscores, TN))
            if leaves:
                dquery = dquery + jnp.concatenate(extra, axis=1)
            dqueries.append(dquery[half] * 0.125)
        dquery_s[at, :] = jnp.concatenate(dqueries, axis=0).T
    sums = jnp.zeros((1, 384), f32)
    for mask, out_ref in reversed(list(enumerate((o0, o1, o2, o3, o4, o5, o6, o7)))):
        at = pl.ds(pl.multiple_of((place_ref[0] ^ mask) * rows, rows), rows)
        dkey = jnp.where(lane < HID, dkey_s[0, at, :], dkey_s[1, at, :])
        dqkv = jnp.concatenate(
            (dquery_s[at, :].astype(bf16), dkey.astype(bf16), dvalue_s[at, :].astype(bf16)), axis=1
        )
        dqkv_ref[mask] = dqkv
        sums = sums + jnp.sum(dqkv.astype(f32), axis=0, keepdims=True)
        out_ref[...] = mm(dqkv, mat_ref[...], NT).astype(out_ref.dtype)
        leave(out_ref)
    sum_ref[...] = jnp.broadcast_to(sums, (8, 384))


def attention_backward(micro, place, parents, slopes, packed, ctx, grad, logs, mat):
    rows = TREE // GROUP
    width = mat.shape[0]
    result = call(
        partial(backward_kernel, micro),
        [far(x) for x in kinds((rows, width))] + [far(shape((GROUP, rows, 384))), shape((8, 384), f32)],
        [grad, far(packed), ctx, logs, mat],
        "tree_attention_back",
        scalars=(place[None], parents, slopes),
        scratch=[
            pltpu.VMEM((2, TREE, 128), bf16),
            pltpu.VMEM((2, TREE, 128), bf16),
            pltpu.VMEM((2, TREE, 128), bf16),
            pltpu.VMEM((2, TREE, 128), bf16),
            pltpu.VMEM((2, TREE, 128), f32),
            pltpu.VMEM((TREE, 128), f32),
            pltpu.VMEM((TREE, 128), f32),
        ],
        flops=10_000_000_000,
        limit=16,
    )
    return result[:GROUP], result[GROUP], result[GROUP + 1][0]


def project_kernel(p0, p1, x_ref, vec_ref, mat_ref, middle_ref, normed_ref, ctx_ref, total_s):
    micros, rows, width = middle_ref.shape
    for m, part in enumerate((p0, p1)):
        for block in range(GROUP):
            total_s[m * rows : (m + 1) * rows, block * 128 : (block + 1) * 128] = part[block]
    attn = mm(total_s[...], mat_ref[...], NN) + vec_ref[0:1]
    for m in range(micros):
        ctx_ref[m] = total_s[m * rows : (m + 1) * rows]
        middle = x_ref[m].astype(f32) + attn[m * rows : (m + 1) * rows]
        middle_ref[m] = middle
        unit, _ = norm_parts(middle)
        normed_ref[m] = (unit * vec_ref[1:2] + vec_ref[2:3]).astype(bf16)


def project(parts, x, vec, mat):
    dims = dims_of(x)
    return call(
        project_kernel,
        [shape(dims, f32), shape(dims), far(shape(dims))],
        [*parts, x, vec, mat],
        "project",
        scratch=[pltpu.VMEM((dims[0] * dims[1], dims[2]), bf16)],
        flops=2 * dims[0] * dims[1] * dims[2] * dims[2],
        limit=16,
    )


def rows_of(refs):
    if len(refs) == 1:
        micros, rows, width = refs[0].shape
        return refs[0][...].reshape(micros * rows, width)
    return jnp.concatenate([ref[...] for ref in refs])


def ffn_kernel(counts, *refs):
    refs = list(refs)

    def take(number):
        taken = refs[:number]
        del refs[:number]
        return taken

    a_refs = [take(number) for number in counts]
    dy_refs = [take(number) for number in counts]
    up_ref, down_ref, bias_ref = take(3)
    y_refs, da_refs = take(len(counts)), take(len(counts))
    act_ref, du_ref, sum_ref = refs
    sums = jnp.zeros((1, up_ref.shape[1]), f32)
    for i in range(len(counts)):
        upper = mm(rows_of(a_refs[i]), up_ref[...], NN) + bias_ref[...]
        square = upper * upper
        bent = jnp.tanh(upper * (0.7978845608028654 + (0.7978845608028654 * 0.044715) * square))
        half = 0.5 * (1.0 + bent)
        active = (upper * half).astype(bf16)
        slope = half + (0.5 * upper) * (1.0 - bent * bent) * (
            0.7978845608028654 + (3.0 * 0.7978845608028654 * 0.044715) * square
        )
        act_ref[i] = active
        du = mm(rows_of(dy_refs[i]), down_ref[...], NT) * slope
        sums = sums + jnp.sum(du, axis=0, keepdims=True)
        du = du.astype(bf16)
        du_ref[i] = du
        kind = da_refs[i].dtype
        da_refs[i][...] = mm(du, up_ref[...], NT).astype(kind).reshape(da_refs[i].shape)
        y_refs[i][...] = mm(active, down_ref[...], NN).astype(bf16).reshape(y_refs[i].shape)
        leave(y_refs[i], da_refs[i])
    sum_ref[...] = jnp.broadcast_to(sums, sum_ref.shape)


def feed_forward(a, dy, masks, up, down, bias, more):
    counts = tuple(len(a[mask]) for mask in masks)
    micros, (rows, width), units = 2, array_of(a[masks[0]][0]).shape[-2:], up.shape[1]
    dims = (micros, rows, width)
    long = (micros, rows + more, width)
    number = len(masks)
    result = call(
        partial(ffn_kernel, counts),
        [far(shape(long), rows=(0, rows)) for _ in masks]
        + [far(x) for x in kinds(dims, masks)]
        + [far(shape((number, micros * rows, units))) for _ in range(2)]
        + [shape((8, units), f32)],
        [far(x) for mask in masks for x in a[mask]]
        + [far(x, rows=(0, rows)) for mask in masks for x in dy[mask]]
        + [up, down, bias],
        "feed_forward",
        flops=8 * number * micros * rows * width * units,
        limit=18,
    )
    return result[:number], result[number : 2 * number], result[-3], result[-2], result[-1][0]


def flat_rows(groups):
    return jnp.concatenate([rows_of(group) for group in groups])


def take_groups(refs, counts):
    groups, at = [], 0
    for number in counts:
        groups.append(refs[at : at + number])
        at += number
    return groups, refs[at:]


def up_grads_kernel(counts, planes, *refs):
    groups, refs = take_groups(refs, counts)
    *du_refs, out_ref = refs
    units = du_refs[0].shape[-1]
    rows = groups[0][0].shape[-1] // planes
    du = jnp.concatenate([ref[...].reshape(-1, units) for ref in du_refs])
    for plane in range(planes):
        at = slice(plane * rows, (plane + 1) * rows)
        parts = [ref[..., at].reshape(-1, rows) for group in groups for ref in group]
        out_ref[plane] = mm(jnp.concatenate(parts), du, TN)


def down_grads_kernel(counts, planes, *refs):
    groups, refs = take_groups(refs, counts)
    *act_refs, out_ref = refs
    units = act_refs[0].shape[-1]
    frow = units // planes
    dy = flat_rows(groups)
    for plane in range(planes):
        at = slice(plane * frow, (plane + 1) * frow)
        act = jnp.concatenate([ref[:, :, at].reshape(-1, frow) for ref in act_refs])
        down = mm(act, dy, TN)
        out_ref[plane, 0:frow] = down[:, :units]
        out_ref[plane, frow:] = down[:, units:]


def ffn_grads(a, dy, masks, act, du, planes):
    counts = tuple(len(a[mask]) for mask in masks)
    width, units = array_of(a[masks[0]][0]).shape[-1], du[0].shape[-1]
    rows, more = width // planes, 2 * (units // planes)
    total = shape((planes, rows + more, units), f32)
    flops = 4 * TREE * width * units
    (up,) = call(
        partial(up_grads_kernel, counts, planes),
        [far(total, rows=(0, rows))],
        [far(x) for mask in masks for x in a[mask]] + [far(x) for x in du],
        "up_grads",
        flops=flops,
        limit=20,
    )
    yield
    (both,) = call(
        partial(down_grads_kernel, counts, planes),
        [far(total, rows=(rows, more))],
        [far(x, rows=(0, TREE // GROUP)) for mask in masks for x in dy[mask]] + [far(x) for x in act],
        "down_grads",
        flops=flops,
        limit=24,
        into=(up,),
    )
    yield both


def second_back_kernel(
    own_ref, back_ref, first_ref, second_ref, dy_ref, middle_ref, vec_ref, mat_ref,
    dh_ref, dattn_ref, dctx_ref, sum_ref,
):
    micros, rows, width = middle_ref.shape
    sums = []
    for m in range(micros):
        grad = (
            own_ref[m].astype(f32)
            + back_ref[m].astype(f32)
            + first_ref[m].astype(f32)
            + second_ref[m].astype(f32)
        )
        unit, scale = norm_parts(middle_ref[m])
        dy = dy_ref[m].astype(f32)
        dh = dy + norm_back(grad, unit, scale, vec_ref[1:2])
        dh_ref[m] = dh
        dattn = dh.astype(bf16)
        dattn_ref[m] = dattn
        sums.append(
            [
                jnp.sum(value, axis=0, keepdims=True)
                for value in (dattn.astype(f32), dy, grad * unit, grad)
            ]
        )
    leave(dh_ref)
    dattn = dattn_ref[...].reshape(micros * rows, width)
    dctx = mm(dattn, mat_ref[...], NT).astype(bf16)
    for m in range(micros):
        for block in range(GROUP):
            dctx_ref[block, m] = dctx[m * rows : (m + 1) * rows, block * 128 : (block + 1) * 128]
    sum_ref[...] = jnp.concatenate(
        [first + second for first, second in zip(*sums)] + [jnp.zeros((4, width), f32)]
    )


def second_back(addends, dy, middle, vec, mat):
    dims = middle.shape
    return call(
        second_back_kernel,
        [
            far(shape(dims, f32)), shape(dims), shape((GROUP, dims[0], dims[1], 128)),
            shape((8, dims[2]), f32),
        ],
        [*addends, dy, middle, vec, mat],
        "norm2_back",
        flops=2 * middle.size * dims[2],
        limit=16,
    )


def first_back_kernel(*refs):
    groups, (x_ref, dh_ref, vec_ref, out_ref) = (refs[0:4], refs[4:8]), refs[8:]
    for m, group in enumerate(groups):
        grad = group[0][...].astype(f32)
        for ref in group[1:]:
            grad = grad + ref[...].astype(f32)
        unit, scale = norm_parts(x_ref[m].astype(f32))
        out_ref[m] = (dh_ref[m] + norm_back(grad, unit, scale, vec_ref[0:1])).astype(bf16)


def output_kernel(more, planes, plane_ref, own_ref, back_ref, first_ref, second_ref, middle_ref, vec_ref, out_ref, *rest):
    micros, rows, width = middle_ref.shape
    for m in range(micros):
        part = slice(0, rows)
        total = own_ref[m, part].astype(f32) + back_ref[m, part].astype(f32)
        total = total + first_ref[m, part].astype(f32) + second_ref[m, part].astype(f32)
        out_ref[m] = (middle_ref[m] + (total + vec_ref[3:4])).astype(bf16)
    leave(out_ref)
    if more:
        part = slice(rows, rows + more)
        for m in range(micros):
            total = own_ref[m, part].astype(f32) + back_ref[m, part].astype(f32)
            total = total + first_ref[m, part].astype(f32) + second_ref[m, part].astype(f32)
            rest[planes][m * more : (m + 1) * more] = total
        size = micros * more // planes
        for step in range(planes):
            at = pl.ds(pl.multiple_of((plane_ref[0] ^ step) * size, size), size)
            rest[step][...] = rest[planes][at, :].astype(rest[step].dtype)


def out_grads_kernel(planes, place_ref, dattn_ref, ctx_ref, *refs):
    outs, total_s = refs[:GROUP], refs[GROUP]
    total_s[...] = mm(rows_of([ctx_ref]), rows_of([dattn_ref]), TN)
    micros, more, _ = outs[0].shape
    size = micros * more // planes
    for mask in range(GROUP):
        for plane in range(planes):
            start = plane * GROUP * size + (place_ref[0] ^ mask) * size
            m, at = divmod(plane * size, more)
            outs[mask][m, at : at + size, :] = total_s[
                pl.ds(pl.multiple_of(start, size), size), :
            ].astype(bf16)
        leave(outs[mask])


def out_grads(place, ctx, dattn, parts, planes):
    width = dattn.shape[-1]
    rows = dattn.shape[1]
    more = parts[0].shape[1] - rows
    return call(
        partial(out_grads_kernel, planes),
        [far(shape(part.shape), rows=(rows, more)) for part in parts],
        [dattn, far(ctx)],
        "out_grads",
        scalars=(place[None],),
        scratch=[pltpu.VMEM((width, width), f32)],
        limit=16,
        light=True,
        into=parts,
    )


def qkv_grads_kernel(planes, plane_ref, sum_ref, g0, g1, u0, u1, mat_ref, vec_ref, *refs):
    *outs, terms_ref = refs
    rows = mat_ref.shape[0] // planes
    sums = sum_ref[0:1]
    lane = lax.broadcasted_iota(jnp.int32, (rows, 128), 1)

    def terms_of(unit_ref, grad_ref):
        grads = rows_of_tree(grad_ref)
        result = []
        for step in range(planes):
            cols = pl.ds(pl.multiple_of((plane_ref[0] ^ step) * rows, 128), rows)
            result.append(mm(unit_ref.at[:, :, cols][...].reshape(-1, rows), grads, TN))
        return result

    products = [a + b for a, b in zip(terms_of(u0, g0), terms_of(u1, g1))]
    for step in (*range(1, planes), 0):
        plane = plane_ref[0] ^ step
        at = pl.ds(pl.multiple_of(plane * rows, rows), rows)
        product = products[step]
        mat = mat_ref[at, :].astype(f32)
        total = product * vec_ref[at, 0:1] + vec_ref[at, 1:2] * sums
        outs[step][...] = total.astype(outs[step].dtype)
        gain = jnp.sum(product * mat, axis=1, keepdims=True)
        bias = jnp.sum(mat * sums, axis=1, keepdims=True)
        terms_ref[at, :] = jnp.where(lane == 0, gain, jnp.where(lane == 1, bias, 0.0))


def rows_of_tree(ref):
    blocks, rows, width = ref.shape
    return ref[...].reshape(blocks * rows, width)


def qkv_grads(sums, grads, units, mat, vec_columns, plane, planes):
    width = mat.shape[0]
    return call(
        partial(qkv_grads_kernel, planes),
        [*kinds((width // planes, 384), range(planes)), shape((width, 128), f32)],
        [sums, *[far(x) for x in grads], *[far(x) for x in units], mat, vec_columns],
        "qkv_grads",
        scalars=(plane[None],),
        flops=2 * TREE * 2 * width * 384,
        limit=20,
    )


def pack_kernel(planes, q_ref, k_ref, v_ref, up_ref, *refs):
    *vectors, sent_ref = refs
    frow = up_ref.shape[1] // (planes * GROUP)
    lanes = sent_ref.shape[2] - 128
    row = lax.broadcasted_iota(jnp.int32, (16, 128), 0)
    tile = jnp.zeros((16, 128), f32)
    for at, ref in enumerate(vectors):
        value = ref[...].astype(f32)
        if ref.shape[1] < 128:
            value = jnp.pad(value, ((0, 0), (0, 128 - ref.shape[1])))
        tile = jnp.where(row == at, value, tile)
    for place in range(GROUP):
        for at, ref in enumerate((q_ref, k_ref, v_ref)):
            sent_ref[place, :, at * 128 : (at + 1) * 128] = ref[:, place * 128 : (place + 1) * 128]
        for plane in range(planes):
            start = (plane * GROUP + place) * frow
            sent_ref[place, :, 384 + plane * frow : 384 + (plane + 1) * frow] = up_ref[
                :, start : start + frow
            ]
        sent_ref[place, 0:16, lanes:] = tile.astype(bf16)


def split_kernel(got_ref, out_ref, down_ref, first_ref, second_ref):
    places, size, lanes = got_ref.shape
    rows, wrow, frow = places * size, out_ref.shape[0], down_ref.shape[0]
    for place in range(places):
        for i in range(3):
            at = i * rows + place * size
            first_ref[at : at + size] = got_ref[place, :, i * 128 : (i + 1) * 128]
        second_ref[place * size : (place + 1) * size] = got_ref[place, :, 384 : lanes - 128]
        at = 3 * rows + GROUP * wrow + place * 16
        first_ref[at : at + 16] = got_ref[place, 0:16, lanes - 128 :]
    for i in range(GROUP):
        at = 3 * rows + i * wrow
        first_ref[at : at + wrow] = out_ref[:, i * 128 : (i + 1) * 128]
    half = down_ref.shape[1] // 2
    second_ref[rows : rows + frow] = down_ref[:, 0:half]
    second_ref[rows + frow :] = down_ref[:, half:]


def home_kernel(planes, ffn_ref, *refs):
    mats, (home_ref, down_ref) = refs[:planes], refs[planes:]
    mat = mats[0][...]
    for part in mats[1:]:
        mat = mat + part[...].astype(f32)
    rows, frow = mat.shape[0], down_ref.shape[0]
    size, half = rows // GROUP, down_ref.shape[1] // 2
    for place in range(GROUP):
        at = slice(place * size, (place + 1) * size)
        home_ref[place, :, 0:384] = mat[at]
        home_ref[place, :, 384:] = ffn_ref[at]
    down_ref[:, 0:half] = ffn_ref[rows : rows + frow]
    down_ref[:, half:] = ffn_ref[rows + frow :]


def unpack_kernel(planes, home_ref, q_ref, k_ref, v_ref, up_ref):
    frow = up_ref.shape[1] // (planes * GROUP)
    for place in range(GROUP):
        for at, ref in enumerate((q_ref, k_ref, v_ref)):
            ref[:, place * 128 : (place + 1) * 128] = home_ref[place, :, at * 128 : (at + 1) * 128]
        for plane in range(planes):
            start = (plane * GROUP + place) * frow
            up_ref[:, start : start + frow] = home_ref[
                place, :, 384 + plane * frow : 384 + (plane + 1) * frow
            ]


def on_device(
    tokens, grad_out, w_query, w_key, w_value, b_query, b_value, w_attn_out, b_attn_out,
    w_up, b_up, w_down, b_down, ln1_gain, ln1_bias, ln2_gain, ln2_bias, leaf_parent,
):
    micro_count, row_count, width = tokens.shape
    count = lax.axis_size("dp")
    planes = count // GROUP
    index = lax.axis_index("dp")
    place = index % GROUP
    plane = index // GROUP
    wrow = w_query.shape[0]
    frow = w_down.shape[0]
    head_width = width // GROUP
    unit_width = planes * frow
    lanes = 3 * head_width + unit_width
    both = range(micro_count)
    chain.last = None

    small = (b_query, b_value, b_attn_out, b_down, ln1_gain, ln1_bias, ln2_gain, ln2_bias, b_up)
    if few(planes):
        (sent,) = call(
            partial(pack_kernel, planes),
            [shape((GROUP, wrow, lanes + 128))],
            [far(x) for x in (w_query, w_key, w_value, w_up, *[piece.reshape(1, -1) for piece in small])],
            "pack",
        )
    else:
        qkv_w = [w.reshape(wrow, GROUP, head_width) for w in (w_query, w_key, w_value)]
        up_w = w_up.reshape(wrow, planes, GROUP, frow).transpose(0, 2, 1, 3)
        sent = jnp.concatenate((*qkv_w, up_w.reshape(wrow, GROUP, unit_width)), axis=2)
        sent = sent.transpose(1, 0, 2)
    got = plane_exchange(sent)
    gather_x = Gather(after(tokens, got))

    if few(planes):
        first, second = call(
            split_kernel,
            [
                shape((4 * GROUP * wrow + 16 * GROUP, 128)),
                shape((GROUP * wrow + 2 * frow, unit_width)),
            ],
            [got, far(w_attn_out), far(w_down)],
            "split",
        )
        gather_x.corners(first)
        first_parts = column_parts(first)
        corner_x = gather_x.corner
        blocks_x = gather_x.blocks(first_parts)
        ffn_rows = lax.all_gather(second, "dp", axis=0, axis_index_groups=column_groups())
        mat_qkv, dy_rows, vec_qkv, vec_one, vec_two, vec_up = call(
            partial(order_kernel, wrow),
            [
                shape((width, 3 * head_width)), far(shape((micro_count, row_count + 2 * wrow, width))),
                shape((1, 3 * head_width), f32),
                shape((2, width), f32), shape((4, width), f32), shape((1, unit_width), f32),
            ],
            [after(first_parts[0], *corner_x), *first_parts[1:], far(grad_out)],
            "rows",
            scalars=(plane[None], place[None]),
            scratch=[pltpu.VMEM((16, width), f32)],
        )
    else:
        vector = jnp.stack(
            [jnp.pad(piece.astype(f32), (0, 128 - piece.shape[0])) for piece in small]
        )
        vectors = lax.all_gather(jnp.pad(vector, ((0, 7), (0, 0))), "dp")
        piece = width // count
        long = vectors[:, :8, :piece].transpose(1, 0, 2).reshape(8, width)
        vec_up = lax.dynamic_index_in_dim(
            vectors.reshape(planes, GROUP, 16, 128)[:, :, 8, :frow], place, 1, keepdims=False
        ).reshape(1, -1)
        vec_qkv = lax.dynamic_slice_in_dim(long[:2], place * head_width, head_width, axis=1)
        vec_qkv = jnp.concatenate(
            (vec_qkv[0], jnp.zeros((head_width,), f32), vec_qkv[1])
        )[None]
        vec_one = long[4:6]
        vec_two = jnp.stack((long[2], long[6], long[7], long[3]))
        got = got.reshape(GROUP * wrow, lanes)
        mat_qkv = column_parts(got[:, : 3 * head_width])[0]
        down_rows = jnp.concatenate((w_down[:, :unit_width], w_down[:, unit_width:]))
        ffn_rows = column_parts(jnp.concatenate((got[:, 3 * head_width :], down_rows)))[0]
        ffn_rows = ffn_rows.reshape(planes, -1, unit_width)
        mat_up = ffn_rows[:, : GROUP * wrow].reshape(width, unit_width)
        halves = ffn_rows[:, GROUP * wrow :].reshape(planes, 2, frow, unit_width)
        mat_down = halves.transpose(0, 2, 1, 3).reshape(unit_width, width)
        mat_out = far(lax.all_gather(w_attn_out, "dp", axis=0, tiled=True))
        dy_rows = grad_out
        gather_x.corners()
        blocks_x = gather_x.blocks(())
    gather_dy = Gather(dy_rows)

    parents = lax.dynamic_index_in_dim(leaf_parent, plane, 1, keepdims=False)
    heads = 2 * place + jnp.arange(2, dtype=jnp.int32)
    slopes = jnp.exp2(-8.0 * (heads.astype(f32) + 1.0) / HEADS)
    forward = []
    for m in both:
        blocks = [far(tokens, m)] + [of_micro(blocks_x[mask], m) for mask in range(1, GROUP)]
        forward.append(
            attention_forward(m, place, parents[m], slopes, blocks, vec_one, mat_qkv, vec_qkv)
        )
    plane_ctx = [plane_exchange(forward[m][0]) for m in both]
    gather_dy.corners(chain.last, plane_ctx[0])
    blocks_dy = gather_dy.blocks(plane_ctx[0], plane_ctx[1])
    if few(planes):
        window_of = (row_count, 2 * wrow)
        (mat_out,) = call(
            partial(out_order_kernel, planes),
            [shape((width, width))],
            [far(x, rows=window_of) for mask in range(GROUP) for x in blocks_dy[mask]],
            "attn_out",
            scalars=(place[None],),
        )

    middle, normed2, context = project(
        plane_ctx,
        far(tokens), vec_two, mat_out
    )
    if few(planes):
        mat_up, mat_down = call(
            ffn_order_kernel,
            [shape((width, unit_width)), shape((unit_width, width))],
            [far(ffn_rows)],
            "units",
        )

    more = 2 * wrow if few(planes) else 0
    split = ((0, 1), (2, 4, 3, 5), (6, 7))
    order = [mask for masks in split for mask in masks]
    grad_vec_up = 0.0
    y_parts, a_parts, act, du = [None] * GROUP, [None] * GROUP, [], []
    blocks_a2 = [[normed2], [swap(normed2, 1)]] + [None] * 6
    gather_a2 = Gather(normed2)
    for number, masks in enumerate(split):
        if number == 1:
            gather_a2.side = dict(zip((2, 4), lax.optimization_barrier((*gather_a2.side.values(), chain.last))))
            gather_a2.corners()
            for mask in (2, 4):
                blocks_a2[mask], blocks_a2[mask ^ 1] = [gather_a2.side[mask]], [swap(gather_a2.side[mask], 1)]
        if number == 2:
            corner = lax.optimization_barrier((*gather_a2.corner, chain.last))[:2]
            blocks_a2[6], blocks_a2[7] = list(corner), [swap(c, 1) for c in corner]
        y, da, act_part, du_part, up_sum = feed_forward(
            blocks_a2, blocks_dy, masks, mat_up, mat_down, vec_up, more
        )
        act.append(act_part)
        du.append(du_part)
        grad_vec_up = grad_vec_up + up_sum
        for i, mask in enumerate(masks):
            y_parts[mask] = y[i]
            a_parts[mask] = da[i]
    scatter2 = Scatter(a_parts)
    scatter2.first()
    if few(planes):
        steps = ffn_grads(blocks_a2, blocks_dy, order, act, du, planes)
        next(steps)
    else:
        flat = lambda blocks: jnp.concatenate(
            [x.reshape(-1, width) for mask in order for x in blocks[mask]]
        )
        units_flat = lambda parts: jnp.concatenate([x.reshape(-1, unit_width) for x in parts])
        grad_up = mm(flat(blocks_a2), units_flat(du), TN)
        grad_down = mm(units_flat(act), flat(blocks_dy), TN)
    scatter2.second()
    if few(planes):
        sum_ffn = lax.psum_scatter(
            after(next(steps), *scatter2.sides), "dp", scatter_dimension=0, axis_index_groups=column_groups()
        )
    dh, dattn, dctx, small_own = second_back(
        scatter2.addends(), far(grad_out), middle, vec_two, mat_out
    )
    plane_dctx = plane_exchange(dctx)
    if few(planes):
        y_parts = out_grads(place, context, dattn, y_parts, planes)
    scatter_y = Scatter(y_parts)
    scatter_y.first()

    scatter1, grad_qkv, sum_qkv = [], [], 0.0
    for m in both:
        parts, dqkv, dsum = attention_backward(
            m, place, parents[m], slopes, forward[m][2], forward[m][0], plane_dctx, forward[m][1], mat_qkv
        )
        scatter1.append(ScatterOne(parts, m, (scatter1[0].corner,) if m else scatter_y.corner))
        grad_qkv.append(dqkv)
        sum_qkv = sum_qkv + dsum
        if m == 0:
            scatter1[0].first()
            scatter_y.second()
    scatter1[0].second()
    scatter1[1].first(*scatter_y.sides)
    sums8 = jnp.broadcast_to(sum_qkv, (8, 384))
    if few(planes):
        own_mat, *others, norm_terms = qkv_grads(
            sums8, grad_qkv, [forward[m][3] for m in both], mat_qkv, vec_one.T, plane, planes
        )
        others = column_send(lax.optimization_barrier((others, scatter1[0].sides))[0])
    else:
        units = jnp.concatenate([forward[m][3].reshape(-1, width) for m in both])
        product = mm(units, jnp.concatenate([g.reshape(-1, 384) for g in grad_qkv]), TN)
        grad_mat = product * vec_one[0][:, None] + vec_one[1][:, None] * sum_qkv[None]
        mat32 = mat_qkv.astype(f32)
        norm_terms = jnp.stack(
            (jnp.sum(product * mat32, axis=1), jnp.sum(mat32 * sum_qkv[None], axis=1)), axis=1
        )
    scatter1[1].second()
    last = chain.last
    output, *out_parts = call(
        partial(output_kernel, more, planes),
        [far(shape(tokens.shape))] + (kinds((wrow, width), range(planes)) if more else []),
        [*scatter_y.addends(), middle, vec_two],
        "output",
        scalars=(plane[None],),
        scratch=[pltpu.VMEM((2 * more, width), f32)] if more else [],
        light=True,
        limit=16,
    )

    if few(planes):
        home, sum_down = call(
            partial(home_kernel, planes),
            [shape((GROUP, wrow, lanes), f32), far(shape((frow, width), f32))],
            [far(after(sum_ffn, *scatter1[1].sides)), own_mat, *others],
            "home",
            light=True,
        )
        home = plane_exchange(home)
        out_sums = column_send(lax.optimization_barrier((out_parts[1:], others))[0])
    else:

        def scattered(value):
            value = value.reshape(planes, -1, value.shape[1])
            return lax.psum_scatter(
                value, "dp", scatter_dimension=0, axis_index_groups=column_groups()
            )

        home = plane_exchange(
            jnp.concatenate((scattered(grad_mat), scattered(grad_up)), axis=1).reshape(
                GROUP, wrow, lanes
            )
        )
        sum_down = scattered(grad_down)
        grad_out_mat = mm(context.reshape(-1, width), dattn.reshape(-1, width), TN)
        sum_out = lax.psum_scatter(grad_out_mat, "dp", scatter_dimension=0, tiled=True)
    (grad_input,) = call(
        first_back_kernel,
        [far(shape(tokens.shape))],
        [*scatter1[0].addends(), *scatter1[1].addends(), far(tokens), far(dh), vec_one],
        "norm1_back",
    )
    if few(planes):
        sum_out = after(out_parts[0], grad_input)
        for part in out_sums:
            sum_out = sum_out + part.astype(f32)
    if few(planes):
        *home_qkv, home_up = call(
            partial(unpack_kernel, planes),
            [far(shape((wrow, width), f32))] * 3 + [far(shape((wrow, unit_width * GROUP), f32))],
            [home],
            "unpack",
        )
    else:
        home_up = home[:, :, 3 * head_width :].reshape(GROUP, wrow, planes, frow)
        home_up = home_up.transpose(1, 2, 0, 3).reshape(wrow, -1)
        home_qkv = [
            home[:, :, at * head_width : (at + 1) * head_width].transpose(1, 0, 2).reshape(wrow, width)
            for at in range(3)
        ]

    sum_qkv, small_own, norm_terms, grad_vec_up, _ = lax.optimization_barrier(
        (sum_qkv, small_own, norm_terms, grad_vec_up, last)
    )

    def placed(piece):
        return lax.dynamic_update_slice_in_dim(
            jnp.zeros((width,), f32), piece, place * head_width, 0
        )

    up_terms = lax.dynamic_update_slice_in_dim(
        jnp.zeros((planes, GROUP, frow), f32),
        grad_vec_up.reshape(planes, 1, frow),
        place,
        1,
    )
    terms = jnp.concatenate(
        [
            piece.reshape(count, -1)
            for piece in (
                placed(sum_qkv[:head_width]),
                placed(sum_qkv[2 * head_width :]),
                small_own[0],
                small_own[1],
                norm_terms[:, 0],
                norm_terms[:, 1],
                small_own[2],
                small_own[3],
                up_terms,
            )
        ],
        axis=1,
    )
    sums = jnp.sum(lax.all_to_all(terms, "dp", 0, 0, tiled=True), axis=0)
    bounds = [0]
    for piece in small:
        bounds.append(bounds[-1] + piece.shape[0])
    pieces = [sums[bounds[at] : bounds[at + 1]] for at in range(len(small))]
    return (
        output, grad_input,
        home_qkv[0], home_qkv[1], home_qkv[2], sum_out, home_up, sum_down,
        pieces[0], pieces[1], pieces[2], pieces[8], pieces[3],
        pieces[4], pieces[5], pieces[6], pieces[7],
    )


def solution(mesh):
    row = P("dp", None)
    vec = P("dp")
    tok = P(None, "dp", None)
    return jax.shard_map(
        on_device,
        mesh=mesh,
        in_specs=(
            tok, tok, row, row, row, vec, vec, row, vec, row, vec, row, vec, vec, vec, vec, vec, P(),
        ),
        out_specs=(
            tok, tok, row, row, row, row, row, row, vec, vec, vec, vec, vec, vec, vec, vec, vec,
        ),
        check_vma=False,
    )
```
